32 devices in a mesh: fsdp: 8 (over z, core), tensor: 4 (over y, x).
Axes of the slice: x: 2, y: 2, z: 4, core: 2. Of those that a mesh axis runs over, the one named last changes fastest.
Arguments:
- inputs: bfloat16 [2, 4, 1024, 2048], P(None, 'tensor', 'fsdp'), may hold values from -6 to 6
- out_grads: bfloat16 [2, 4, 1024, 2048], P(None, 'tensor', 'fsdp'), may hold values from -6 to 6
- prefix_len: int32 [2, 4], replicated, may hold values from 102 to 512
- positions: int32 [2, 4, 1024], P(None, None, 'fsdp'), may hold values from 0 to 1535, as said below
- attn_gain: bfloat16 [2048], P('fsdp'), may hold values from 0.5 to 1.5
- w_query: bfloat16 [2048, 2048], P('fsdp', 'tensor'), may hold values from -0.1875 to 0.1875
- w_key: bfloat16 [2048, 2048], P('fsdp', 'tensor'), may hold values from -0.1875 to 0.1875
- w_value: bfloat16 [2048, 2048], P('fsdp', 'tensor'), may hold values from -0.125 to 0.125
- w_out: bfloat16 [2048, 2048], P('fsdp', 'tensor'), may hold values from -0.75 to 0.75
- mlp_gain: bfloat16 [2048], P('fsdp'), may hold values from 0.5 to 1.5
- w_gate: bfloat16 [2048, 8192], P('fsdp', 'tensor'), may hold values from -0.125 to 0.125
- w_up: bfloat16 [2048, 8192], P('fsdp', 'tensor'), may hold values from -0.125 to 0.125
- w_down: bfloat16 [2048, 8192], P('fsdp', 'tensor'), may hold values from -0.09375 to 0.09375
Outputs:
- output: bfloat16 [2, 4, 1024, 2048], P(None, 'tensor', 'fsdp')
- input_grad: float32 [2, 4, 1024, 2048], P(None, 'tensor', 'fsdp')
- attn_gain_grad: float32 [2048], P('fsdp')
- w_query_grad: float32 [2048, 2048], P('fsdp', 'tensor')
- w_key_grad: float32 [2048, 2048], P('fsdp', 'tensor')
- w_value_grad: float32 [2048, 2048], P('fsdp', 'tensor')
- w_out_grad: float32 [2048, 2048], P('fsdp', 'tensor')
- mlp_gain_grad: float32 [2048], P('fsdp')
- w_gate_grad: float32 [2048, 8192], P('fsdp', 'tensor')
- w_up_grad: float32 [2048, 8192], P('fsdp', 'tensor')
- w_down_grad: float32 [2048, 8192], P('fsdp', 'tensor')
- rms_stats: float32 [2, 4, 3], P(None, 'tensor')
The draws below stay inside these ranges and needn't reach their ends.
Inputs may be any that keep to these rules, and one draw needn't show every extreme that they name: Within each sequence positions start at 0 and rise by 1 or 2 from token to token, by 2 at exactly 512 of the steps, so every sequence ends at the max.
All inputs are finite; a program needn't handle non-finite values.
Results may differ from the reference program's by a relative error of at most 0.023.
Values may be sent and summed in bfloat16 or wider, within the bound.
No kernel may reach another device: no remote copies, remote signals or barrier semaphores. Data moves between devices by JAX's collectives and lax.ppermute only.
A program may use at most 192 MiB of HBM per device.

```python
import math
import jax
import jax.numpy as jnp
from jax import lax

D = 2048
HEADS = 32
HEAD_DIM = 64
FF = 8192
SEQ_LEN = 1024
MICRO = 2
SEQ_MB = 4


def draw_positions(key, part):
    row_keys = jax.random.split(key, MICRO * SEQ_MB)
    orders = jax.vmap(lambda one_key: jax.random.permutation(one_key, SEQ_LEN - 1))(row_keys)
    increments = 1 + (orders < SEQ_LEN // 2).astype(jnp.int32)
    summed = jnp.cumsum(increments, axis=-1)
    starts = jnp.zeros((MICRO * SEQ_MB, 1), jnp.int32)
    whole = jnp.concatenate([starts, summed.astype(jnp.int32)], axis=-1)
    return whole.reshape(MICRO, SEQ_MB, SEQ_LEN).astype(jnp.int32)


def plant(values, rng, smallest, top_value):
    place = [jax.random.randint(jax.random.fold_in(rng, axis), (), 0, length) for axis, length in enumerate(values.shape)]
    widest = values.shape.index(max(values.shape))
    neighbour = place[:widest] + [(place[widest] + 1) % values.shape[widest]] + place[widest + 1:]
    return values.at[tuple(place)].set(smallest).at[tuple(neighbour)].set(top_value)


def levels(key, shape, shards, least, top_value):
    level = 1.0
    for dim, blocks in shards:
        steps = jax.random.uniform(jax.random.fold_in(jax.random.fold_in(key, 6), dim), (blocks,), jnp.float32, least / len(shards), top_value / len(shards))
        level = level * jnp.repeat(jnp.exp(steps), shape[dim] // blocks).reshape((-1,) + (1,) * (len(shape) - 1 - dim))
    return level


def bell_draw(stream_key, dims, scale, reach, cuts=(), kind=jnp.bfloat16):
    values = jax.random.normal(stream_key, dims, jnp.float32) * scale
    if len(cuts) > 0:
        values = levels(stream_key, dims, cuts, -0.22, 0.18) * values
    return jnp.clip(values, min=-reach, max=reach).astype(kind)


def setup_inputs(seed: int = 0) -> dict:
    streams_of = jax.random.split(jax.random.key(seed), 14)
    inputs = bell_draw(streams_of[0], (MICRO, SEQ_MB, SEQ_LEN, D), 1.0, 6.0, ((1, 4), (2, 8)))
    out_grads = bell_draw(streams_of[1], (MICRO, SEQ_MB, SEQ_LEN, D), 1.0, 6.0, ((1, 4), (2, 8)))
    prefix_len = plant(jax.random.randint(streams_of[2], (MICRO, SEQ_MB), SEQ_LEN // 10, SEQ_LEN // 2 + 1), jax.random.fold_in(streams_of[2], 1), SEQ_LEN // 10, (SEQ_LEN // 2 + 1) - 1).astype(jnp.int32)
    positions = draw_positions(jax.random.fold_in(streams_of[13], 71), 0)
    attn_gain = jnp.clip(1.0 + 0.1 * jax.random.normal(streams_of[4], (D,), jnp.float32), 0.5, 1.5).astype(jnp.bfloat16)
    w_query = bell_draw(streams_of[5], (D, D), (D // 2) ** -0.5, 0.1875, ((0, 8), (1, 4)))
    w_key = bell_draw(streams_of[6], (D, D), (D // 2) ** -0.5, 0.1875, ((0, 8), (1, 4)))
    w_value = bell_draw(streams_of[7], (D, D), D ** -0.5, 0.125, ((0, 8), (1, 4)))
    w_out = bell_draw(streams_of[8], (D, D), (D // 32) ** -0.5, 0.75, ((0, 8), (1, 4)))
    mlp_gain = jnp.clip(1.0 + 0.1 * jax.random.normal(streams_of[9], (D,), jnp.float32), 0.5, 1.5).astype(jnp.bfloat16)
    w_gate = bell_draw(streams_of[10], (D, FF), D ** -0.5, 0.125, ((0, 8), (1, 4)))
    w_up = bell_draw(streams_of[11], (D, FF), D ** -0.5, 0.125, ((0, 8), (1, 4)))
    w_down = bell_draw(streams_of[12], (D, FF), (FF // 2) ** -0.5, 0.09375, ((0, 8), (1, 4)))
    return dict(inputs=inputs, out_grads=out_grads, prefix_len=prefix_len, positions=positions, attn_gain=attn_gain, w_query=w_query, w_key=w_key, w_value=w_value, w_out=w_out, mlp_gain=mlp_gain, w_gate=w_gate, w_up=w_up, w_down=w_down)


rope_base = 130000.0
norm_eps = 1e-05
stat_eps = 1e-06

@jax.custom_vjp
def low(v):
    return lax.optimization_barrier(v.astype(jnp.bfloat16)).astype(jnp.float32)

@jax.custom_vjp
def low_back(v):
    return v

def low_keep(v):
    return (low(v), None)

def low_pass(kept, grad):
    return (grad,)

def back_keep(v):
    return (v, None)

def back_low(kept, grad):
    return (low(grad),)
low.defvjp(low_keep, low_pass)
low_back.defvjp(back_keep, back_low)

def rms_scale(values, gain):
    return values * lax.rsqrt(lax.optimization_barrier(jnp.mean(values * values, axis=-1, keepdims=True)) + norm_eps) * gain

def rope_tables(token_pos):
    half_dim = HEAD_DIM // 2
    ladder = jnp.arange(half_dim, dtype=jnp.float32) * (2.0 / HEAD_DIM)
    inverse = 1.0 / rope_base ** ladder
    angles = token_pos.astype(jnp.float32)[..., None] * inverse
    return (jnp.cos(angles)[..., None, :], jnp.sin(angles)[..., None, :])

def rotate(values, cos_tab, sin_tab):
    half_dim = HEAD_DIM // 2
    first_half = values[..., :half_dim]
    second = values[..., half_dim:]
    return jnp.concatenate([first_half * cos_tab - second * sin_tab, second * cos_tab + first_half * sin_tab], axis=-1)

def project(left_side, right_side, form):
    return jnp.einsum(form, left_side, right_side, precision=lax.Precision.HIGHEST)

def attend(packed):
    queries, keys, values, prefix = packed
    scores = jnp.einsum('qhd,khd->hqk', queries, keys, precision=lax.Precision.HIGHEST) * HEAD_DIM ** (-0.5)
    scores = low_back(scores)
    index = jnp.arange(SEQ_LEN, dtype=jnp.int32)
    allowed = (index[None, :] <= index[:, None]) | (index[None, :] < prefix)
    probs = jax.nn.softmax(jnp.where(allowed[None], scores, -1e+30), axis=-1)
    return jnp.einsum('hqk,khd->qhd', low(probs), values, precision=lax.Precision.HIGHEST)

def layer(params, block_in, token_pos, prefix):
    attn_gain, w_query, w_key, w_value, w_out, mlp_gain, w_gate, w_up, w_down = params
    groups = block_in.shape[0]
    shape_four = (groups, SEQ_LEN, HEADS, HEAD_DIM)
    normed = low(rms_scale(block_in, attn_gain))
    q_raw = low_back(project(normed, w_query, 'gtd,de->gte'))
    k_raw = low_back(project(normed, w_key, 'gtd,de->gte'))
    v_all = low(low_back(project(normed, w_value, 'gtd,de->gte')))
    cos_tab, sin_tab = rope_tables(token_pos)
    queries = low(rotate(q_raw.reshape(shape_four), cos_tab, sin_tab))
    keys = low(rotate(k_raw.reshape(shape_four), cos_tab, sin_tab))
    values = v_all.reshape(shape_four)
    mixed = lax.map(jax.checkpoint(attend), (queries, keys, values, prefix))
    mixed = low(low_back(mixed.reshape(groups, SEQ_LEN, D)))
    branch = low_back(project(mixed, w_out, 'gte,de->gtd'))
    resid = block_in + branch
    normed_mlp = low(rms_scale(resid, mlp_gain))
    gate_val = low_back(project(normed_mlp, w_gate, 'gtd,df->gtf'))
    up_val = low_back(project(normed_mlp, w_up, 'gtd,df->gtf'))
    hidden = low(gate_val * jax.nn.sigmoid(gate_val) * up_val)
    mlp_out = low_back(project(hidden, w_down, 'gtf,df->gtd'))
    return (resid + mlp_out, (branch, mlp_out))

def reference(inputs, out_grads, prefix_len, positions, attn_gain, w_query, w_key, w_value, w_out, mlp_gain, w_gate, w_up, w_down):
    params = tuple((weight.astype(jnp.float32) for weight in (attn_gain, w_query, w_key, w_value, w_out, mlp_gain, w_gate, w_up, w_down)))
    total_seqs = MICRO * SEQ_MB
    group_size = math.gcd(max(1, 4096 // SEQ_LEN), total_seqs)
    n_groups = total_seqs // group_size
    block_in = inputs.astype(jnp.float32).reshape(n_groups, group_size, SEQ_LEN, D)
    block_grad = out_grads.astype(jnp.float32).reshape(n_groups, group_size, SEQ_LEN, D)
    prefix = prefix_len.reshape(n_groups, group_size)
    token_pos = positions.reshape(n_groups, group_size, SEQ_LEN)

    def group_step(sums, packed):
        x_in, grad_out, pre_len, pos_ids = packed

        def forward(weights, values):
            return layer(weights, values, pos_ids, pre_len)
        result, pull_back, aux = jax.vjp(forward, params, x_in, has_aux=True)
        branch, mlp_out = aux
        weight_grads, in_grad = pull_back(grad_out)
        sums = jax.tree.map(jnp.add, sums, weight_grads)
        index = jnp.arange(SEQ_LEN, dtype=jnp.int32)
        valid = (index[None, :] >= pre_len[:, None])[..., None]
        counts = ((SEQ_LEN - pre_len) * D).astype(jnp.float32)
        stats = [jnp.sqrt(lax.optimization_barrier(jnp.sum(jnp.where(valid, part * part, 0.0), axis=(1, 2))) / counts + stat_eps) for part in (result, branch, mlp_out)]
        return (sums, (result.astype(jnp.bfloat16), in_grad, jnp.stack(stats, axis=-1)))
    zero_grads = tuple((jnp.zeros_like(weight) for weight in params))
    sums, outs = lax.scan(group_step, zero_grads, (block_in, block_grad, prefix, token_pos))
    outputs, in_grads, stats = outs
    return (outputs.reshape(MICRO, SEQ_MB, SEQ_LEN, D), in_grads.reshape(MICRO, SEQ_MB, SEQ_LEN, D), sums[0], sums[1], sums[2], sums[3], sums[4], sums[5], sums[6], sums[7], sums[8], stats.reshape(MICRO, SEQ_MB, 3))
```

```python
import math

import jax
import jax.numpy as jnp
from jax import lax
from jax.experimental import pallas as pl
from jax.experimental.pallas import tpu as pltpu
from jax.sharding import PartitionSpec as P

HEAD_DIM = 64

rope_base = 130000.0
norm_eps = 1e-05
stat_eps = 1e-06
LOG2E = math.log2(math.e)
MASKED = -1e30
BF16 = jnp.bfloat16
F32 = jnp.float32


def dot(left, right, left_dim, right_dim):
    return lax.dot_general(
        left, right, (((left_dim,), (right_dim,)), ((), ())), preferred_element_type=F32
    )


def normalize(values):
    row_scale = lax.rsqrt(jnp.mean(values * values, axis=-1, keepdims=True) + norm_eps)
    return (values * row_scale, row_scale)


def norm_back(grad_in, unit_rows, row_scale, gain):
    scaled = grad_in * gain
    inner_mean = jnp.mean(scaled * unit_rows, axis=-1, keepdims=True)
    return (
        row_scale * (scaled - unit_rows * inner_mean),
        jnp.sum(grad_in * unit_rows, axis=(0, 1)),
    )


def rotate(values, cos_tab, sin_tab, rot_sign):
    first_half = values[..., 0, :, :]
    second = values[..., 1, :, :]
    return jnp.stack(
        [
            first_half * cos_tab - rot_sign * second * sin_tab,
            second * cos_tab + rot_sign * first_half * sin_tab,
        ],
        axis=-3,
    )


def swap(value, axis, distance):
    count = lax.axis_size(axis)
    return lax.ppermute(value, axis, [(a, a ^ distance) for a in range(count)])


def spread(value):
    blocks = [value]
    for k in range(1, lax.axis_size("tensor")):
        blocks.append(swap(value, "tensor", k))
    return jnp.concatenate(blocks, axis=0)


def collect(parts):
    count = lax.axis_size("tensor")
    own = parts.shape[0] // count
    total = parts[:own]
    for k in range(1, count):
        total = total + swap(parts[k * own : (k + 1) * own].astype(BF16), "tensor", k).astype(F32)
    return total


def tree_sum(value, axis):
    step = 1
    while step < lax.axis_size(axis):
        value = value + swap(value, axis, step)
        step *= 2
    return value


def span_block(ref, first, count, lo, hi):
    return jnp.concatenate([ref[first + i, 0, lo:hi, :] for i in range(count)], axis=1)


def attn_blocks(spans, span_len):
    group = max(1, min(spans, 256 // span_len))
    while spans % group:
        group -= 1
    return group, spans // group


def key_count(q_block, block, prefix, blocks):
    return jnp.minimum(jnp.maximum(q_block + 1, (prefix + block - 1) // block), blocks)


def allowed_mask(k_block, q_block, block, prefix):
    key_id = k_block * block + lax.broadcasted_iota(jnp.int32, (block, block), 0)
    query_id = q_block * block + lax.broadcasted_iota(jnp.int32, (block, block), 1)
    return (key_id <= query_id) | (key_id < prefix)


def forward_kernel(prefix_ref, x_ref, out_ref, lse_ref, key_ref):
    spans, _, _, span_len = x_ref.shape
    group, blocks = attn_blocks(spans, span_len)
    block = group * span_len
    prefix = prefix_ref[pl.program_id(0)]
    coef = HEAD_DIM**-0.5 * LOG2E
    for kb in range(blocks):
        key_ref[pl.ds(kb * block, block), :] = span_block(
            x_ref, kb * group, group, HEAD_DIM, 2 * HEAD_DIM
        ).T
    for qb in range(blocks):
        q_t = span_block(x_ref, qb * group, group, 0, HEAD_DIM)

        def step(kb, carry):
            top, total, acc = carry
            keys = key_ref[pl.ds(pl.multiple_of(kb * block, block), block), :]
            scores = dot(keys, q_t, 1, 0) * coef
            scores = jnp.where(allowed_mask(kb, qb, block, prefix), scores, MASKED)
            new_top = jnp.maximum(top, jnp.max(scores, axis=0, keepdims=True))
            probs = jnp.exp2(scores - new_top)
            shrink = jnp.exp2(top - new_top)
            total = shrink * total + jnp.sum(probs, axis=0, keepdims=True)
            v_t = span_block(x_ref, kb * group, group, 2 * HEAD_DIM, 3 * HEAD_DIM)
            acc = shrink * acc + dot(v_t, probs.astype(BF16), 1, 0)
            return new_top, total, acc

        top, total, acc = lax.fori_loop(
            0,
            key_count(qb, block, prefix, blocks),
            step,
            (
                jnp.full((1, block), MASKED, F32),
                jnp.zeros((1, block), F32),
                jnp.zeros((HEAD_DIM, block), F32),
            ),
        )
        out = (acc / total).astype(BF16)
        for i in range(group):
            out_ref[qb * group + i, 0] = out[:, i * span_len : (i + 1) * span_len]
        lse_ref[0, :, qb * block : (qb + 1) * block] = top + jnp.log2(total)


def backward_kernel(
    prefix_ref, x_ref, o_ref, do_ref, lse_ref, dx_ref, key_ref, val_ref, dk_ref, dv_ref
):
    spans, _, _, span_len = x_ref.shape
    group, blocks = attn_blocks(spans, span_len)
    block = group * span_len
    prefix = prefix_ref[pl.program_id(0)]
    scale = HEAD_DIM**-0.5
    coef = scale * LOG2E
    for kb in range(blocks):
        rows = pl.ds(kb * block, block)
        key_ref[rows, :] = span_block(x_ref, kb * group, group, HEAD_DIM, 2 * HEAD_DIM).T
        val_ref[rows, :] = span_block(x_ref, kb * group, group, 2 * HEAD_DIM, 3 * HEAD_DIM).T
    dk_ref[...] = jnp.zeros_like(dk_ref)
    dv_ref[...] = jnp.zeros_like(dv_ref)
    for qb in range(blocks):
        q_t = span_block(x_ref, qb * group, group, 0, HEAD_DIM)
        do_t = span_block(do_ref, qb * group, group, 0, HEAD_DIM)
        o_t = span_block(o_ref, qb * group, group, 0, HEAD_DIM)
        delta = jnp.sum(do_t.astype(F32) * o_t.astype(F32), axis=0, keepdims=True)
        lse = lse_ref[0, :, qb * block : (qb + 1) * block]

        def step(kb, dq):
            rows = pl.ds(pl.multiple_of(kb * block, block), block)
            scores = dot(key_ref[rows, :], q_t, 1, 0) * coef
            scores = jnp.where(allowed_mask(kb, qb, block, prefix), scores, MASKED)
            probs = jnp.exp2(scores - lse)
            grad_probs = dot(val_ref[rows, :], do_t, 1, 0)
            grad_scores = (probs * (grad_probs - delta)).astype(BF16)
            dv_ref[kb] += dot(do_t, probs.astype(BF16), 1, 1)
            dk_ref[kb] += dot(q_t, grad_scores, 1, 1)
            k_t = span_block(x_ref, kb * group, group, HEAD_DIM, 2 * HEAD_DIM)
            return dq + dot(k_t, grad_scores, 1, 0)

        dq = lax.fori_loop(
            0,
            key_count(qb, block, prefix, blocks),
            step,
            jnp.zeros((HEAD_DIM, block), F32),
        )
        dq = (dq * scale).astype(BF16)
        for i in range(group):
            dx_ref[qb * group + i, 0, :HEAD_DIM, :] = dq[:, i * span_len : (i + 1) * span_len]
    for kb in range(blocks):
        dk = (dk_ref[kb] * scale).astype(BF16)
        dv = dv_ref[kb].astype(BF16)
        for i in range(group):
            cols = slice(i * span_len, (i + 1) * span_len)
            dx_ref[kb * group + i, 0, HEAD_DIM : 2 * HEAD_DIM, :] = dk[:, cols]
            dx_ref[kb * group + i, 0, 2 * HEAD_DIM :, :] = dv[:, cols]


def pair_spec(shape):
    return pl.BlockSpec((shape[0], 1) + shape[2:], lambda p, pre: (0, p, 0, 0))


def lse_spec(tokens):
    return pl.BlockSpec((1, 1, tokens), lambda p, pre: (p, 0, 0))


def attend_forward(prefix, packed):
    spans, pairs, width, span_len = packed.shape
    tokens = spans * span_len
    out_shape = (spans, pairs, HEAD_DIM, span_len)
    return pl.pallas_call(
        forward_kernel,
        out_shape=(
            jax.ShapeDtypeStruct(out_shape, BF16),
            jax.ShapeDtypeStruct((pairs, 1, tokens), F32),
        ),
        grid_spec=pltpu.PrefetchScalarGridSpec(
            num_scalar_prefetch=1,
            grid=(pairs,),
            in_specs=[pair_spec(packed.shape)],
            out_specs=[pair_spec(out_shape), lse_spec(tokens)],
            scratch_shapes=[pltpu.VMEM((tokens, HEAD_DIM), BF16)],
        ),
        compiler_params=pltpu.CompilerParams(dimension_semantics=("arbitrary",)),
        name="attend_forward",
    )(prefix, packed)


def attend_back(prefix, packed, out, grad_out, lse):
    spans, pairs, width, span_len = packed.shape
    tokens = spans * span_len
    group, blocks = attn_blocks(spans, span_len)
    acc = pltpu.VMEM((blocks, HEAD_DIM, group * span_len), F32)
    return pl.pallas_call(
        backward_kernel,
        out_shape=jax.ShapeDtypeStruct(packed.shape, BF16),
        grid_spec=pltpu.PrefetchScalarGridSpec(
            num_scalar_prefetch=1,
            grid=(pairs,),
            in_specs=[
                pair_spec(packed.shape),
                pair_spec(out.shape),
                pair_spec(out.shape),
                lse_spec(tokens),
            ],
            out_specs=pair_spec(packed.shape),
            scratch_shapes=[
                pltpu.VMEM((tokens, HEAD_DIM), BF16),
                pltpu.VMEM((tokens, HEAD_DIM), BF16),
                acc,
                acc,
            ],
        ),
        compiler_params=pltpu.CompilerParams(dimension_semantics=("arbitrary",)),
        name="attend_back",
    )(prefix, packed, out, grad_out, lse)


class HeadSplit:
    def __init__(self, n_fsdp, head_count, seqs, span_len):
        self.head_groups = math.gcd(n_fsdp, head_count)
        self.seq_groups = n_fsdp // self.head_groups
        self.heads_per = head_count // self.head_groups
        self.seqs_per = seqs // self.seq_groups
        self.span_len = span_len
        self.pairs = self.heads_per * self.seqs_per

    def to_heads(self, stack):
        kinds = stack.shape[0]
        stack = stack.reshape(
            kinds,
            self.head_groups,
            self.heads_per,
            HEAD_DIM,
            self.seq_groups,
            self.seqs_per,
            self.span_len,
        )
        stack = stack.transpose(4, 1, 2, 5, 0, 3, 6)
        stack = stack.reshape(-1, self.pairs, kinds * HEAD_DIM, self.span_len)
        return lax.all_to_all(stack, "fsdp", split_axis=0, concat_axis=0, tiled=True)

    def to_spans(self, stack):
        kinds = stack.shape[2] // HEAD_DIM
        stack = lax.all_to_all(stack, "fsdp", split_axis=0, concat_axis=0, tiled=True)
        stack = stack.reshape(
            self.seq_groups,
            self.head_groups,
            self.heads_per,
            self.seqs_per,
            kinds,
            HEAD_DIM,
            self.span_len,
        )
        stack = stack.transpose(4, 1, 2, 5, 0, 3, 6)
        return stack.reshape(
            kinds,
            self.head_groups * self.heads_per * HEAD_DIM,
            self.seq_groups * self.seqs_per * self.span_len,
        )

    def pair_prefix(self, prefix, fsdp_index):
        mine = lax.dynamic_slice_in_dim(
            prefix, (fsdp_index // self.head_groups) * self.seqs_per, self.seqs_per, 0
        )
        return jnp.tile(mine, self.heads_per)


def body(
    inputs,
    out_grads,
    prefix_len,
    positions,
    attn_gain,
    w_query,
    w_key,
    w_value,
    w_out,
    mlp_gain,
    w_gate,
    w_up,
    w_down,
):
    micro_count, seq_dev, span_len, model_width = inputs.shape
    n_tensor = lax.axis_size("tensor")
    n_fsdp = lax.axis_size("fsdp")
    seq_mb = seq_dev * n_tensor
    seq_len = span_len * n_fsdp
    row_count = seq_mb * span_len
    own_rows = seq_dev * span_len
    head_cols = w_query.shape[1]
    head_count = head_cols // HEAD_DIM
    ff_cols = w_gate.shape[1]
    fsdp_index = lax.axis_index("fsdp")
    tensor_index = lax.axis_index("tensor")
    query_index = fsdp_index * span_len + jnp.arange(span_len, dtype=jnp.int32)
    split = HeadSplit(n_fsdp, head_count, seq_mb, span_len)
    micros = range(micro_count)

    def gather(shard):
        return lax.all_gather(shard, "fsdp", axis=0, tiled=True)

    def scatter(grad):
        return lax.psum_scatter(grad, "fsdp", scatter_dimension=0, tiled=True).astype(F32)

    gains = lax.all_gather(jnp.stack([attn_gain, mlp_gain]), "fsdp", axis=1, tiled=True)
    gain_attn = gains[0].astype(F32)
    gain_mlp = gains[1].astype(F32)
    full_qkv = gather(jnp.concatenate([w_query, w_key, w_value], axis=1))
    full_out = gather(w_out)
    full_gu = gather(jnp.concatenate([w_gate, w_up], axis=1))
    full_down = gather(w_down)

    order = (
        ((tensor_index ^ jnp.arange(n_tensor, dtype=jnp.int32)) * seq_dev)[:, None]
        + jnp.arange(seq_dev, dtype=jnp.int32)
    ).reshape(-1)
    prefix_all = jnp.take(prefix_len, order, axis=1)
    own_prefix = prefix_all[:, :seq_dev]
    pos_all = jnp.take(positions, order, axis=1)
    half_dim = HEAD_DIM // 2
    ladder = jnp.arange(half_dim, dtype=F32) * (2.0 / HEAD_DIM)
    inverse = 1.0 / rope_base**ladder

    x_float, unit_attn, scale_attn, normed_rows, grad_rows = [], [], [], [], []
    cos_tab, sin_tab, pair_prefix = [], [], []
    packed, attn_out, attn_lse = [], [], []
    for m in micros:
        x = inputs[m].astype(F32)
        unit, scale = normalize(x)
        normed = (unit * gain_attn).astype(BF16)
        x_float.append(x)
        unit_attn.append(unit)
        scale_attn.append(scale)
        normed_rows.append(spread(normed.reshape(own_rows, model_width)))
        angles = inverse[:, None] * pos_all[m].astype(F32).reshape(-1)[None, :]
        cos_tab.append(jnp.cos(angles))
        sin_tab.append(jnp.sin(angles))
        pair_prefix.append(split.pair_prefix(prefix_all[m], fsdp_index))
    for m in micros:
        grad_rows.append(spread(out_grads[m].reshape(own_rows, model_width)))
    for m in micros:
        raw = dot(full_qkv, normed_rows[m], 0, 1).reshape(3, head_cols, row_count)
        turned = rotate(
            raw[:2].reshape(2, head_count, 2, half_dim, row_count), cos_tab[m], sin_tab[m], 1.0
        ).reshape(2, head_cols, row_count)
        stack = jnp.concatenate([turned.astype(BF16), raw[2:].astype(BF16)], axis=0)
        packed.append(split.to_heads(stack))
    mix_t, branch, resid, unit_mlp, scale_mlp, mlp_rows = [], [], [], [], [], []
    for m in micros:
        out, lse = attend_forward(pair_prefix[m], packed[m])
        attn_out.append(out)
        attn_lse.append(lse)
        mix = split.to_spans(out)[0]
        mix_t.append(mix)
        part = collect(dot(mix, full_out, 0, 1)).reshape(seq_dev, span_len, model_width)
        res = x_float[m] + part
        unit, scale = normalize(res)
        branch.append(part)
        resid.append(res)
        unit_mlp.append(unit)
        scale_mlp.append(scale)
        normed = (unit * gain_mlp).astype(BF16)
        mlp_rows.append(spread(normed.reshape(own_rows, model_width)))

    hidden, gate_val, up_val = [], [], []
    for m in micros:
        gate_up = dot(mlp_rows[m], full_gu, 1, 0)
        gate = gate_up[:, :ff_cols]
        up = gate_up[:, ff_cols:]
        gate_val.append(gate)
        up_val.append(up)
        hidden.append((gate * jax.nn.sigmoid(gate) * up).astype(BF16))
    down_grad = dot(
        jnp.concatenate(grad_rows, axis=0), jnp.concatenate(hidden, axis=0), 0, 0
    ).astype(BF16)
    own_down = scatter(down_grad)
    grad_gu = []
    for m in micros:
        grad_hidden = dot(grad_rows[m], full_down, 1, 0)
        sig = jax.nn.sigmoid(gate_val[m])
        slope = sig * (1.0 + gate_val[m] * (1.0 - sig))
        grad_gu.append(
            jnp.concatenate(
                [
                    (grad_hidden * up_val[m] * slope).astype(BF16),
                    (grad_hidden * gate_val[m] * sig).astype(BF16),
                ],
                axis=1,
            )
        )
    gu_grad = dot(
        jnp.concatenate(mlp_rows, axis=0), jnp.concatenate(grad_gu, axis=0), 0, 0
    ).astype(BF16)
    own_gu = scatter(gu_grad)
    grad_resid, grad_mix, branch_rows = [], [], []
    mlp_gain_sum = jnp.zeros((model_width,), F32)
    for m in micros:
        grad_normed = collect(dot(grad_gu[m], full_gu, 1, 1)).reshape(
            seq_dev, span_len, model_width
        )
        part, gain_part = norm_back(grad_normed, unit_mlp[m], scale_mlp[m], gain_mlp)
        mlp_gain_sum = mlp_gain_sum + gain_part
        grad_res = out_grads[m].astype(F32) + part
        grad_resid.append(grad_res)
        rows = spread(grad_res.astype(BF16).reshape(own_rows, model_width))
        branch_rows.append(rows)
        grad_mix.append(dot(full_out, rows, 0, 1).astype(BF16))
    out_grad = dot(
        jnp.concatenate(branch_rows, axis=0), jnp.concatenate(mix_t, axis=1), 0, 1
    ).astype(BF16)
    own_out = scatter(out_grad)

    out_list, stat_list = [], []
    for m in micros:
        mlp_out = collect(dot(hidden[m], full_down, 1, 1)).reshape(seq_dev, span_len, model_width)
        result = resid[m] + mlp_out
        out_list.append(result.astype(BF16))
        valid = (query_index[None, :] >= own_prefix[m][:, None])[..., None]
        stat_list.append(
            jnp.stack(
                [
                    jnp.sum(jnp.where(valid, part * part, 0.0), axis=(1, 2))
                    for part in (result, branch[m], mlp_out)
                ],
                axis=-1,
            )
        )

    grad_qkv = []
    for m in micros:
        grad_out = split.to_heads(grad_mix[m][None])
        packed_grad = attend_back(pair_prefix[m], packed[m], attn_out[m], grad_out, attn_lse[m])
        raw = split.to_spans(packed_grad)
        turned = rotate(
            raw[:2].reshape(2, head_count, 2, half_dim, row_count).astype(F32),
            cos_tab[m],
            sin_tab[m],
            -1.0,
        ).reshape(2, head_cols, row_count)
        grad_qkv.append(
            jnp.concatenate([turned.astype(BF16), raw[2:]], axis=0).reshape(
                3 * head_cols, row_count
            )
        )
    qkv_grad = dot(
        jnp.concatenate(normed_rows, axis=0), jnp.concatenate(grad_qkv, axis=1), 0, 1
    ).astype(BF16)
    own_qkv = scatter(qkv_grad)
    grad_list = []
    attn_gain_sum = jnp.zeros((model_width,), F32)
    for m in micros:
        grad_normed = collect(dot(grad_qkv[m], full_qkv, 0, 1)).reshape(
            seq_dev, span_len, model_width
        )
        part, gain_part = norm_back(grad_normed, unit_attn[m], scale_attn[m], gain_attn)
        attn_gain_sum = attn_gain_sum + gain_part
        grad_list.append(grad_resid[m] + part)

    stats = jnp.stack(stat_list, axis=0)
    stat_sum = tree_sum(stats, "fsdp")
    gain_sum = tree_sum(tree_sum(jnp.stack([attn_gain_sum, mlp_gain_sum]), "tensor"), "fsdp")
    row_share = model_width // n_fsdp
    own_gain = lax.dynamic_slice_in_dim(gain_sum, fsdp_index * row_share, row_share, 1)
    counts = ((seq_len - own_prefix) * model_width).astype(F32)
    rms_stats = jnp.sqrt(stat_sum / counts[..., None] + stat_eps)
    return (
        jnp.stack(out_list, axis=0),
        jnp.stack(grad_list, axis=0),
        own_gain[0],
        own_qkv[:, :head_cols],
        own_qkv[:, head_cols : 2 * head_cols],
        own_qkv[:, 2 * head_cols :],
        own_out,
        own_gain[1],
        own_gu[:, :ff_cols],
        own_gu[:, ff_cols:],
        own_down,
        rms_stats,
    )


def solution(mesh):
    in_specs = (
        P(None, "tensor", "fsdp", None),
        P(None, "tensor", "fsdp", None),
        P(),
        P(None, None, "fsdp"),
        P("fsdp"),
        P("fsdp", "tensor"),
        P("fsdp", "tensor"),
        P("fsdp", "tensor"),
        P("fsdp", "tensor"),
        P("fsdp"),
        P("fsdp", "tensor"),
        P("fsdp", "tensor"),
        P("fsdp", "tensor"),
    )
    out_specs = (
        P(None, "tensor", "fsdp", None),
        P(None, "tensor", "fsdp", None),
        P("fsdp"),
        P("fsdp", "tensor"),
        P("fsdp", "tensor"),
        P("fsdp", "tensor"),
        P("fsdp", "tensor"),
        P("fsdp"),
        P("fsdp", "tensor"),
        P("fsdp", "tensor"),
        P("fsdp", "tensor"),
        P(None, "tensor", None),
    )
    return jax.shard_map(body, mesh=mesh, in_specs=in_specs, out_specs=out_specs, check_vma=False)
```

```python
import math

import jax
import jax.numpy as jnp
from jax import lax
from jax.experimental import pallas as pl
from jax.experimental.pallas import tpu as pltpu
from jax.sharding import PartitionSpec as P

HEAD_DIM = 64

rope_base = 130000.0
norm_eps = 1e-05
stat_eps = 1e-06
LOG2E = math.log2(math.e)
MASKED = -1e30
PAIR = 2
BF16 = jnp.bfloat16
F32 = jnp.float32


def dot(left, right, left_dim, right_dim):
    return lax.dot_general(
        left, right, (((left_dim,), (right_dim,)), ((), ())), preferred_element_type=F32
    )


def normalize(values):
    row_scale = lax.rsqrt(jnp.mean(values * values, axis=-1, keepdims=True) + norm_eps)
    return (values * row_scale, row_scale)


def norm_back(grad_in, unit_rows, row_scale, gain):
    scaled = grad_in * gain
    inner_mean = jnp.mean(scaled * unit_rows, axis=-1, keepdims=True)
    return (
        row_scale * (scaled - unit_rows * inner_mean),
        jnp.sum(grad_in * unit_rows, axis=tuple(range(grad_in.ndim - 1))),
    )


def rotate(values, cos_tab, sin_tab, rot_sign):
    first_half = values[..., 0, :, :]
    second = values[..., 1, :, :]
    return jnp.stack(
        [
            first_half * cos_tab - rot_sign * second * sin_tab,
            second * cos_tab + rot_sign * first_half * sin_tab,
        ],
        axis=-3,
    )


def swap(value, axis, distance):
    count = lax.axis_size(axis)
    return lax.ppermute(value, axis, [(a, a ^ distance) for a in range(count)])


def after(value, *others):
    return lax.optimization_barrier((value, others))[0]


def spread(value, direct=True):
    count = lax.axis_size("tensor")
    if direct or count != 4:
        return [value] + [swap(value, "tensor", k) for k in range(1, count)]
    half = value.shape[0] // 2
    one = swap(value, "tensor", 1)
    two = swap(value, "tensor", 2)
    low = swap(two[:half], "tensor", 1)
    high = swap(one[half:], "tensor", 2)
    return [value, one, two, jnp.concatenate([low, high], axis=0)]


def collect(parts, direct=True, token=None):
    count = lax.axis_size("tensor")
    if direct or count != 4:
        blocks = [swap(parts[k].astype(BF16), "tensor", k) for k in range(1, count)]
        if token is not None:
            blocks = after(blocks, token)
        total = parts[0]
        for block in blocks:
            total = total + block.astype(F32)
        return total
    half = parts[0].shape[0] // 2
    far = parts[3].astype(BF16)
    low = swap(far[:half], "tensor", 1).astype(F32)
    high = swap(far[half:], "tensor", 2).astype(F32)
    one = jnp.concatenate([parts[1][:half], parts[1][half:] + high], axis=0)
    two = jnp.concatenate([parts[2][:half] + low, parts[2][half:]], axis=0)
    one = swap(one.astype(BF16), "tensor", 1).astype(F32)
    two = swap(two.astype(BF16), "tensor", 2).astype(F32)
    return parts[0] + one + two


def pair_join(value, micros):
    other = swap(value, "fsdp", PAIR)
    size = value.shape[0] // micros
    parts = [v[m * size : (m + 1) * size] for m in range(micros) for v in (value, other)]
    return jnp.concatenate(parts, axis=0)


def gather_rows(blocks, micros):
    size = blocks[0].shape[0] // micros
    return jnp.concatenate(
        [b[m * size : (m + 1) * size] for m in range(micros) for b in blocks], axis=0
    )


def peer_blocks(rows, micros, peers):
    size = rows.shape[0] // (micros * peers)
    return [
        jnp.concatenate(
            [rows[(m * peers + k) * size : (m * peers + k + 1) * size] for m in range(micros)],
            axis=0,
        )
        for k in range(peers)
    ]


def paired(values):
    count = lax.axis_size("fsdp")
    size = values.shape[-1] // count
    order = [(f & ~3) | ((f & 1) << 1) | ((f >> 1) & 1) for f in range(count)]
    parts = [lax.slice_in_dim(values, f * size, (f + 1) * size, axis=-1) for f in order]
    return jnp.concatenate(parts, axis=-1)


def pair_groups():
    count = lax.axis_size("fsdp")
    return [[f for f in range(count) if bool(f & PAIR) == side] for side in (False, True)]


def half_of(shards, side):
    half = shards[0].shape[1] // 2
    return jnp.concatenate(
        [lax.dynamic_slice_in_dim(s, side * half, half, 1) for s in shards], axis=1
    )


def order_pair(side, mine, other):
    return jnp.where(side == 0, mine, other), jnp.where(side == 0, other, mine)


def own_half(side, mine, other):
    return jnp.concatenate(order_pair(side, mine, other), axis=0)


def gather_half(shard):
    return lax.all_gather(
        shard,
        "fsdp",
        axis=0,
        tiled=True,
        axis_index_groups=pair_groups(),
    )


def scatter_half(grad):
    return lax.psum_scatter(
        grad, "fsdp", scatter_dimension=0, tiled=True, axis_index_groups=pair_groups()
    )


def settle_half(part, side, pieces, token):
    rows = part.shape[0] // 2
    mine = lax.dynamic_slice_in_dim(part, side * rows, rows, 0)
    other = swap(lax.dynamic_slice_in_dim(part, (1 - side) * rows, rows, 0), "fsdp", PAIR)
    low, high = order_pair(side, mine, after(other, token))
    half = part.shape[1] // pieces
    return [
        jnp.concatenate(
            [low[:, i * half : (i + 1) * half], high[:, i * half : (i + 1) * half]], axis=1
        ).astype(F32)
        for i in range(pieces)
    ]


def tree_sum(value, axis):
    step = 1
    while step < lax.axis_size(axis):
        value = value + swap(value, axis, step)
        step *= 2
    return value


def span_block(ref, first, count, lo, hi):
    return jnp.concatenate([ref[first + i, 0, lo:hi, :] for i in range(count)], axis=1)


def attn_blocks(spans, span_len):
    group = max(1, min(spans, 256 // span_len))
    while spans % group:
        group -= 1
    return group, spans // group


def key_count(q_block, block, prefix, blocks):
    return jnp.minimum(jnp.maximum(q_block + 1, (prefix + block - 1) // block), blocks)


def allowed_mask(k_block, q_block, block, prefix):
    key_id = k_block * block + lax.broadcasted_iota(jnp.int32, (block, block), 0)
    query_id = q_block * block + lax.broadcasted_iota(jnp.int32, (block, block), 1)
    return (key_id <= query_id) | (key_id < prefix)


def forward_kernel(prefix_ref, x_ref, out_ref, lse_ref, key_ref):
    spans, _, _, span_len = x_ref.shape
    group, blocks = attn_blocks(spans, span_len)
    block = group * span_len
    prefix = prefix_ref[pl.program_id(0)]
    coef = HEAD_DIM**-0.5 * LOG2E
    for kb in range(blocks):
        key_ref[pl.ds(kb * block, block), :] = span_block(
            x_ref, kb * group, group, HEAD_DIM, 2 * HEAD_DIM
        ).T
    for qb in range(blocks):
        q_t = span_block(x_ref, qb * group, group, 0, HEAD_DIM)

        def step(kb, carry):
            top, total, acc = carry
            keys = key_ref[pl.ds(pl.multiple_of(kb * block, block), block), :]
            scores = dot(keys, q_t, 1, 0) * coef
            scores = jnp.where(allowed_mask(kb, qb, block, prefix), scores, MASKED)
            new_top = jnp.maximum(top, jnp.max(scores, axis=0, keepdims=True))
            probs = jnp.exp2(scores - new_top)
            shrink = jnp.exp2(top - new_top)
            total = shrink * total + jnp.sum(probs, axis=0, keepdims=True)
            v_t = span_block(x_ref, kb * group, group, 2 * HEAD_DIM, 3 * HEAD_DIM)
            acc = shrink * acc + dot(v_t, probs.astype(BF16), 1, 0)
            return new_top, total, acc

        top, total, acc = lax.fori_loop(
            0,
            key_count(qb, block, prefix, blocks),
            step,
            (
                jnp.full((1, block), MASKED, F32),
                jnp.zeros((1, block), F32),
                jnp.zeros((HEAD_DIM, block), F32),
            ),
        )
        out = (acc / total).astype(BF16)
        for i in range(group):
            out_ref[qb * group + i, 0] = out[:, i * span_len : (i + 1) * span_len]
        lse_ref[0, :, qb * block : (qb + 1) * block] = top + jnp.log2(total)


def backward_kernel(
    prefix_ref, x_ref, o_ref, do_ref, lse_ref, dx_ref, key_ref, val_ref, dk_ref, dv_ref
):
    spans, _, _, span_len = x_ref.shape
    group, blocks = attn_blocks(spans, span_len)
    block = group * span_len
    prefix = prefix_ref[pl.program_id(0)]
    scale = HEAD_DIM**-0.5
    coef = scale * LOG2E
    for kb in range(blocks):
        rows = pl.ds(kb * block, block)
        key_ref[rows, :] = span_block(x_ref, kb * group, group, HEAD_DIM, 2 * HEAD_DIM).T
        val_ref[rows, :] = span_block(x_ref, kb * group, group, 2 * HEAD_DIM, 3 * HEAD_DIM).T
    dk_ref[...] = jnp.zeros_like(dk_ref)
    dv_ref[...] = jnp.zeros_like(dv_ref)
    for qb in range(blocks):
        q_t = span_block(x_ref, qb * group, group, 0, HEAD_DIM)
        do_t = span_block(do_ref, qb * group, group, 0, HEAD_DIM)
        o_t = span_block(o_ref, qb * group, group, 0, HEAD_DIM)
        delta = jnp.sum(do_t.astype(F32) * o_t.astype(F32), axis=0, keepdims=True)
        lse = lse_ref[0, :, qb * block : (qb + 1) * block]

        def step(kb, dq):
            rows = pl.ds(pl.multiple_of(kb * block, block), block)
            scores = dot(key_ref[rows, :], q_t, 1, 0) * coef
            scores = jnp.where(allowed_mask(kb, qb, block, prefix), scores, MASKED)
            probs = jnp.exp2(scores - lse)
            grad_probs = dot(val_ref[rows, :], do_t, 1, 0)
            grad_scores = (probs * (grad_probs - delta)).astype(BF16)
            dv_ref[kb] += dot(do_t, probs.astype(BF16), 1, 1)
            dk_ref[kb] += dot(q_t, grad_scores, 1, 1)
            k_t = span_block(x_ref, kb * group, group, HEAD_DIM, 2 * HEAD_DIM)
            return dq + dot(k_t, grad_scores, 1, 0)

        dq = lax.fori_loop(
            0,
            key_count(qb, block, prefix, blocks),
            step,
            jnp.zeros((HEAD_DIM, block), F32),
        )
        dq = (dq * scale).astype(BF16)
        for i in range(group):
            dx_ref[qb * group + i, 0, :HEAD_DIM, :] = dq[:, i * span_len : (i + 1) * span_len]
    for kb in range(blocks):
        dk = (dk_ref[kb] * scale).astype(BF16)
        dv = dv_ref[kb].astype(BF16)
        for i in range(group):
            cols = slice(i * span_len, (i + 1) * span_len)
            dx_ref[kb * group + i, 0, HEAD_DIM : 2 * HEAD_DIM, :] = dk[:, cols]
            dx_ref[kb * group + i, 0, 2 * HEAD_DIM :, :] = dv[:, cols]


def pair_spec(shape, first=0):
    return pl.BlockSpec((shape[0], 1) + shape[2:], lambda p, pre: (0, first + p, 0, 0))


def lse_spec(tokens):
    return pl.BlockSpec((1, 1, tokens), lambda p, pre: (p, 0, 0))


def attend_forward(prefix, packed, micro):
    spans, _, _, span_len = packed.shape
    pairs = prefix.shape[0]
    tokens = spans * span_len
    out_shape = (spans, pairs, HEAD_DIM, span_len)
    return pl.pallas_call(
        forward_kernel,
        out_shape=(
            jax.ShapeDtypeStruct(out_shape, BF16),
            jax.ShapeDtypeStruct((pairs, 1, tokens), F32),
        ),
        grid_spec=pltpu.PrefetchScalarGridSpec(
            num_scalar_prefetch=1,
            grid=(pairs,),
            in_specs=[pair_spec(packed.shape, micro * pairs)],
            out_specs=[pair_spec(out_shape), lse_spec(tokens)],
            scratch_shapes=[pltpu.VMEM((tokens, HEAD_DIM), BF16)],
        ),
        compiler_params=pltpu.CompilerParams(dimension_semantics=("arbitrary",)),
        name="attend_forward",
    )(prefix, packed)


def attend_back(prefix, packed, out, grad_out, lse, micro):
    spans, _, width, span_len = packed.shape
    pairs = prefix.shape[0]
    grad_shape = (spans, pairs, width, span_len)
    tokens = spans * span_len
    group, blocks = attn_blocks(spans, span_len)
    acc = pltpu.VMEM((blocks, HEAD_DIM, group * span_len), F32)
    return pl.pallas_call(
        backward_kernel,
        out_shape=jax.ShapeDtypeStruct(grad_shape, BF16),
        grid_spec=pltpu.PrefetchScalarGridSpec(
            num_scalar_prefetch=1,
            grid=(pairs,),
            in_specs=[
                pair_spec(packed.shape),
                pair_spec(out.shape),
                pair_spec(grad_out.shape, micro * pairs),
                lse_spec(tokens),
            ],
            out_specs=pair_spec(grad_shape),
            scratch_shapes=[
                pltpu.VMEM((tokens, HEAD_DIM), BF16),
                pltpu.VMEM((tokens, HEAD_DIM), BF16),
                acc,
                acc,
            ],
        ),
        compiler_params=pltpu.CompilerParams(dimension_semantics=("arbitrary",)),
        name="attend_back",
    )(prefix, packed, out, grad_out, lse)


class HeadSplit:
    def __init__(self, n_fsdp, head_count, seqs, span_len):
        self.head_groups = math.gcd(n_fsdp, head_count)
        self.seq_groups = n_fsdp // self.head_groups
        self.heads_per = head_count // self.head_groups
        self.seqs_per = seqs // self.seq_groups
        self.span_len = span_len

    def to_heads(self, stack):
        kinds = stack.shape[0]
        stack = stack.reshape(
            kinds,
            self.head_groups,
            self.heads_per,
            HEAD_DIM,
            -1,
            self.seq_groups,
            self.seqs_per,
            self.span_len,
        )
        stack = stack.transpose(5, 1, 4, 2, 6, 0, 3, 7)
        count = self.seq_groups * self.head_groups
        stack = stack.reshape(count, -1, kinds * HEAD_DIM, self.span_len)
        return lax.all_to_all(stack, "fsdp", split_axis=0, concat_axis=0, tiled=True)

    def to_spans(self, stack):
        kinds = stack.shape[2] // HEAD_DIM
        stack = lax.all_to_all(stack, "fsdp", split_axis=0, concat_axis=0, tiled=True)
        stack = stack.reshape(
            self.seq_groups,
            self.head_groups,
            -1,
            self.heads_per,
            self.seqs_per,
            kinds,
            HEAD_DIM,
            self.span_len,
        )
        stack = stack.transpose(5, 1, 3, 6, 2, 0, 4, 7)
        return stack.reshape(kinds, self.head_groups * self.heads_per * HEAD_DIM, -1)

    def pair_prefix(self, prefix, fsdp_index):
        mine = lax.dynamic_slice_in_dim(
            prefix, (fsdp_index // self.head_groups) * self.seqs_per, self.seqs_per, 0
        )
        return jnp.tile(mine, self.heads_per)


def layer(
    inputs,
    out_grads,
    prefix_len,
    positions,
    attn_gain,
    w_query,
    w_key,
    w_value,
    w_out,
    mlp_gain,
    w_gate,
    w_up,
    w_down,
):
    micro_count, seq_dev, span_len, model_width = inputs.shape
    n_tensor = lax.axis_size("tensor")
    n_fsdp = lax.axis_size("fsdp")
    seq_mb = seq_dev * n_tensor
    seq_len = span_len * n_fsdp
    row_count = seq_mb * span_len
    own_rows = seq_dev * span_len
    head_cols = w_query.shape[1]
    head_count = head_cols // HEAD_DIM
    ff_cols = w_gate.shape[1]
    fsdp_index = lax.axis_index("fsdp")
    tensor_index = lax.axis_index("tensor")
    query_index = fsdp_index * span_len + jnp.arange(span_len, dtype=jnp.int32)
    split = HeadSplit(n_fsdp, head_count, seq_mb, span_len)
    micros = range(micro_count)

    def gather(shard):
        return lax.all_gather(shard, "fsdp", axis=0, tiled=True)

    def scatter(grad):
        return lax.psum_scatter(grad, "fsdp", scatter_dimension=0, tiled=True).astype(F32)

    gains = lax.all_gather(jnp.stack([attn_gain, mlp_gain]), "fsdp", axis=1, tiled=True)
    gain_attn = gains[0].astype(F32)
    gain_mlp = gains[1].astype(F32)
    full_qkv = gather(jnp.concatenate([w_query, w_key, w_value], axis=1))
    full_out = gather(w_out)
    side = (fsdp_index // PAIR) % 2

    order = (
        ((tensor_index ^ jnp.arange(n_tensor, dtype=jnp.int32)) * seq_dev)[:, None]
        + jnp.arange(seq_dev, dtype=jnp.int32)
    ).reshape(-1)
    prefix_all = jnp.take(prefix_len, order, axis=1)
    own_prefix = prefix_all[:, :seq_dev]
    pos_all = jnp.take(positions, order, axis=1)
    half_dim = HEAD_DIM // 2
    ladder = jnp.arange(half_dim, dtype=F32) * (2.0 / HEAD_DIM)
    inverse = 1.0 / rope_base**ladder

    x_float = inputs.reshape(micro_count * own_rows, model_width).astype(F32)
    grad_own = out_grads.reshape(micro_count * own_rows, model_width)
    unit_attn, scale_attn = normalize(x_float)
    normed = (unit_attn * gain_attn).astype(BF16)
    normed_blocks = spread(normed)
    normed_rows = gather_rows(normed_blocks, micro_count)
    cos_tab, sin_tab, pair_prefix = [], [], []
    for m in micros:
        angles = inverse[:, None] * pos_all[m].astype(F32).reshape(-1)[None, :]
        cos_tab.append(jnp.cos(angles))
        sin_tab.append(jnp.sin(angles))
        pair_prefix.append(split.pair_prefix(prefix_all[m], fsdp_index))
    cos_all = jnp.concatenate(cos_tab, axis=1)
    sin_all = jnp.concatenate(sin_tab, axis=1)
    all_rows = micro_count * row_count
    half_cols = ff_cols // 2
    ffn_near = half_of([w_gate, w_up, w_down], side)
    ffn_far = half_of([w_gate, w_up, w_down], 1 - side)
    grad_pair = pair_join(after(paired(grad_own), full_qkv), micro_count)
    raw = dot(full_qkv, normed_rows, 0, 1).reshape(3, head_cols, all_rows)
    turned = rotate(
        raw[:2].reshape(2, head_count, 2, half_dim, all_rows), cos_all, sin_all, 1.0
    ).reshape(2, head_cols, all_rows)
    stack = jnp.concatenate([turned.astype(BF16), raw[2:].astype(BF16)], axis=0)
    packed = []
    for m in micros:
        packed.append(split.to_heads(stack[:, :, m * row_count : (m + 1) * row_count]))
    grad_pair = after(grad_pair, stack)
    grad_blocks = spread(grad_pair)
    ffn_other = swap(after(ffn_far, packed[-1]), "fsdp", PAIR)
    attn_out, attn_lse = [], []
    branch, resid, unit_mlp, scale_mlp, mlp_rows, normed_mlp = [], [], [], [], [], []
    for m in micros:
        out, lse = attend_forward(pair_prefix[m], packed[m], 0)
        attn_out.append(out)
        attn_lse.append(lse)
    mix_all = split.to_spans(jnp.concatenate(attn_out, axis=1))[0]
    ffn_other = after(ffn_other, attn_lse)
    shard_gu = own_half(side, ffn_near[:, : 2 * half_cols], ffn_other[:, : 2 * half_cols])
    shard_down = own_half(side, ffn_near[:, 2 * half_cols :], ffn_other[:, 2 * half_cols :])
    full_gu = gather_half(after(shard_gu, mix_all))
    full_down = gather_half(shard_down)
    for m in micros:
        mix = mix_all[:, m * row_count : (m + 1) * row_count]
        part = collect(peer_blocks(dot(mix, full_out, 0, 1), 1, n_tensor))
        res = x_float[m * own_rows : (m + 1) * own_rows] + part
        unit, scale = normalize(res)
        branch.append(part)
        resid.append(res)
        unit_mlp.append(unit)
        scale_mlp.append(scale)
        normed = paired((unit * gain_mlp).astype(BF16))
        normed_mlp.append(normed)
        mlp_rows.append(gather_rows(spread(pair_join(normed, 1), False), 1))

    grad_rows = gather_rows(after(grad_blocks, normed_mlp), micro_count)

    ffn_rows = 2 * row_count
    hidden, gate_val, up_val = [], [], []
    for m in micros:
        gate_up = dot(mlp_rows[m], full_gu, 1, 0)
        gate = gate_up[:, :half_cols]
        up = gate_up[:, half_cols:]
        gate_val.append(gate)
        up_val.append(up)
        hidden.append((gate * jax.nn.sigmoid(gate) * up).astype(BF16))
    hidden = jnp.concatenate(hidden, axis=0)
    down_grad = dot(grad_rows, hidden, 0, 0).astype(BF16)
    full_down = after(full_down, down_grad)
    part_down = scatter_half(down_grad)
    grad_gu = []
    for m in micros:
        rows = grad_rows[m * ffn_rows : (m + 1) * ffn_rows]
        grad_hidden = dot(rows, full_down, 1, 0)
        sig = jax.nn.sigmoid(gate_val[m])
        slope = sig * (1.0 + gate_val[m] * (1.0 - sig))
        grad_gu.append(
            jnp.concatenate(
                [
                    (grad_hidden * up_val[m] * slope).astype(BF16),
                    (grad_hidden * gate_val[m] * sig).astype(BF16),
                ],
                axis=1,
            )
        )
    normed_part = [dot(grad_gu[m], full_gu, 1, 1) for m in micros]
    gu_left = jnp.concatenate(after(mlp_rows, normed_part), axis=0)
    gu_right = jnp.concatenate(grad_gu, axis=0)
    gu_grad = dot(gu_left, gu_right, 0, 0).astype(BF16)
    part_gu = scatter_half(after(gu_grad, part_down))
    grad_resid, grad_mix, branch_rows = [], [], []
    mlp_gain_sum = jnp.zeros((model_width,), F32)
    for m in micros:
        total = collect(peer_blocks(normed_part[m], 1, n_tensor), False)
        grad_normed = total[:own_rows] + swap(
            total[own_rows:].astype(BF16), "fsdp", PAIR
        ).astype(F32)
        part, gain_part = norm_back(paired(grad_normed), unit_mlp[m], scale_mlp[m], gain_mlp)
        mlp_gain_sum = mlp_gain_sum + gain_part
        grad_res = grad_own[m * own_rows : (m + 1) * own_rows].astype(F32) + part
        grad_resid.append(grad_res)
        if m == 0:
            grad_res = after(grad_res, gu_grad)
        rows = gather_rows(spread(grad_res.astype(BF16)), 1)
        branch_rows.append(rows)
        grad_mix.append(dot(full_out, rows, 0, 1).astype(BF16))
    grad_out_all = split.to_heads(jnp.concatenate(grad_mix, axis=1)[None])
    out_grad = dot(
        jnp.concatenate(after(branch_rows, grad_mix), axis=0),
        mix_all,
        0,
        1,
    ).astype(BF16)

    mlp_rows_out = dot(after(hidden, out_grad), full_down, 1, 1)
    mlp_blocks = peer_blocks(mlp_rows_out, micro_count, n_tensor)
    own_out = scatter(after(out_grad, part_gu))

    grad_raw = []
    for m in micros:
        grad_out = after(grad_out_all, mlp_rows_out, part_down if m else own_out)
        packed_grad = attend_back(pair_prefix[m], packed[m], attn_out[m], grad_out, attn_lse[m], m)
        grad_raw.append(split.to_spans(packed_grad))

    raw = jnp.concatenate(grad_raw, axis=2)
    turned = rotate(
        raw[:2].reshape(2, head_count, 2, half_dim, all_rows).astype(F32), cos_all, sin_all, -1.0
    ).reshape(2, head_cols, all_rows)
    grad_qkv = jnp.concatenate([turned.astype(BF16), raw[2:]], axis=0).reshape(
        3 * head_cols, all_rows
    )
    qkv_grad = dot(normed_rows, grad_qkv, 0, 1).astype(BF16)
    own_down = settle_half(part_down, side, 1, qkv_grad)
    own_gu = settle_half(part_gu, side, 2, qkv_grad)
    part = dot(after(grad_qkv, qkv_grad), full_qkv, 0, 1)
    grad_normed = collect(peer_blocks(part, micro_count, n_tensor))
    mlp_part = collect(mlp_blocks, token=part)
    near = [mlp_part[2 * m * own_rows : (2 * m + 1) * own_rows] for m in micros]
    far = [mlp_part[(2 * m + 1) * own_rows : (2 * m + 2) * own_rows] for m in micros]
    far = swap(jnp.concatenate(far, axis=0).astype(BF16), "fsdp", PAIR).astype(F32)
    mlp_out = paired(jnp.concatenate(near, axis=0) + far)
    branch = jnp.concatenate(branch, axis=0)
    result = jnp.concatenate(resid, axis=0) + mlp_out
    output = result.astype(BF16).reshape(inputs.shape)
    valid = (query_index[None, None, :] >= own_prefix[:, :, None]).reshape(-1)
    stats = jnp.stack(
        [
            jnp.sum(
                jnp.where(valid, jnp.sum(part * part, axis=1), 0.0).reshape(
                    micro_count, seq_dev, span_len
                ),
                axis=2,
            )
            for part in (result, branch, mlp_out)
        ],
        axis=-1,
    )

    own_qkv = scatter(qkv_grad)
    part, attn_gain_sum = norm_back(grad_normed, unit_attn, scale_attn, gain_attn)
    input_grad = (jnp.concatenate(grad_resid, axis=0) + part).reshape(inputs.shape)

    stat_sum = tree_sum(stats, "fsdp")
    gain_sum = tree_sum(tree_sum(jnp.stack([attn_gain_sum, mlp_gain_sum]), "tensor"), "fsdp")
    row_share = model_width // n_fsdp
    own_gain = lax.dynamic_slice_in_dim(gain_sum, fsdp_index * row_share, row_share, 1)
    counts = ((seq_len - own_prefix) * model_width).astype(F32)
    rms_stats = jnp.sqrt(stat_sum / counts[..., None] + stat_eps)
    return (
        output,
        input_grad,
        own_gain[0],
        own_qkv[:, :head_cols],
        own_qkv[:, head_cols : 2 * head_cols],
        own_qkv[:, 2 * head_cols :],
        own_out,
        own_gain[1],
        own_gu[0],
        own_gu[1],
        own_down[0],
        rms_stats,
    )


def solution(mesh):
    in_specs = (
        P(None, "tensor", "fsdp", None),
        P(None, "tensor", "fsdp", None),
        P(),
        P(None, None, "fsdp"),
        P("fsdp"),
        P("fsdp", "tensor"),
        P("fsdp", "tensor"),
        P("fsdp", "tensor"),
        P("fsdp", "tensor"),
        P("fsdp"),
        P("fsdp", "tensor"),
        P("fsdp", "tensor"),
        P("fsdp", "tensor"),
    )
    out_specs = (
        P(None, "tensor", "fsdp", None),
        P(None, "tensor", "fsdp", None),
        P("fsdp"),
        P("fsdp", "tensor"),
        P("fsdp", "tensor"),
        P("fsdp", "tensor"),
        P("fsdp", "tensor"),
        P("fsdp"),
        P("fsdp", "tensor"),
        P("fsdp", "tensor"),
        P("fsdp", "tensor"),
        P(None, "tensor", None),
    )
    return jax.shard_map(layer, mesh=mesh, in_specs=in_specs, out_specs=out_specs, check_vma=False)
```

```python
import functools
import math

import jax
import jax.numpy as jnp
from jax import lax
from jax.experimental import pallas as pl
from jax.experimental.pallas import tpu as pltpu
from jax.sharding import PartitionSpec as P

HEAD_DIM = 64

rope_base = 130000.0
norm_eps = 1e-05
stat_eps = 1e-06
LOG2E = math.log2(math.e)
MASKED = -1e30
PAIR = 2
BF16 = jnp.bfloat16
F32 = jnp.float32


def dot(left, right, left_dim, right_dim):
    return lax.dot_general(
        left, right, (((left_dim,), (right_dim,)), ((), ())), preferred_element_type=F32
    )


def normalize(values):
    row_scale = lax.rsqrt(jnp.mean(values * values, axis=-1, keepdims=True) + norm_eps)
    return (values * row_scale, row_scale)


def norm_back(grad_in, unit_rows, row_scale, gain):
    scaled = grad_in * gain
    inner_mean = jnp.mean(scaled * unit_rows, axis=-1, keepdims=True)
    return (
        row_scale * (scaled - unit_rows * inner_mean),
        jnp.sum(grad_in * unit_rows, axis=tuple(range(grad_in.ndim - 1))),
    )


def rotate(values, cos_tab, sin_tab, rot_sign):
    first_half = values[..., 0, :, :]
    second = values[..., 1, :, :]
    return jnp.stack(
        [
            first_half * cos_tab - rot_sign * second * sin_tab,
            second * cos_tab + rot_sign * first_half * sin_tab,
        ],
        axis=-3,
    )


def swap(value, axis, distance):
    count = lax.axis_size(axis)
    return lax.ppermute(value, axis, [(a, a ^ distance) for a in range(count)])


def after(value, *others):
    return lax.optimization_barrier((value, others))[0]


def spread(value, direct=True):
    count = lax.axis_size("tensor")
    if direct or count != 4:
        return [value] + [swap(value, "tensor", k) for k in range(1, count)]
    half = value.shape[0] // 2
    one = swap(value, "tensor", 1)
    two = swap(value, "tensor", 2)
    low = swap(two[:half], "tensor", 1)
    high = swap(one[half:], "tensor", 2)
    return [value, one, two, jnp.concatenate([low, high], axis=0)]


def collect(parts, direct=True, token=None):
    count = lax.axis_size("tensor")
    if direct or count != 4:
        blocks = [swap(parts[k].astype(BF16), "tensor", k) for k in range(1, count)]
        if token is not None:
            blocks = after(blocks, token)
        total = parts[0]
        for block in blocks:
            total = total + block.astype(F32)
        return total
    half = parts[0].shape[0] // 2
    far = parts[3].astype(BF16)
    low = swap(far[:half], "tensor", 1).astype(F32)
    high = swap(far[half:], "tensor", 2).astype(F32)
    one = jnp.concatenate([parts[1][:half], parts[1][half:] + high], axis=0)
    two = jnp.concatenate([parts[2][:half] + low, parts[2][half:]], axis=0)
    one = swap(one.astype(BF16), "tensor", 1).astype(F32)
    two = swap(two.astype(BF16), "tensor", 2).astype(F32)
    return parts[0] + one + two


def pair_join(value, micros):
    other = swap(value, "fsdp", PAIR)
    size = value.shape[0] // micros
    parts = [v[m * size : (m + 1) * size] for m in range(micros) for v in (value, other)]
    return jnp.concatenate(parts, axis=0)


def gather_rows(blocks, micros):
    size = blocks[0].shape[0] // micros
    return jnp.concatenate(
        [b[m * size : (m + 1) * size] for m in range(micros) for b in blocks], axis=0
    )


def peer_blocks(rows, micros, peers):
    size = rows.shape[0] // (micros * peers)
    return [
        jnp.concatenate(
            [rows[(m * peers + k) * size : (m * peers + k + 1) * size] for m in range(micros)],
            axis=0,
        )
        for k in range(peers)
    ]


def paired(values):
    count = lax.axis_size("fsdp")
    size = values.shape[-1] // count
    order = [(f & ~3) | ((f & 1) << 1) | ((f >> 1) & 1) for f in range(count)]
    parts = [lax.slice_in_dim(values, f * size, (f + 1) * size, axis=-1) for f in order]
    return jnp.concatenate(parts, axis=-1)


def pair_groups():
    count = lax.axis_size("fsdp")
    return [[f for f in range(count) if bool(f & PAIR) == side] for side in (False, True)]


def half_of(shards, side):
    half = shards[0].shape[1] // 2
    return jnp.concatenate(
        [lax.dynamic_slice_in_dim(s, side * half, half, 1) for s in shards], axis=1
    )


def order_pair(side, mine, other):
    return jnp.where(side == 0, mine, other), jnp.where(side == 0, other, mine)


def own_half(side, mine, other):
    return jnp.concatenate(order_pair(side, mine, other), axis=0)


def gather_half(shard):
    return lax.all_gather(
        shard,
        "fsdp",
        axis=0,
        tiled=True,
        axis_index_groups=pair_groups(),
    )


def scatter_half(grad):
    return lax.psum_scatter(
        grad, "fsdp", scatter_dimension=0, tiled=True, axis_index_groups=pair_groups()
    )


def settle_half(part, side, pieces, token):
    rows = part.shape[0] // 2
    mine = lax.dynamic_slice_in_dim(part, side * rows, rows, 0)
    other = swap(lax.dynamic_slice_in_dim(part, (1 - side) * rows, rows, 0), "fsdp", PAIR)
    low, high = order_pair(side, mine, after(other, token))
    half = part.shape[1] // pieces
    return [
        jnp.concatenate(
            [low[:, i * half : (i + 1) * half], high[:, i * half : (i + 1) * half]], axis=1
        ).astype(F32)
        for i in range(pieces)
    ]


def tree_sum(value, axis):
    step = 1
    while step < lax.axis_size(axis):
        value = value + swap(value, axis, step)
        step *= 2
    return value


def span_block(ref, first, count, lo, hi):
    return jnp.concatenate([ref[first + i, 0, lo:hi, :] for i in range(count)], axis=1)


def attn_blocks(spans, span_len):
    group = max(1, min(spans, 256 // span_len))
    while spans % group:
        group -= 1
    return group, spans // group


def key_count(q_block, block, prefix, blocks):
    return jnp.minimum(jnp.maximum(q_block + 1, (prefix + block - 1) // block), blocks)


def allowed_mask(k_block, q_block, block, prefix):
    key_id = k_block * block + lax.broadcasted_iota(jnp.int32, (block, block), 0)
    query_id = q_block * block + lax.broadcasted_iota(jnp.int32, (block, block), 1)
    return (key_id <= query_id) | (key_id < prefix)


def forward_kernel(prefix_ref, x_ref, out_ref, lse_ref, key_ref):
    spans, _, _, span_len = x_ref.shape
    group, blocks = attn_blocks(spans, span_len)
    block = group * span_len
    prefix = prefix_ref[pl.program_id(0)]
    coef = HEAD_DIM**-0.5 * LOG2E
    for kb in range(blocks):
        key_ref[pl.ds(kb * block, block), :] = span_block(
            x_ref, kb * group, group, HEAD_DIM, 2 * HEAD_DIM
        ).T
    for qb in range(blocks):
        q_t = span_block(x_ref, qb * group, group, 0, HEAD_DIM)

        def step(kb, carry):
            top, total, acc = carry
            keys = key_ref[pl.ds(pl.multiple_of(kb * block, block), block), :]
            scores = dot(keys, q_t, 1, 0) * coef
            scores = jnp.where(allowed_mask(kb, qb, block, prefix), scores, MASKED)
            new_top = jnp.maximum(top, jnp.max(scores, axis=0, keepdims=True))
            probs = jnp.exp2(scores - new_top)
            shrink = jnp.exp2(top - new_top)
            total = shrink * total + jnp.sum(probs, axis=0, keepdims=True)
            v_t = span_block(x_ref, kb * group, group, 2 * HEAD_DIM, 3 * HEAD_DIM)
            acc = shrink * acc + dot(v_t, probs.astype(BF16), 1, 0)
            return new_top, total, acc

        top, total, acc = lax.fori_loop(
            0,
            key_count(qb, block, prefix, blocks),
            step,
            (
                jnp.full((1, block), MASKED, F32),
                jnp.zeros((1, block), F32),
                jnp.zeros((HEAD_DIM, block), F32),
            ),
        )
        out = (acc / total).astype(BF16)
        for i in range(group):
            out_ref[qb * group + i, 0] = out[:, i * span_len : (i + 1) * span_len]
        lse_ref[0, :, qb * block : (qb + 1) * block] = top + jnp.log2(total)


def backward_kernel(
    prefix_ref, x_ref, o_ref, do_ref, lse_ref, dx_ref, key_ref, val_ref, dk_ref, dv_ref
):
    spans, _, _, span_len = x_ref.shape
    group, blocks = attn_blocks(spans, span_len)
    block = group * span_len
    prefix = prefix_ref[pl.program_id(0)]
    scale = HEAD_DIM**-0.5
    coef = scale * LOG2E
    for kb in range(blocks):
        rows = pl.ds(kb * block, block)
        key_ref[rows, :] = span_block(x_ref, kb * group, group, HEAD_DIM, 2 * HEAD_DIM).T
        val_ref[rows, :] = span_block(x_ref, kb * group, group, 2 * HEAD_DIM, 3 * HEAD_DIM).T
    dk_ref[...] = jnp.zeros_like(dk_ref)
    dv_ref[...] = jnp.zeros_like(dv_ref)
    for qb in range(blocks):
        q_t = span_block(x_ref, qb * group, group, 0, HEAD_DIM)
        do_t = span_block(do_ref, qb * group, group, 0, HEAD_DIM)
        o_t = span_block(o_ref, qb * group, group, 0, HEAD_DIM)
        delta = jnp.sum(do_t.astype(F32) * o_t.astype(F32), axis=0, keepdims=True)
        lse = lse_ref[0, :, qb * block : (qb + 1) * block]

        def step(kb, dq):
            rows = pl.ds(pl.multiple_of(kb * block, block), block)
            scores = dot(key_ref[rows, :], q_t, 1, 0) * coef
            scores = jnp.where(allowed_mask(kb, qb, block, prefix), scores, MASKED)
            probs = jnp.exp2(scores - lse)
            grad_probs = dot(val_ref[rows, :], do_t, 1, 0)
            grad_scores = (probs * (grad_probs - delta)).astype(BF16)
            dv_ref[kb] += dot(do_t, probs.astype(BF16), 1, 1)
            dk_ref[kb] += dot(q_t, grad_scores, 1, 1)
            k_t = span_block(x_ref, kb * group, group, HEAD_DIM, 2 * HEAD_DIM)
            return dq + dot(k_t, grad_scores, 1, 0)

        dq = lax.fori_loop(
            0,
            key_count(qb, block, prefix, blocks),
            step,
            jnp.zeros((HEAD_DIM, block), F32),
        )
        dq = (dq * scale).astype(BF16)
        for i in range(group):
            dx_ref[qb * group + i, 0, :HEAD_DIM, :] = dq[:, i * span_len : (i + 1) * span_len]
    for kb in range(blocks):
        dk = (dk_ref[kb] * scale).astype(BF16)
        dv = dv_ref[kb].astype(BF16)
        for i in range(group):
            cols = slice(i * span_len, (i + 1) * span_len)
            dx_ref[kb * group + i, 0, HEAD_DIM : 2 * HEAD_DIM, :] = dk[:, cols]
            dx_ref[kb * group + i, 0, 2 * HEAD_DIM :, :] = dv[:, cols]


def pair_spec(shape, first=0):
    return pl.BlockSpec((shape[0], 1) + shape[2:], lambda p, pre: (0, first + p, 0, 0))


def lse_spec(tokens):
    return pl.BlockSpec((1, 1, tokens), lambda p, pre: (p, 0, 0))


def attend_forward(prefix, packed):
    spans, _, _, span_len = packed.shape
    pairs = prefix.shape[0]
    tokens = spans * span_len
    out_shape = (spans, pairs, HEAD_DIM, span_len)
    return pl.pallas_call(
        forward_kernel,
        out_shape=(
            jax.ShapeDtypeStruct(out_shape, BF16),
            jax.ShapeDtypeStruct((pairs, 1, tokens), F32),
        ),
        grid_spec=pltpu.PrefetchScalarGridSpec(
            num_scalar_prefetch=1,
            grid=(pairs,),
            in_specs=[pair_spec(packed.shape)],
            out_specs=[pair_spec(out_shape), lse_spec(tokens)],
            scratch_shapes=[pltpu.VMEM((tokens, HEAD_DIM), BF16)],
        ),
        compiler_params=pltpu.CompilerParams(dimension_semantics=("arbitrary",)),
        name="attend_forward",
    )(prefix, packed)


def attend_back(prefix, packed, out, grad_out, lse, micro):
    spans, _, width, span_len = packed.shape
    pairs = prefix.shape[0]
    grad_shape = (spans, pairs, width, span_len)
    tokens = spans * span_len
    group, blocks = attn_blocks(spans, span_len)
    acc = pltpu.VMEM((blocks, HEAD_DIM, group * span_len), F32)
    return pl.pallas_call(
        backward_kernel,
        out_shape=jax.ShapeDtypeStruct(grad_shape, BF16),
        grid_spec=pltpu.PrefetchScalarGridSpec(
            num_scalar_prefetch=1,
            grid=(pairs,),
            in_specs=[
                pair_spec(packed.shape),
                pair_spec(out.shape),
                pair_spec(grad_out.shape, micro * pairs),
                lse_spec(tokens),
            ],
            out_specs=pair_spec(grad_shape),
            scratch_shapes=[
                pltpu.VMEM((tokens, HEAD_DIM), BF16),
                pltpu.VMEM((tokens, HEAD_DIM), BF16),
                acc,
                acc,
            ],
        ),
        compiler_params=pltpu.CompilerParams(dimension_semantics=("arbitrary",)),
        name="attend_back",
    )(prefix, packed, out, grad_out, lse)


def tile_of(size):
    return math.gcd(size, 256)


def whole(shape):
    return pl.BlockSpec(shape, lambda n: (0,) * len(shape), pipeline_mode=pl.Buffered(1))


def col_tile(rows, tile):
    return pl.BlockSpec((rows, tile), lambda n: (0, n))


def ffn_forward_kernel(x_ref, wg_ref, wu_ref, g_ref, u_ref, h_ref):
    x = x_ref[...]
    gate = dot(x, wg_ref[...], 1, 0)
    up = dot(x, wu_ref[...], 1, 0)
    g_ref[...] = gate
    u_ref[...] = up
    h_ref[...] = (gate * jax.nn.sigmoid(gate) * up).astype(BF16)


def ffn_forward(rows, w_gate, w_up):
    count, width = rows.shape
    units = w_gate.shape[1]
    tile = tile_of(units)
    return pl.pallas_call(
        ffn_forward_kernel,
        grid=(units // tile,),
        in_specs=[whole(rows.shape), col_tile(width, tile), col_tile(width, tile)],
        out_specs=[col_tile(count, tile)] * 3,
        out_shape=[
            jax.ShapeDtypeStruct((count, units), F32),
            jax.ShapeDtypeStruct((count, units), F32),
            jax.ShapeDtypeStruct((count, units), BF16),
        ],
        name="ffn_forward",
    )(rows, w_gate, w_up)


def ffn_back_kernel(dy_ref, wd_ref, g_ref, u_ref, dg_ref, du_ref):
    grad_hidden = dot(dy_ref[...], wd_ref[...], 1, 0)
    gate = g_ref[...]
    sig = jax.nn.sigmoid(gate)
    slope = sig * (1.0 + gate * (1.0 - sig))
    dg_ref[...] = (grad_hidden * u_ref[...] * slope).astype(BF16)
    du_ref[...] = (grad_hidden * (gate * sig)).astype(BF16)


def ffn_back(grad_rows, micro, w_down, gate, up):
    count, units = gate.shape
    width = w_down.shape[0]
    tile = tile_of(units)
    return pl.pallas_call(
        ffn_back_kernel,
        grid=(units // tile,),
        in_specs=[
            pl.BlockSpec((count, width), lambda n: (micro, 0), pipeline_mode=pl.Buffered(1)),
            col_tile(width, tile),
            col_tile(count, tile),
            col_tile(count, tile),
        ],
        out_specs=[col_tile(count, tile)] * 2,
        out_shape=[jax.ShapeDtypeStruct((count, units), BF16)] * 2,
        name="ffn_back",
    )(grad_rows, w_down, gate, up)


def to_peers_kernel(terms, micros, *refs):
    left = [r[...] for r in refs[:terms]]
    right = [r[...] for r in refs[terms : 2 * terms]]
    outs = refs[2 * terms :]
    total = None
    for a, b in zip(left, right):
        part = dot(a, b, 1, 1)
        total = part if total is None else total + part
    size = outs[0].shape[0] // micros
    for m in range(micros):
        for k, out in enumerate(outs):
            first = (m * len(outs) + k) * size
            out[m * size : (m + 1) * size, :] = total[first : first + size].astype(out.dtype)


def to_peers(lefts, rights, micros, peers):
    count, units = lefts[0].shape
    width = rights[0].shape[0]
    tile = tile_of(width)
    terms = len(lefts)
    rows = count // peers
    return pl.pallas_call(
        functools.partial(to_peers_kernel, terms, micros),
        grid=(width // tile,),
        in_specs=[whole(left.shape) for left in lefts]
        + [pl.BlockSpec((tile, units), lambda n: (n, 0))] * terms,
        out_specs=[col_tile(rows, tile)] * peers,
        out_shape=[
            jax.ShapeDtypeStruct((rows, width), BF16 if k else F32) for k in range(peers)
        ],
        name="to_peers",
    )(*lefts, *rights)


class HeadSplit:
    def __init__(self, n_fsdp, head_count, seqs, span_len):
        self.head_groups = math.gcd(n_fsdp, head_count)
        self.seq_groups = n_fsdp // self.head_groups
        self.heads_per = head_count // self.head_groups
        self.seqs_per = seqs // self.seq_groups
        self.span_len = span_len

    def to_heads(self, stack):
        kinds = stack.shape[0]
        stack = stack.reshape(
            kinds,
            self.head_groups,
            self.heads_per,
            HEAD_DIM,
            -1,
            self.seq_groups,
            self.seqs_per,
            self.span_len,
        )
        stack = stack.transpose(5, 1, 4, 2, 6, 0, 3, 7)
        count = self.seq_groups * self.head_groups
        stack = stack.reshape(count, -1, kinds * HEAD_DIM, self.span_len)
        return lax.all_to_all(stack, "fsdp", split_axis=0, concat_axis=0, tiled=True)

    def to_spans(self, stack):
        kinds = stack.shape[2] // HEAD_DIM
        stack = lax.all_to_all(stack, "fsdp", split_axis=0, concat_axis=0, tiled=True)
        stack = stack.reshape(
            self.seq_groups,
            self.head_groups,
            -1,
            self.heads_per,
            self.seqs_per,
            kinds,
            HEAD_DIM,
            self.span_len,
        )
        stack = stack.transpose(5, 1, 3, 6, 2, 0, 4, 7)
        return stack.reshape(kinds, self.head_groups * self.heads_per * HEAD_DIM, -1)

    def pair_prefix(self, prefix, fsdp_index):
        mine = lax.dynamic_slice_in_dim(
            prefix, (fsdp_index // self.head_groups) * self.seqs_per, self.seqs_per, 0
        )
        return jnp.tile(mine, self.heads_per)


def layer(
    inputs,
    out_grads,
    prefix_len,
    positions,
    attn_gain,
    w_query,
    w_key,
    w_value,
    w_out,
    mlp_gain,
    w_gate,
    w_up,
    w_down,
):
    micro_count, seq_dev, span_len, model_width = inputs.shape
    n_tensor = lax.axis_size("tensor")
    n_fsdp = lax.axis_size("fsdp")
    seq_mb = seq_dev * n_tensor
    seq_len = span_len * n_fsdp
    row_count = seq_mb * span_len
    own_rows = seq_dev * span_len
    head_cols = w_query.shape[1]
    head_count = head_cols // HEAD_DIM
    ff_cols = w_gate.shape[1]
    fsdp_index = lax.axis_index("fsdp")
    tensor_index = lax.axis_index("tensor")
    query_index = fsdp_index * span_len + jnp.arange(span_len, dtype=jnp.int32)
    split = HeadSplit(n_fsdp, head_count, seq_mb, span_len)
    micros = range(micro_count)

    def gather(shard):
        return lax.all_gather(shard, "fsdp", axis=0, tiled=True)

    def scatter(grad):
        return lax.psum_scatter(grad, "fsdp", scatter_dimension=0, tiled=True).astype(F32)

    gains = lax.all_gather(jnp.stack([attn_gain, mlp_gain]), "fsdp", axis=1, tiled=True)
    gain_attn = gains[0].astype(F32)
    gain_mlp = gains[1].astype(F32)
    full_qkv = gather(jnp.concatenate([w_query, w_key, w_value], axis=1))
    full_out = gather(w_out)
    side = (fsdp_index // PAIR) % 2

    order = (
        ((tensor_index ^ jnp.arange(n_tensor, dtype=jnp.int32)) * seq_dev)[:, None]
        + jnp.arange(seq_dev, dtype=jnp.int32)
    ).reshape(-1)
    prefix_all = jnp.take(prefix_len, order, axis=1)
    own_prefix = prefix_all[:, :seq_dev]
    pos_all = jnp.take(positions, order, axis=1)
    half_dim = HEAD_DIM // 2
    ladder = jnp.arange(half_dim, dtype=F32) * (2.0 / HEAD_DIM)
    inverse = 1.0 / rope_base**ladder

    x_float = inputs.reshape(micro_count * own_rows, model_width).astype(F32)
    grad_own = out_grads.reshape(micro_count * own_rows, model_width)
    unit_attn, scale_attn = normalize(x_float)
    normed = (unit_attn * gain_attn).astype(BF16)
    normed_blocks = spread(normed, False)
    normed_rows = gather_rows(normed_blocks, micro_count)
    cos_tab, sin_tab, pair_prefix = [], [], []
    for m in micros:
        angles = inverse[:, None] * pos_all[m].astype(F32).reshape(-1)[None, :]
        cos_tab.append(jnp.cos(angles))
        sin_tab.append(jnp.sin(angles))
        pair_prefix.append(split.pair_prefix(prefix_all[m], fsdp_index))
    cos_all = jnp.concatenate(cos_tab, axis=1)
    sin_all = jnp.concatenate(sin_tab, axis=1)
    all_rows = micro_count * row_count
    half_cols = ff_cols // 2
    ffn_near = half_of([w_gate, w_up, w_down], side)
    ffn_far = half_of([w_gate, w_up, w_down], 1 - side)
    grad_pair = pair_join(after(paired(grad_own), full_qkv), micro_count)
    raw = dot(full_qkv, normed_rows, 0, 1).reshape(3, head_cols, all_rows)
    turned = rotate(
        raw[:2].reshape(2, head_count, 2, half_dim, all_rows), cos_all, sin_all, 1.0
    ).reshape(2, head_cols, all_rows)
    stack = jnp.concatenate([turned.astype(BF16), raw[2:].astype(BF16)], axis=0)
    packed = []
    for m in micros:
        packed.append(split.to_heads(stack[:, :, m * row_count : (m + 1) * row_count]))
    grad_pair = after(grad_pair, stack)
    grad_blocks = spread(grad_pair)
    ffn_other = swap(after(ffn_far, packed[-1]), "fsdp", PAIR)
    attn_out, attn_lse = [None] * micro_count, [None] * micro_count
    done = full_out
    for m in reversed(micros):
        attn_out[m], attn_lse[m] = attend_forward(pair_prefix[m], after(packed[m], done))
        done = attn_lse[m]
    mix_all = split.to_spans(jnp.concatenate(attn_out, axis=1))[0]
    ffn_other = after(ffn_other, attn_lse)
    shards = [
        own_half(
            side,
            ffn_near[:, i * half_cols : (i + 1) * half_cols],
            ffn_other[:, i * half_cols : (i + 1) * half_cols],
        )
        for i in range(3)
    ]
    full_gate = gather_half(after(shards[0], mix_all))
    branch, resid, unit_mlp, scale_mlp, joined = [], [], [], [], []
    parts = []
    for m in micros:
        mix = mix_all[:, m * row_count : (m + 1) * row_count]
        parts.append(dot(after(mix, parts) if parts else mix, full_out, 0, 1))
    for m in micros:
        part = collect(peer_blocks(parts[m], 1, n_tensor))
        res = x_float[m * own_rows : (m + 1) * own_rows] + part
        unit, scale = normalize(res)
        branch.append(part)
        resid.append(res)
        unit_mlp.append(unit)
        scale_mlp.append(scale)
        normed = paired((unit * gain_mlp).astype(BF16))
        joined.append(pair_join(normed, 1))
    full_up = gather_half(after(shards[1], joined))
    full_down = gather_half(shards[2])
    mlp_rows, first = [], None
    for m in micros:
        blocks = spread(joined[m] if first is None else after(joined[m], first), False)
        if first is None:
            first = blocks[1:3]
            grad_rows = gather_rows(after(grad_blocks, first), micro_count)
        mlp_rows.append(gather_rows(blocks, 1))

    hidden, gate_val, up_val = [], [], []
    for m in micros:
        gate, up, hid = ffn_forward(mlp_rows[m], full_gate, full_up)
        gate_val.append(gate)
        up_val.append(up)
        hidden.append(hid)
    hidden = jnp.concatenate(hidden, axis=0)
    down_grad = dot(grad_rows, hidden, 0, 0).astype(BF16)
    full_down = after(full_down, down_grad)
    part_down = scatter_half(down_grad)
    grad_gu, normed_part = [], []
    for m in micros:
        gate, up = ffn_back(grad_rows, m, full_down, gate_val[m], up_val[m])
        grad_gu.append(jnp.concatenate([gate, up], axis=1))
        normed_part.append(to_peers([gate, up], [full_gate, full_up], 1, n_tensor))
    all_mlp_rows = jnp.concatenate(after(mlp_rows, normed_part), axis=0)
    gu_grad = dot(all_mlp_rows, jnp.concatenate(grad_gu, axis=0), 0, 0).astype(BF16)
    part_gu = scatter_half(after(gu_grad, part_down))
    grad_resid, grad_mix, branch_rows = [], [], []
    mlp_gain_sum = jnp.zeros((model_width,), F32)
    for m in micros:
        total = collect(normed_part[m])
        grad_normed = total[:own_rows] + swap(
            total[own_rows:].astype(BF16), "fsdp", PAIR
        ).astype(F32)
        part, gain_part = norm_back(paired(grad_normed), unit_mlp[m], scale_mlp[m], gain_mlp)
        mlp_gain_sum = mlp_gain_sum + gain_part
        grad_res = grad_own[m * own_rows : (m + 1) * own_rows].astype(F32) + part
        grad_resid.append(grad_res)
        if m == 0:
            grad_res = after(grad_res, gu_grad)
        rows = gather_rows(spread(grad_res.astype(BF16)), 1)
        branch_rows.append(rows)
        grad_mix.append(dot(full_out, rows, 0, 1).astype(BF16))
    grad_out_all = split.to_heads(jnp.concatenate(grad_mix, axis=1)[None])
    out_grad = dot(
        jnp.concatenate(after(branch_rows, grad_mix), axis=0),
        mix_all,
        0,
        1,
    ).astype(BF16)

    mlp_blocks = to_peers([after(hidden, out_grad)], [full_down], micro_count, n_tensor)
    own_out = scatter(after(out_grad, part_gu))

    grad_raw = []
    for m in micros:
        grad_out = after(grad_out_all, mlp_blocks, part_down if m else own_out)
        packed_grad = attend_back(pair_prefix[m], packed[m], attn_out[m], grad_out, attn_lse[m], m)
        grad_raw.append(split.to_spans(packed_grad))

    raw = jnp.concatenate(grad_raw, axis=2)
    turned = rotate(
        raw[:2].reshape(2, head_count, 2, half_dim, all_rows).astype(F32), cos_all, sin_all, -1.0
    ).reshape(2, head_cols, all_rows)
    grad_qkv = jnp.concatenate([turned.astype(BF16), raw[2:]], axis=0).reshape(
        3 * head_cols, all_rows
    )
    qkv_grad = dot(normed_rows, grad_qkv, 0, 1).astype(BF16)
    own_gate, own_up = settle_half(part_gu, side, 2, qkv_grad)
    (own_down,) = settle_half(part_down, side, 1, qkv_grad)
    part = dot(after(grad_qkv, qkv_grad), full_qkv, 0, 1)
    grad_normed = collect(peer_blocks(part, micro_count, n_tensor))
    mlp_part = collect(mlp_blocks, token=part)
    near = [mlp_part[2 * m * own_rows : (2 * m + 1) * own_rows] for m in micros]
    far = [mlp_part[(2 * m + 1) * own_rows : (2 * m + 2) * own_rows] for m in micros]
    far = swap(jnp.concatenate(far, axis=0).astype(BF16), "fsdp", PAIR).astype(F32)
    mlp_out = paired(jnp.concatenate(near, axis=0) + far)
    branch = jnp.concatenate(branch, axis=0)
    result = jnp.concatenate(resid, axis=0) + mlp_out
    output = result.astype(BF16).reshape(inputs.shape)
    valid = (query_index[None, None, :] >= own_prefix[:, :, None]).reshape(-1)
    stats = jnp.stack(
        [
            jnp.sum(
                jnp.where(valid, jnp.sum(part * part, axis=1), 0.0).reshape(
                    micro_count, seq_dev, span_len
                ),
                axis=2,
            )
            for part in (result, branch, mlp_out)
        ],
        axis=-1,
    )

    own_qkv = scatter(qkv_grad)
    part, attn_gain_sum = norm_back(grad_normed, unit_attn, scale_attn, gain_attn)
    input_grad = (jnp.concatenate(grad_resid, axis=0) + part).reshape(inputs.shape)

    stat_sum = tree_sum(stats, "fsdp")
    gain_sum = tree_sum(tree_sum(jnp.stack([attn_gain_sum, mlp_gain_sum]), "tensor"), "fsdp")
    row_share = model_width // n_fsdp
    own_gain = lax.dynamic_slice_in_dim(gain_sum, fsdp_index * row_share, row_share, 1)
    counts = ((seq_len - own_prefix) * model_width).astype(F32)
    rms_stats = jnp.sqrt(stat_sum / counts[..., None] + stat_eps)
    return (
        output,
        input_grad,
        own_gain[0],
        own_qkv[:, :head_cols],
        own_qkv[:, head_cols : 2 * head_cols],
        own_qkv[:, 2 * head_cols :],
        own_out,
        own_gain[1],
        own_gate,
        own_up,
        own_down,
        rms_stats,
    )


def solution(mesh):
    in_specs = (
        P(None, "tensor", "fsdp", None),
        P(None, "tensor", "fsdp", None),
        P(),
        P(None, None, "fsdp"),
        P("fsdp"),
        P("fsdp", "tensor"),
        P("fsdp", "tensor"),
        P("fsdp", "tensor"),
        P("fsdp", "tensor"),
        P("fsdp"),
        P("fsdp", "tensor"),
        P("fsdp", "tensor"),
        P("fsdp", "tensor"),
    )
    out_specs = (
        P(None, "tensor", "fsdp", None),
        P(None, "tensor", "fsdp", None),
        P("fsdp"),
        P("fsdp", "tensor"),
        P("fsdp", "tensor"),
        P("fsdp", "tensor"),
        P("fsdp", "tensor"),
        P("fsdp"),
        P("fsdp", "tensor"),
        P("fsdp", "tensor"),
        P("fsdp", "tensor"),
        P(None, "tensor", None),
    )
    return jax.shard_map(layer, mesh=mesh, in_specs=in_specs, out_specs=out_specs, check_vma=False)
```

```python
import functools
import math

import jax
import jax.numpy as jnp
from jax import lax
from jax.experimental import pallas as pl
from jax.experimental.pallas import tpu as pltpu
from jax.sharding import PartitionSpec as P

HEAD_DIM = 64

rope_base = 130000.0
norm_eps = 1e-05
stat_eps = 1e-06
LOG2E = math.log2(math.e)
MASKED = -1e30
PAIR = 2
BF16 = jnp.bfloat16
F32 = jnp.float32


def dot(left, right, left_dim, right_dim):
    return lax.dot_general(
        left, right, (((left_dim,), (right_dim,)), ((), ())), preferred_element_type=F32
    )


def normalize(values):
    row_scale = lax.rsqrt(jnp.mean(values * values, axis=-1, keepdims=True) + norm_eps)
    return (values * row_scale, row_scale)


def norm_back(grad_in, unit_rows, row_scale, gain):
    scaled = grad_in * gain
    inner_mean = jnp.mean(scaled * unit_rows, axis=-1, keepdims=True)
    return (
        row_scale * (scaled - unit_rows * inner_mean),
        jnp.sum(grad_in * unit_rows, axis=tuple(range(grad_in.ndim - 1))),
    )


def swap(value, axis, distance):
    count = lax.axis_size(axis)
    return lax.ppermute(value, axis, [(a, a ^ distance) for a in range(count)])


def after(value, *others):
    return lax.optimization_barrier((value, others))[0]


def spread_pieces(value, direct=True):
    count = lax.axis_size("tensor")
    if direct or count != 4:
        return [value] + [swap(value, "tensor", k) for k in range(1, count)]
    half = value.shape[0] // 2
    one = swap(value, "tensor", 1)
    two = swap(value, "tensor", 2)
    low = swap(two[:half], "tensor", 1)
    high = swap(one[half:], "tensor", 2)
    return [value, one, two, low, high]


def whole_blocks(pieces):
    rows = pieces[0].shape[0]
    far = [p for p in pieces if p.shape[0] < rows]
    return [p for p in pieces if p.shape[0] == rows] + (
        [jnp.concatenate(far, axis=0)] if far else []
    )


def spread(value, direct=True):
    return whole_blocks(spread_pieces(value, direct))


def collect(parts, direct=True, token=None):
    count = lax.axis_size("tensor")
    if direct or count != 4:
        blocks = [swap(parts[k].astype(BF16), "tensor", k) for k in range(1, count)]
        if token is not None:
            blocks = after(blocks, token)
        total = parts[0]
        for block in blocks:
            total = total + block.astype(F32)
        return total
    half = parts[0].shape[0] // 2
    far = parts[3].astype(BF16)
    low = swap(far[:half], "tensor", 1).astype(F32)
    high = swap(far[half:], "tensor", 2).astype(F32)
    one = jnp.concatenate([parts[1][:half], parts[1][half:] + high], axis=0)
    two = jnp.concatenate([parts[2][:half] + low, parts[2][half:]], axis=0)
    one = swap(one.astype(BF16), "tensor", 1).astype(F32)
    two = swap(two.astype(BF16), "tensor", 2).astype(F32)
    return parts[0] + one + two


def pair_join(value, micros):
    other = swap(value, "fsdp", PAIR)
    size = value.shape[0] // micros
    parts = [v[m * size : (m + 1) * size] for m in range(micros) for v in (value, other)]
    return jnp.concatenate(parts, axis=0)


def gather_rows(blocks, micros):
    size = blocks[0].shape[0] // micros
    return jnp.concatenate(
        [b[m * size : (m + 1) * size] for m in range(micros) for b in blocks], axis=0
    )


def paired(values):
    count = lax.axis_size("fsdp")
    size = values.shape[-1] // count
    order = [(f & ~3) | ((f & 1) << 1) | ((f >> 1) & 1) for f in range(count)]
    parts = [lax.slice_in_dim(values, f * size, (f + 1) * size, axis=-1) for f in order]
    return jnp.concatenate(parts, axis=-1)


def pair_groups():
    count = lax.axis_size("fsdp")
    return [[f for f in range(count) if bool(f & PAIR) == side] for side in (False, True)]


def half_of(shards, side):
    half = shards[0].shape[1] // 2
    return jnp.concatenate(
        [lax.dynamic_slice_in_dim(s, side * half, half, 1) for s in shards], axis=1
    )


def order_pair(side, mine, other):
    return jnp.where(side == 0, mine, other), jnp.where(side == 0, other, mine)


def own_half(side, mine, other):
    return jnp.concatenate(order_pair(side, mine, other), axis=0)


def gather_half(shard):
    return lax.all_gather(
        shard,
        "fsdp",
        axis=0,
        tiled=True,
        axis_index_groups=pair_groups(),
    )


def scatter_half(grad):
    return lax.psum_scatter(
        grad, "fsdp", scatter_dimension=0, tiled=True, axis_index_groups=pair_groups()
    )


def settle_half(part, side, pieces, token):
    rows = part.shape[0] // 2
    mine = lax.dynamic_slice_in_dim(part, side * rows, rows, 0)
    other = swap(lax.dynamic_slice_in_dim(part, (1 - side) * rows, rows, 0), "fsdp", PAIR)
    low, high = order_pair(side, mine, after(other, token))
    half = part.shape[1] // pieces
    return [
        jnp.concatenate(
            [low[:, i * half : (i + 1) * half], high[:, i * half : (i + 1) * half]], axis=1
        ).astype(F32)
        for i in range(pieces)
    ]


def tree_sum(value, axis):
    step = 1
    while step < lax.axis_size(axis):
        value = value + swap(value, axis, step)
        step *= 2
    return value


def span_block(ref, first, count, lo, hi):
    return jnp.concatenate([ref[first + i, 0, lo:hi, :] for i in range(count)], axis=1)


def attn_blocks(spans, span_len):
    group = max(1, min(spans, 256 // span_len))
    while spans % group:
        group -= 1
    return group, spans // group


def key_count(q_block, block, prefix, blocks):
    return jnp.minimum(jnp.maximum(q_block + 1, (prefix + block - 1) // block), blocks)


def allowed_mask(k_block, q_block, block, prefix):
    key_id = k_block * block + lax.broadcasted_iota(jnp.int32, (block, block), 0)
    query_id = q_block * block + lax.broadcasted_iota(jnp.int32, (block, block), 1)
    return (key_id <= query_id) | (key_id < prefix)


def forward_kernel(prefix_ref, x_ref, out_ref, lse_ref, key_ref):
    spans, _, _, span_len = x_ref.shape
    group, blocks = attn_blocks(spans, span_len)
    block = group * span_len
    prefix = prefix_ref[pl.program_id(0)]
    coef = HEAD_DIM**-0.5 * LOG2E
    for kb in range(blocks):
        key_ref[pl.ds(kb * block, block), :] = span_block(
            x_ref, kb * group, group, HEAD_DIM, 2 * HEAD_DIM
        ).T
    for qb in range(blocks):
        q_t = span_block(x_ref, qb * group, group, 0, HEAD_DIM)

        def step(kb, carry):
            top, total, acc = carry
            keys = key_ref[pl.ds(pl.multiple_of(kb * block, block), block), :]
            scores = dot(keys, q_t, 1, 0) * coef
            scores = jnp.where(allowed_mask(kb, qb, block, prefix), scores, MASKED)
            new_top = jnp.maximum(top, jnp.max(scores, axis=0, keepdims=True))
            probs = jnp.exp2(scores - new_top)
            shrink = jnp.exp2(top - new_top)
            total = shrink * total + jnp.sum(probs, axis=0, keepdims=True)
            v_t = span_block(x_ref, kb * group, group, 2 * HEAD_DIM, 3 * HEAD_DIM)
            acc = shrink * acc + dot(v_t, probs.astype(BF16), 1, 0)
            return new_top, total, acc

        top, total, acc = lax.fori_loop(
            0,
            key_count(qb, block, prefix, blocks),
            step,
            (
                jnp.full((1, block), MASKED, F32),
                jnp.zeros((1, block), F32),
                jnp.zeros((HEAD_DIM, block), F32),
            ),
        )
        out = (acc / total).astype(BF16)
        for i in range(group):
            out_ref[qb * group + i, 0] = out[:, i * span_len : (i + 1) * span_len]
        lse_ref[0, :, qb * block : (qb + 1) * block] = top + jnp.log2(total)


def backward_kernel(
    prefix_ref, x_ref, o_ref, do_ref, lse_ref, dx_ref, key_ref, val_ref, dk_ref, dv_ref
):
    spans, _, _, span_len = x_ref.shape
    group, blocks = attn_blocks(spans, span_len)
    block = group * span_len
    prefix = prefix_ref[pl.program_id(0)]
    scale = HEAD_DIM**-0.5
    coef = scale * LOG2E
    for kb in range(blocks):
        rows = pl.ds(kb * block, block)
        key_ref[rows, :] = span_block(x_ref, kb * group, group, HEAD_DIM, 2 * HEAD_DIM).T
        val_ref[rows, :] = span_block(x_ref, kb * group, group, 2 * HEAD_DIM, 3 * HEAD_DIM).T
    dk_ref[...] = jnp.zeros_like(dk_ref)
    dv_ref[...] = jnp.zeros_like(dv_ref)
    for qb in range(blocks):
        q_t = span_block(x_ref, qb * group, group, 0, HEAD_DIM)
        do_t = span_block(do_ref, qb * group, group, 0, HEAD_DIM)
        o_t = span_block(o_ref, qb * group, group, 0, HEAD_DIM)
        delta = jnp.sum(do_t.astype(F32) * o_t.astype(F32), axis=0, keepdims=True)
        lse = lse_ref[0, :, qb * block : (qb + 1) * block]

        def step(kb, dq):
            rows = pl.ds(pl.multiple_of(kb * block, block), block)
            scores = dot(key_ref[rows, :], q_t, 1, 0) * coef
            scores = jnp.where(allowed_mask(kb, qb, block, prefix), scores, MASKED)
            probs = jnp.exp2(scores - lse)
            grad_probs = dot(val_ref[rows, :], do_t, 1, 0)
            grad_scores = (probs * (grad_probs - delta)).astype(BF16)
            dv_ref[kb] += dot(do_t, probs.astype(BF16), 1, 1)
            dk_ref[kb] += dot(q_t, grad_scores, 1, 1)
            k_t = span_block(x_ref, kb * group, group, HEAD_DIM, 2 * HEAD_DIM)
            return dq + dot(k_t, grad_scores, 1, 0)

        dq = lax.fori_loop(
            0,
            key_count(qb, block, prefix, blocks),
            step,
            jnp.zeros((HEAD_DIM, block), F32),
        )
        dq = (dq * scale).astype(BF16)
        for i in range(group):
            dx_ref[qb * group + i, 0, :HEAD_DIM, :] = dq[:, i * span_len : (i + 1) * span_len]
    for kb in range(blocks):
        dk = (dk_ref[kb] * scale).astype(BF16)
        dv = dv_ref[kb].astype(BF16)
        for i in range(group):
            cols = slice(i * span_len, (i + 1) * span_len)
            dx_ref[kb * group + i, 0, HEAD_DIM : 2 * HEAD_DIM, :] = dk[:, cols]
            dx_ref[kb * group + i, 0, 2 * HEAD_DIM :, :] = dv[:, cols]


def pair_spec(shape, first=0):
    return pl.BlockSpec((shape[0], 1) + shape[2:], lambda p, pre: (0, first + p, 0, 0))


def lse_spec(tokens):
    return pl.BlockSpec((1, 1, tokens), lambda p, pre: (p, 0, 0))


def attend_forward(prefix, packed):
    spans, _, _, span_len = packed.shape
    pairs = prefix.shape[0]
    tokens = spans * span_len
    out_shape = (spans, pairs, HEAD_DIM, span_len)
    return pl.pallas_call(
        forward_kernel,
        out_shape=(
            jax.ShapeDtypeStruct(out_shape, BF16),
            jax.ShapeDtypeStruct((pairs, 1, tokens), F32),
        ),
        grid_spec=pltpu.PrefetchScalarGridSpec(
            num_scalar_prefetch=1,
            grid=(pairs,),
            in_specs=[pair_spec(packed.shape)],
            out_specs=[pair_spec(out_shape), lse_spec(tokens)],
            scratch_shapes=[pltpu.VMEM((tokens, HEAD_DIM), BF16)],
        ),
        compiler_params=pltpu.CompilerParams(dimension_semantics=("arbitrary",)),
        name="attend_forward",
    )(prefix, packed)


def attend_back(prefix, packed, out, grad_out, lse, micro):
    spans, _, width, span_len = packed.shape
    pairs = prefix.shape[0]
    grad_shape = (spans, pairs, width, span_len)
    tokens = spans * span_len
    group, blocks = attn_blocks(spans, span_len)
    acc = pltpu.VMEM((blocks, HEAD_DIM, group * span_len), F32)
    return pl.pallas_call(
        backward_kernel,
        out_shape=jax.ShapeDtypeStruct(grad_shape, BF16),
        grid_spec=pltpu.PrefetchScalarGridSpec(
            num_scalar_prefetch=1,
            grid=(pairs,),
            in_specs=[
                pair_spec(packed.shape),
                pair_spec(out.shape),
                pair_spec(grad_out.shape, micro * pairs),
                lse_spec(tokens),
            ],
            out_specs=pair_spec(grad_shape),
            scratch_shapes=[
                pltpu.VMEM((tokens, HEAD_DIM), BF16),
                pltpu.VMEM((tokens, HEAD_DIM), BF16),
                acc,
                acc,
            ],
        ),
        compiler_params=pltpu.CompilerParams(dimension_semantics=("arbitrary",)),
        name="attend_back",
    )(prefix, packed, out, grad_out, lse)


def tile_of(size):
    return math.gcd(size, 256)


def whole(shape):
    return pl.BlockSpec(shape, lambda n: (0,) * len(shape), pipeline_mode=pl.Buffered(1))


def col_tile(rows, tile):
    return pl.BlockSpec((rows, tile), lambda n: (0, n))


def ffn_forward_kernel(x_ref, wg_ref, wu_ref, g_ref, u_ref, h_ref):
    x = x_ref[...]
    gate = dot(x, wg_ref[...], 1, 0)
    up = dot(x, wu_ref[...], 1, 0)
    g_ref[...] = gate
    u_ref[...] = up
    h_ref[...] = (gate * jax.nn.sigmoid(gate) * up).astype(BF16)


def ffn_forward(rows, w_gate, w_up):
    count, width = rows.shape
    units = w_gate.shape[1]
    tile = tile_of(units)
    return pl.pallas_call(
        ffn_forward_kernel,
        grid=(units // tile,),
        in_specs=[whole(rows.shape), col_tile(width, tile), col_tile(width, tile)],
        out_specs=[col_tile(count, tile)] * 3,
        out_shape=[
            jax.ShapeDtypeStruct((count, units), F32),
            jax.ShapeDtypeStruct((count, units), F32),
            jax.ShapeDtypeStruct((count, units), BF16),
        ],
        name="ffn_forward",
    )(rows, w_gate, w_up)


def ffn_back_kernel(dy_ref, wd_ref, g_ref, u_ref, dg_ref, du_ref):
    grad_hidden = dot(dy_ref[...], wd_ref[...], 1, 0)
    gate = g_ref[...]
    sig = jax.nn.sigmoid(gate)
    slope = sig * (1.0 + gate * (1.0 - sig))
    dg_ref[...] = (grad_hidden * u_ref[...] * slope).astype(BF16)
    du_ref[...] = (grad_hidden * (gate * sig)).astype(BF16)


def ffn_back(grad_rows, micro, w_down, gate, up):
    count, units = gate.shape
    width = w_down.shape[0]
    tile = tile_of(units)
    return pl.pallas_call(
        ffn_back_kernel,
        grid=(units // tile,),
        in_specs=[
            pl.BlockSpec((count, width), lambda n: (micro, 0), pipeline_mode=pl.Buffered(1)),
            col_tile(width, tile),
            col_tile(count, tile),
            col_tile(count, tile),
        ],
        out_specs=[col_tile(count, tile)] * 2,
        out_shape=[jax.ShapeDtypeStruct((count, units), BF16)] * 2,
        name="ffn_back",
    )(grad_rows, w_down, gate, up)


def to_peers_kernel(terms, micros, *refs):
    left = [r[...] for r in refs[:terms]]
    right = [r[...] for r in refs[terms : 2 * terms]]
    outs = refs[2 * terms :]
    total = None
    for a, b in zip(left, right):
        part = dot(a, b, 1, 1)
        total = part if total is None else total + part
    size = outs[0].shape[0] // micros
    for m in range(micros):
        for k, out in enumerate(outs):
            first = (m * len(outs) + k) * size
            out[m * size : (m + 1) * size, :] = total[first : first + size].astype(out.dtype)


def to_peers(lefts, rights, micros, peers):
    count, units = lefts[0].shape
    width = rights[0].shape[0]
    tile = tile_of(width)
    terms = len(lefts)
    rows = count // peers
    return pl.pallas_call(
        functools.partial(to_peers_kernel, terms, micros),
        grid=(width // tile,),
        in_specs=[whole(left.shape) for left in lefts]
        + [pl.BlockSpec((tile, units), lambda n: (n, 0))] * terms,
        out_specs=[col_tile(rows, tile)] * peers,
        out_shape=[
            jax.ShapeDtypeStruct((rows, width), BF16 if k else F32) for k in range(peers)
        ],
        name="to_peers",
    )(*lefts, *rights)


def turn(values, cos_tab, sin_tab):
    half = HEAD_DIM // 2
    first, second = values[:half], values[half:]
    return jnp.concatenate(
        [first * cos_tab - second * sin_tab, second * cos_tab + first * sin_tab], axis=0
    )


def project_kernel(labels, *refs):
    count = len(labels)
    wq_ref, wk_ref, wv_ref, cos_ref, sin_ref = refs[count : count + 5]
    outs = refs[count + 5 :]
    span = outs[0].shape[3]
    weights = jnp.concatenate([wq_ref[...], wk_ref[...], wv_ref[...]], axis=1)
    for ref, places in zip(refs, labels):
        cols_all = dot(ref[...], weights, 1, 0).T
        for i, (m, k) in enumerate(places):
            cols = cols_all[:, i * span : (i + 1) * span]
            cos_tab = cos_ref[m, :, k * span : (k + 1) * span]
            sin_tab = sin_ref[m, :, k * span : (k + 1) * span]
            for h in range(2):
                for kind in range(3):
                    first = (2 * kind + h) * HEAD_DIM
                    value = cols[first : first + HEAD_DIM]
                    if kind < 2:
                        value = turn(value, cos_tab, sin_tab)
                    outs[m][h, k, kind * HEAD_DIM : (kind + 1) * HEAD_DIM, :] = value.astype(BF16)


def project(pieces, labels, weights, cos_tab, sin_tab, span):
    micros, _, tokens = cos_tab.shape
    width = weights.shape[0]
    cols = weights.shape[1] // 3
    blocks = cols // (2 * HEAD_DIM)
    seqs = tokens // span
    out = (cols // HEAD_DIM, seqs, 3 * HEAD_DIM, span)
    return pl.pallas_call(
        functools.partial(project_kernel, labels),
        grid=(blocks,),
        in_specs=[whole(p.shape) for p in pieces]
        + [
            pl.BlockSpec((width, 2 * HEAD_DIM), lambda n, kind=kind: (0, kind * blocks + n))
            for kind in range(3)
        ]
        + [whole(cos_tab.shape)] * 2,
        out_specs=[pl.BlockSpec((2,) + out[1:], lambda n: (n, 0, 0, 0))] * micros,
        out_shape=[jax.ShapeDtypeStruct(out, BF16)] * micros,
        name="project",
    )(*pieces, weights, weights, weights, cos_tab, sin_tab)


def mix_out_kernel(micros, x_ref, w_ref, mix_ref, *outs):
    heads, seqs, _, span = x_ref.shape
    peers = len(outs) // micros
    own = seqs // (micros * peers)

    @pl.when(pl.program_id(0) == 0)
    def _():
        for q in range(seqs):
            mix = x_ref[:, q].reshape(heads * HEAD_DIM, span)
            mix_ref[q * span : (q + 1) * span, :] = mix.T

    total = dot(mix_ref[...], w_ref[...], 1, 1)
    size = own * span
    for i, out in enumerate(outs):
        out[...] = total[i * size : (i + 1) * size].astype(out.dtype)


def mix_out(packed, weights, micros, peers):
    _, seqs, _, span = packed.shape
    width, cols = weights.shape
    tile = tile_of(width)
    rows = seqs * span // (micros * peers)
    kinds = [BF16 if k else F32 for _ in range(micros) for k in range(peers)]
    return pl.pallas_call(
        functools.partial(mix_out_kernel, micros),
        grid=(width // tile,),
        in_specs=[whole(packed.shape), pl.BlockSpec((tile, cols), lambda n: (n, 0))],
        out_specs=[pl.BlockSpec((seqs * span, cols), lambda n: (0, 0))]
        + [col_tile(rows, tile)] * len(kinds),
        out_shape=[jax.ShapeDtypeStruct((seqs * span, cols), BF16)]
        + [jax.ShapeDtypeStruct((rows, width), kind) for kind in kinds],
        name="mix_out",
    )(packed, weights)


def mix_back_kernel(*refs):
    pieces, (w_ref, out_ref) = refs[:-2], refs[-2:]
    heads, _, _, span = out_ref.shape
    q = 0
    for ref in pieces:
        cols = dot(ref[...], w_ref[...], 1, 0).T.astype(BF16)
        for i in range(ref.shape[0] // span):
            for h in range(heads):
                out_ref[h, q] = cols[
                    h * HEAD_DIM : (h + 1) * HEAD_DIM, i * span : (i + 1) * span
                ]
            q += 1


def mix_back(pieces, weights, span):
    width, cols = weights.shape
    tile = tile_of(cols)
    seqs = sum(p.shape[0] for p in pieces) // span
    heads = cols // HEAD_DIM
    return pl.pallas_call(
        mix_back_kernel,
        grid=(cols // tile,),
        in_specs=[whole(p.shape) for p in pieces] + [col_tile(width, tile)],
        out_specs=pl.BlockSpec((tile // HEAD_DIM, seqs, HEAD_DIM, span), lambda n: (n, 0, 0, 0)),
        out_shape=jax.ShapeDtypeStruct((heads, seqs, HEAD_DIM, span), BF16),
        name="mix_back",
    )(*pieces, weights)


def unturn_kernel(blocks, *refs):
    packed, (cos_ref, sin_ref, out_ref) = refs[:-3], refs[-3:]
    _, seqs, _, span = packed[0].shape
    plain = pl.program_id(0) >= 2 * blocks
    for m, ref in enumerate(packed):
        for k in range(seqs):
            cos_tab = jnp.where(plain, 1.0, cos_ref[m, :, k * span : (k + 1) * span])
            sin_tab = jnp.where(plain, 0.0, -sin_ref[m, :, k * span : (k + 1) * span])
            pair = jnp.concatenate(
                [turn(ref[h, k].astype(F32), cos_tab, sin_tab) for h in range(2)], axis=0
            )
            first = (m * seqs + k) * span
            out_ref[first : first + span, :] = pair.T.astype(BF16)


def unturn(packed, cos_tab, sin_tab):
    heads, seqs, _, span = packed[0].shape
    blocks = heads // 2
    rows = len(packed) * seqs * span
    return pl.pallas_call(
        functools.partial(unturn_kernel, blocks),
        grid=(3 * blocks,),
        in_specs=[
            pl.BlockSpec(
                (2, seqs, HEAD_DIM, span), lambda n: (n % blocks, 0, n // blocks, 0)
            )
        ]
        * len(packed)
        + [whole(cos_tab.shape)] * 2,
        out_specs=col_tile(rows, 2 * HEAD_DIM),
        out_shape=jax.ShapeDtypeStruct((rows, 3 * heads * HEAD_DIM), BF16),
        name="unturn",
    )(*packed, cos_tab, sin_tab)


class HeadSplit:
    def __init__(self, n_fsdp, head_count, seqs):
        self.head_groups = math.gcd(n_fsdp, head_count)
        self.seq_groups = n_fsdp // self.head_groups
        self.heads_per = head_count // self.head_groups
        self.seqs_per = seqs // self.seq_groups

    def to_heads(self, packed):
        width, span = packed.shape[2:]
        packed = packed.reshape(
            self.head_groups, self.heads_per, -1, self.seq_groups, self.seqs_per, width, span
        ).transpose(3, 0, 2, 1, 4, 5, 6)
        packed = packed.reshape(self.seq_groups * self.head_groups, -1, width, span)
        return lax.all_to_all(packed, "fsdp", split_axis=0, concat_axis=0, tiled=True)

    def to_spans(self, packed):
        width, span = packed.shape[2:]
        packed = lax.all_to_all(packed, "fsdp", split_axis=0, concat_axis=0, tiled=True)
        packed = packed.reshape(
            self.seq_groups, self.head_groups, -1, self.heads_per, self.seqs_per, width, span
        ).transpose(1, 3, 2, 0, 4, 5, 6)
        return packed.reshape(self.head_groups * self.heads_per, -1, width, span)

    def pair_prefix(self, prefix, fsdp_index):
        mine = lax.dynamic_slice_in_dim(
            prefix, (fsdp_index // self.head_groups) * self.seqs_per, self.seqs_per, 0
        )
        return jnp.tile(mine, self.heads_per)


def layer(
    inputs,
    out_grads,
    prefix_len,
    positions,
    attn_gain,
    w_query,
    w_key,
    w_value,
    w_out,
    mlp_gain,
    w_gate,
    w_up,
    w_down,
):
    micro_count, seq_dev, span_len, model_width = inputs.shape
    n_tensor = lax.axis_size("tensor")
    n_fsdp = lax.axis_size("fsdp")
    seq_mb = seq_dev * n_tensor
    seq_len = span_len * n_fsdp
    own_rows = seq_dev * span_len
    head_cols = w_query.shape[1]
    head_count = head_cols // HEAD_DIM
    ff_cols = w_gate.shape[1]
    fsdp_index = lax.axis_index("fsdp")
    tensor_index = lax.axis_index("tensor")
    query_index = fsdp_index * span_len + jnp.arange(span_len, dtype=jnp.int32)
    split = HeadSplit(n_fsdp, head_count, seq_mb)
    micros = range(micro_count)

    def gather(shard):
        return lax.all_gather(shard, "fsdp", axis=0, tiled=True)

    def scatter(grad):
        return lax.psum_scatter(grad, "fsdp", scatter_dimension=0, tiled=True).astype(F32)

    gains = lax.all_gather(jnp.stack([attn_gain, mlp_gain]), "fsdp", axis=1, tiled=True)
    gain_attn = gains[0].astype(F32)
    gain_mlp = gains[1].astype(F32)
    full_qkv = gather(jnp.concatenate([w_query, w_key, w_value], axis=1))
    full_out = gather(w_out)
    side = (fsdp_index // PAIR) % 2

    order = (
        ((tensor_index ^ jnp.arange(n_tensor, dtype=jnp.int32)) * seq_dev)[:, None]
        + jnp.arange(seq_dev, dtype=jnp.int32)
    ).reshape(-1)
    prefix_all = jnp.take(prefix_len, order, axis=1)
    own_prefix = prefix_all[:, :seq_dev]
    pos_all = jnp.take(positions, order, axis=1)
    half_dim = HEAD_DIM // 2
    ladder = jnp.arange(half_dim, dtype=F32) * (2.0 / HEAD_DIM)
    inverse = 1.0 / rope_base**ladder

    x_float = inputs.reshape(micro_count * own_rows, model_width).astype(F32)
    grad_own = out_grads.reshape(micro_count * own_rows, model_width)
    unit_attn, scale_attn = normalize(x_float)
    normed = (unit_attn * gain_attn).astype(BF16)
    normed_pieces = spread_pieces(normed, False)
    cos_tab, sin_tab, pair_prefix = [], [], []
    for m in micros:
        angles = inverse[:, None] * pos_all[m].astype(F32).reshape(-1)[None, :]
        cos_tab.append(jnp.cos(angles))
        sin_tab.append(jnp.sin(angles))
        pair_prefix.append(split.pair_prefix(prefix_all[m], fsdp_index))
    cos_all = jnp.stack(cos_tab)
    sin_all = jnp.stack(sin_tab)
    half_cols = ff_cols // 2
    ffn_near = half_of([w_gate, w_up, w_down], side)
    ffn_far = half_of([w_gate, w_up, w_down], 1 - side)
    grad_pair = pair_join(after(paired(grad_own), full_qkv), micro_count)
    labels, taken = [], [0] * n_tensor
    spans_of = [(m, r) for m in micros for r in range(seq_dev)]
    peer = 0
    for piece in normed_pieces:
        size = piece.shape[0] // span_len
        start = taken[peer]
        labels.append(
            tuple((m, peer * seq_dev + r) for m, r in spans_of[start : start + size])
        )
        taken[peer] += size
        if taken[peer] == len(spans_of):
            peer += 1
    stack = project(normed_pieces, tuple(labels), full_qkv, cos_all, sin_all, span_len)
    packed = []
    for m in micros:
        packed.append(split.to_heads(stack[m]))
    normed_rows = gather_rows(whole_blocks(after(normed_pieces, stack)), micro_count)
    grad_pair = after(grad_pair, stack)
    grad_blocks = spread(grad_pair)
    ffn_other = swap(after(ffn_far, packed[-1]), "fsdp", PAIR)
    attn_out, attn_lse = [None] * micro_count, [None] * micro_count
    done = full_out
    for m in reversed(micros):
        attn_out[m], attn_lse[m] = attend_forward(pair_prefix[m], after(packed[m], done))
        done = attn_lse[m]
    mix_packed = split.to_spans(jnp.concatenate(attn_out, axis=1))
    ffn_other = after(ffn_other, attn_lse)
    shards = [
        own_half(
            side,
            ffn_near[:, i * half_cols : (i + 1) * half_cols],
            ffn_other[:, i * half_cols : (i + 1) * half_cols],
        )
        for i in range(3)
    ]
    full_gate = gather_half(after(shards[0], mix_packed))
    branch, resid, unit_mlp, scale_mlp, joined = [], [], [], [], []
    mix_rows, *parts = mix_out(mix_packed, full_out, micro_count, n_tensor)
    for m in micros:
        part = collect(parts[m * n_tensor : (m + 1) * n_tensor])
        res = x_float[m * own_rows : (m + 1) * own_rows] + part
        unit, scale = normalize(res)
        branch.append(part)
        resid.append(res)
        unit_mlp.append(unit)
        scale_mlp.append(scale)
        normed = paired((unit * gain_mlp).astype(BF16))
        joined.append(pair_join(normed, 1))
    full_up = gather_half(after(shards[1], joined))
    full_down = gather_half(shards[2])
    mlp_rows, first = [], None
    for m in micros:
        blocks = spread(joined[m] if first is None else after(joined[m], first), False)
        if first is None:
            first = blocks[1:3]
            grad_rows = gather_rows(after(grad_blocks, first), micro_count)
        mlp_rows.append(gather_rows(blocks, 1))

    hidden, gate_val, up_val = [], [], []
    for m in micros:
        gate, up, hid = ffn_forward(mlp_rows[m], full_gate, full_up)
        gate_val.append(gate)
        up_val.append(up)
        hidden.append(hid)
    hidden = jnp.concatenate(hidden, axis=0)
    down_grad = dot(grad_rows, hidden, 0, 0).astype(BF16)
    full_down = after(full_down, down_grad)
    part_down = scatter_half(down_grad)
    grad_gu, normed_part = [], []
    for m in micros:
        gate, up = ffn_back(grad_rows, m, full_down, gate_val[m], up_val[m])
        grad_gu.append(jnp.concatenate([gate, up], axis=1))
        normed_part.append(to_peers([gate, up], [full_gate, full_up], 1, n_tensor))
    all_mlp_rows = jnp.concatenate(after(mlp_rows, normed_part), axis=0)
    gu_grad = dot(all_mlp_rows, jnp.concatenate(grad_gu, axis=0), 0, 0).astype(BF16)
    part_gu = scatter_half(after(gu_grad, part_down))
    grad_resid, branch_rows = [], []
    mlp_gain_sum = jnp.zeros((model_width,), F32)
    for m in micros:
        total = collect(normed_part[m])
        grad_normed = total[:own_rows] + swap(
            total[own_rows:].astype(BF16), "fsdp", PAIR
        ).astype(F32)
        part, gain_part = norm_back(paired(grad_normed), unit_mlp[m], scale_mlp[m], gain_mlp)
        mlp_gain_sum = mlp_gain_sum + gain_part
        grad_res = grad_own[m * own_rows : (m + 1) * own_rows].astype(F32) + part
        grad_resid.append(grad_res)
        if m == 0:
            grad_res = after(grad_res, gu_grad)
        branch_rows += spread(grad_res.astype(BF16))
    grad_mix = mix_back(branch_rows, full_out, span_len)
    grad_out_all = split.to_heads(grad_mix)
    out_grad = dot(
        jnp.concatenate(after(branch_rows, grad_mix), axis=0), mix_rows, 0, 0
    ).astype(BF16)

    mlp_blocks = to_peers([after(hidden, out_grad)], [full_down], micro_count, n_tensor)
    own_out = scatter(after(out_grad, part_gu))

    grad_raw = []
    for m in micros:
        grad_out = after(grad_out_all, mlp_blocks, part_down if m else own_out)
        packed_grad = attend_back(pair_prefix[m], packed[m], attn_out[m], grad_out, attn_lse[m], m)
        grad_raw.append(split.to_spans(packed_grad))

    grad_qkv = unturn(grad_raw, cos_all, sin_all)
    qkv_grad = dot(normed_rows, grad_qkv, 0, 0).astype(BF16)
    own_gate, own_up = settle_half(part_gu, side, 2, qkv_grad)
    (own_down,) = settle_half(part_down, side, 1, qkv_grad)
    part = to_peers([after(grad_qkv, qkv_grad)], [full_qkv], micro_count, n_tensor)
    grad_normed = collect(part)
    mlp_part = collect(mlp_blocks, token=part)
    near = [mlp_part[2 * m * own_rows : (2 * m + 1) * own_rows] for m in micros]
    far = [mlp_part[(2 * m + 1) * own_rows : (2 * m + 2) * own_rows] for m in micros]
    far = swap(jnp.concatenate(far, axis=0).astype(BF16), "fsdp", PAIR).astype(F32)
    mlp_out = paired(jnp.concatenate(near, axis=0) + far)
    branch = jnp.concatenate(branch, axis=0)
    result = jnp.concatenate(resid, axis=0) + mlp_out
    output = result.astype(BF16).reshape(inputs.shape)
    valid = (query_index[None, None, :] >= own_prefix[:, :, None]).reshape(-1)
    stats = jnp.stack(
        [
            jnp.sum(
                jnp.where(valid, jnp.sum(part * part, axis=1), 0.0).reshape(
                    micro_count, seq_dev, span_len
                ),
                axis=2,
            )
            for part in (result, branch, mlp_out)
        ],
        axis=-1,
    )

    own_qkv = scatter(qkv_grad)
    part, attn_gain_sum = norm_back(grad_normed, unit_attn, scale_attn, gain_attn)
    input_grad = (jnp.concatenate(grad_resid, axis=0) + part).reshape(inputs.shape)

    stat_sum = tree_sum(stats, "fsdp")
    gain_sum = tree_sum(tree_sum(jnp.stack([attn_gain_sum, mlp_gain_sum]), "tensor"), "fsdp")
    row_share = model_width // n_fsdp
    own_gain = lax.dynamic_slice_in_dim(gain_sum, fsdp_index * row_share, row_share, 1)
    counts = ((seq_len - own_prefix) * model_width).astype(F32)
    rms_stats = jnp.sqrt(stat_sum / counts[..., None] + stat_eps)
    return (
        output,
        input_grad,
        own_gain[0],
        own_qkv[:, :head_cols],
        own_qkv[:, head_cols : 2 * head_cols],
        own_qkv[:, 2 * head_cols :],
        own_out,
        own_gain[1],
        own_gate,
        own_up,
        own_down,
        rms_stats,
    )


def solution(mesh):
    in_specs = (
        P(None, "tensor", "fsdp", None),
        P(None, "tensor", "fsdp", None),
        P(),
        P(None, None, "fsdp"),
        P("fsdp"),
        P("fsdp", "tensor"),
        P("fsdp", "tensor"),
        P("fsdp", "tensor"),
        P("fsdp", "tensor"),
        P("fsdp"),
        P("fsdp", "tensor"),
        P("fsdp", "tensor"),
        P("fsdp", "tensor"),
    )
    out_specs = (
        P(None, "tensor", "fsdp", None),
        P(None, "tensor", "fsdp", None),
        P("fsdp"),
        P("fsdp", "tensor"),
        P("fsdp", "tensor"),
        P("fsdp", "tensor"),
        P("fsdp", "tensor"),
        P("fsdp"),
        P("fsdp", "tensor"),
        P("fsdp", "tensor"),
        P("fsdp", "tensor"),
        P(None, "tensor", None),
    )
    return jax.shard_map(layer, mesh=mesh, in_specs=in_specs, out_specs=out_specs, check_vma=False)
```

```python
import functools
import math

import jax
import jax.numpy as jnp
from jax import lax
from jax.experimental import pallas as pl
from jax.experimental.pallas import tpu as pltpu
from jax.sharding import PartitionSpec as P

HEAD_DIM = 64

rope_base = 130000.0
norm_eps = 1e-05
stat_eps = 1e-06
LOG2E = math.log2(math.e)
MASKED = -1e30
PAIR = 2
BF16 = jnp.bfloat16
F32 = jnp.float32


def dot(left, right, left_dim, right_dim):
    return lax.dot_general(
        left, right, (((left_dim,), (right_dim,)), ((), ())), preferred_element_type=F32
    )


def normalize(values):
    row_scale = lax.rsqrt(jnp.mean(values * values, axis=-1, keepdims=True) + norm_eps)
    return (values * row_scale, row_scale)


def norm_back(grad_in, unit_rows, row_scale, gain):
    scaled = grad_in * gain
    inner_mean = jnp.mean(scaled * unit_rows, axis=-1, keepdims=True)
    return (
        row_scale * (scaled - unit_rows * inner_mean),
        jnp.sum(grad_in * unit_rows, axis=tuple(range(grad_in.ndim - 1))),
    )


def swap(value, axis, distance):
    count = lax.axis_size(axis)
    return lax.ppermute(value, axis, [(a, a ^ distance) for a in range(count)])


def after(value, *others):
    return lax.optimization_barrier((value, others))[0]


def spread_pieces(value, direct=True):
    count = lax.axis_size("tensor")
    if direct or count != 4:
        return [value] + [swap(value, "tensor", k) for k in range(1, count)]
    half = value.shape[0] // 2
    one = swap(value, "tensor", 1)
    two = swap(value, "tensor", 2)
    low = swap(two[:half], "tensor", 1)
    high = swap(one[half:], "tensor", 2)
    return [value, one, two, low, high]


def whole_blocks(pieces):
    rows = pieces[0].shape[0]
    far = [p for p in pieces if p.shape[0] < rows]
    return [p for p in pieces if p.shape[0] == rows] + (
        [jnp.concatenate(far, axis=0)] if far else []
    )


def spread(value, direct=True):
    return whole_blocks(spread_pieces(value, direct))


def collect(parts, direct=True, token=None):
    count = lax.axis_size("tensor")
    if direct or count != 4:
        blocks = [swap(parts[k].astype(BF16), "tensor", k) for k in range(1, count)]
        if token is not None:
            blocks = after(blocks, token)
        total = parts[0]
        for block in blocks:
            total = total + block.astype(F32)
        return total
    half = parts[0].shape[0] // 2
    far = parts[3].astype(BF16)
    low = swap(far[:half], "tensor", 1).astype(F32)
    high = swap(far[half:], "tensor", 2).astype(F32)
    one = jnp.concatenate([parts[1][:half], parts[1][half:] + high], axis=0)
    two = jnp.concatenate([parts[2][:half] + low, parts[2][half:]], axis=0)
    one = swap(one.astype(BF16), "tensor", 1).astype(F32)
    two = swap(two.astype(BF16), "tensor", 2).astype(F32)
    return parts[0] + one + two


def peer_swaps(parts):
    return [swap(part, "tensor", k) for k, part in enumerate(parts) if k]


def pair_join(value, micros):
    other = swap(value, "fsdp", PAIR)
    size = value.shape[0] // micros
    parts = [v[m * size : (m + 1) * size] for m in range(micros) for v in (value, other)]
    return jnp.concatenate(parts, axis=0)


def gather_rows(blocks, micros):
    size = blocks[0].shape[0] // micros
    return jnp.concatenate(
        [b[m * size : (m + 1) * size] for m in range(micros) for b in blocks], axis=0
    )


def paired_order(count):
    return [(f & ~3) | ((f & 1) << 1) | ((f >> 1) & 1) for f in range(count)]


def paired(values):
    count = lax.axis_size("fsdp")
    size = values.shape[-1] // count
    order = paired_order(count)
    parts = [lax.slice_in_dim(values, f * size, (f + 1) * size, axis=-1) for f in order]
    return jnp.concatenate(parts, axis=-1)


def pair_groups():
    count = lax.axis_size("fsdp")
    return [[f for f in range(count) if bool(f & PAIR) == side] for side in (False, True)]


def half_of(shards, side):
    half = shards[0].shape[1] // 2
    return jnp.concatenate(
        [lax.dynamic_slice_in_dim(s, side * half, half, 1) for s in shards], axis=1
    )


def order_pair(side, mine, other):
    return jnp.where(side == 0, mine, other), jnp.where(side == 0, other, mine)


def own_half(side, mine, other):
    return jnp.concatenate(order_pair(side, mine, other), axis=0)


def gather_half(shard):
    return lax.all_gather(
        shard,
        "fsdp",
        axis=0,
        tiled=True,
        axis_index_groups=pair_groups(),
    )


def scatter_half(grad):
    return lax.psum_scatter(
        grad, "fsdp", scatter_dimension=0, tiled=True, axis_index_groups=pair_groups()
    )


def settle_half(part, side, pieces, token):
    rows = part.shape[0] // 2
    mine = lax.dynamic_slice_in_dim(part, side * rows, rows, 0)
    other = swap(lax.dynamic_slice_in_dim(part, (1 - side) * rows, rows, 0), "fsdp", PAIR)
    low, high = order_pair(side, mine, after(other, token))
    half = part.shape[1] // pieces
    return [
        jnp.concatenate(
            [low[:, i * half : (i + 1) * half], high[:, i * half : (i + 1) * half]], axis=1
        ).astype(F32)
        for i in range(pieces)
    ]


def tree_sum(value, axis):
    step = 1
    while step < lax.axis_size(axis):
        value = value + swap(value, axis, step)
        step *= 2
    return value


def span_block(ref, first, count, lo, hi):
    return jnp.concatenate([ref[first + i, 0, lo:hi, :] for i in range(count)], axis=1)


def attn_blocks(spans, span_len):
    group = max(1, min(spans, 256 // span_len))
    while spans % group:
        group -= 1
    return group, spans // group


def key_count(q_block, block, prefix, blocks):
    return jnp.minimum(jnp.maximum(q_block + 1, (prefix + block - 1) // block), blocks)


def allowed_mask(k_block, q_block, block, prefix):
    key_id = k_block * block + lax.broadcasted_iota(jnp.int32, (block, block), 0)
    query_id = q_block * block + lax.broadcasted_iota(jnp.int32, (block, block), 1)
    return (key_id <= query_id) | (key_id < prefix)


def forward_kernel(prefix_ref, x_ref, out_ref, lse_ref, key_ref):
    spans, _, _, span_len = x_ref.shape
    group, blocks = attn_blocks(spans, span_len)
    block = group * span_len
    prefix = prefix_ref[pl.program_id(0)]
    coef = HEAD_DIM**-0.5 * LOG2E
    for kb in range(blocks):
        key_ref[pl.ds(kb * block, block), :] = span_block(
            x_ref, kb * group, group, HEAD_DIM, 2 * HEAD_DIM
        ).T
    for qb in range(blocks):
        q_t = span_block(x_ref, qb * group, group, 0, HEAD_DIM)

        def step(kb, carry):
            top, total, acc = carry
            keys = key_ref[pl.ds(pl.multiple_of(kb * block, block), block), :]
            scores = dot(keys, q_t, 1, 0) * coef
            scores = jnp.where(allowed_mask(kb, qb, block, prefix), scores, MASKED)
            new_top = jnp.maximum(top, jnp.max(scores, axis=0, keepdims=True))
            probs = jnp.exp2(scores - new_top)
            shrink = jnp.exp2(top - new_top)
            total = shrink * total + jnp.sum(probs, axis=0, keepdims=True)
            v_t = span_block(x_ref, kb * group, group, 2 * HEAD_DIM, 3 * HEAD_DIM)
            acc = shrink * acc + dot(v_t, probs.astype(BF16), 1, 0)
            return new_top, total, acc

        top, total, acc = lax.fori_loop(
            0,
            key_count(qb, block, prefix, blocks),
            step,
            (
                jnp.full((1, block), MASKED, F32),
                jnp.zeros((1, block), F32),
                jnp.zeros((HEAD_DIM, block), F32),
            ),
        )
        out = (acc / total).astype(BF16)
        for i in range(group):
            out_ref[qb * group + i, 0] = out[:, i * span_len : (i + 1) * span_len]
        lse_ref[0, :, qb * block : (qb + 1) * block] = top + jnp.log2(total)


def backward_kernel(
    prefix_ref, x_ref, o_ref, do_ref, lse_ref, dx_ref, key_ref, val_ref, dk_ref, dv_ref
):
    spans, _, _, span_len = x_ref.shape
    group, blocks = attn_blocks(spans, span_len)
    block = group * span_len
    prefix = prefix_ref[pl.program_id(0)]
    scale = HEAD_DIM**-0.5
    coef = scale * LOG2E
    for kb in range(blocks):
        rows = pl.ds(kb * block, block)
        key_ref[rows, :] = span_block(x_ref, kb * group, group, HEAD_DIM, 2 * HEAD_DIM).T
        val_ref[rows, :] = span_block(x_ref, kb * group, group, 2 * HEAD_DIM, 3 * HEAD_DIM).T
    dk_ref[...] = jnp.zeros_like(dk_ref)
    dv_ref[...] = jnp.zeros_like(dv_ref)
    for qb in range(blocks):
        q_t = span_block(x_ref, qb * group, group, 0, HEAD_DIM)
        do_t = span_block(do_ref, qb * group, group, 0, HEAD_DIM)
        o_t = span_block(o_ref, qb * group, group, 0, HEAD_DIM)
        delta = jnp.sum(do_t.astype(F32) * o_t.astype(F32), axis=0, keepdims=True)
        lse = lse_ref[0, :, qb * block : (qb + 1) * block]

        def step(kb, dq):
            rows = pl.ds(pl.multiple_of(kb * block, block), block)
            scores = dot(key_ref[rows, :], q_t, 1, 0) * coef
            scores = jnp.where(allowed_mask(kb, qb, block, prefix), scores, MASKED)
            probs = jnp.exp2(scores - lse)
            grad_probs = dot(val_ref[rows, :], do_t, 1, 0)
            grad_scores = (probs * (grad_probs - delta)).astype(BF16)
            dv_ref[kb] += dot(do_t, probs.astype(BF16), 1, 1)
            dk_ref[kb] += dot(q_t, grad_scores, 1, 1)
            k_t = span_block(x_ref, kb * group, group, HEAD_DIM, 2 * HEAD_DIM)
            return dq + dot(k_t, grad_scores, 1, 0)

        dq = lax.fori_loop(
            0,
            key_count(qb, block, prefix, blocks),
            step,
            jnp.zeros((HEAD_DIM, block), F32),
        )
        dq = (dq * scale).astype(BF16)
        for i in range(group):
            dx_ref[qb * group + i, 0, :HEAD_DIM, :] = dq[:, i * span_len : (i + 1) * span_len]
    for kb in range(blocks):
        dk = (dk_ref[kb] * scale).astype(BF16)
        dv = dv_ref[kb].astype(BF16)
        for i in range(group):
            cols = slice(i * span_len, (i + 1) * span_len)
            dx_ref[kb * group + i, 0, HEAD_DIM : 2 * HEAD_DIM, :] = dk[:, cols]
            dx_ref[kb * group + i, 0, 2 * HEAD_DIM :, :] = dv[:, cols]


def pair_spec(shape, first=0):
    return pl.BlockSpec((shape[0], 1) + shape[2:], lambda p, pre: (0, first + p, 0, 0))


def lse_spec(tokens):
    return pl.BlockSpec((1, 1, tokens), lambda p, pre: (p, 0, 0))


def attend_forward(prefix, packed):
    spans, _, _, span_len = packed.shape
    pairs = prefix.shape[0]
    tokens = spans * span_len
    out_shape = (spans, pairs, HEAD_DIM, span_len)
    return pl.pallas_call(
        forward_kernel,
        out_shape=(
            jax.ShapeDtypeStruct(out_shape, BF16),
            jax.ShapeDtypeStruct((pairs, 1, tokens), F32),
        ),
        grid_spec=pltpu.PrefetchScalarGridSpec(
            num_scalar_prefetch=1,
            grid=(pairs,),
            in_specs=[pair_spec(packed.shape)],
            out_specs=[pair_spec(out_shape), lse_spec(tokens)],
            scratch_shapes=[pltpu.VMEM((tokens, HEAD_DIM), BF16)],
        ),
        compiler_params=pltpu.CompilerParams(dimension_semantics=("arbitrary",)),
        name="attend_forward",
    )(prefix, packed)


def attend_back(prefix, packed, out, grad_out, lse, micro):
    spans, _, width, span_len = packed.shape
    pairs = prefix.shape[0]
    grad_shape = (spans, pairs, width, span_len)
    tokens = spans * span_len
    group, blocks = attn_blocks(spans, span_len)
    acc = pltpu.VMEM((blocks, HEAD_DIM, group * span_len), F32)
    return pl.pallas_call(
        backward_kernel,
        out_shape=jax.ShapeDtypeStruct(grad_shape, BF16),
        grid_spec=pltpu.PrefetchScalarGridSpec(
            num_scalar_prefetch=1,
            grid=(pairs,),
            in_specs=[
                pair_spec(packed.shape),
                pair_spec(out.shape),
                pair_spec(grad_out.shape, micro * pairs),
                lse_spec(tokens),
            ],
            out_specs=pair_spec(grad_shape),
            scratch_shapes=[
                pltpu.VMEM((tokens, HEAD_DIM), BF16),
                pltpu.VMEM((tokens, HEAD_DIM), BF16),
                acc,
                acc,
            ],
        ),
        compiler_params=pltpu.CompilerParams(dimension_semantics=("arbitrary",)),
        name="attend_back",
    )(prefix, packed, out, grad_out, lse)


def tile_of(size):
    return math.gcd(size, 256)


def whole(shape):
    return pl.BlockSpec(shape, lambda n: (0,) * len(shape), pipeline_mode=pl.Buffered(1))


def col_tile(rows, tile):
    return pl.BlockSpec((rows, tile), lambda n: (0, n))


def ffn_forward_kernel(x_ref, wg_ref, wu_ref, g_ref, u_ref, h_ref):
    x = x_ref[...]
    gate = dot(x, wg_ref[...], 1, 0)
    up = dot(x, wu_ref[...], 1, 0)
    g_ref[...] = gate
    u_ref[...] = up
    h_ref[...] = (gate * jax.nn.sigmoid(gate) * up).astype(BF16)


def ffn_forward(rows, w_gate, w_up):
    count, width = rows.shape
    units = w_gate.shape[1]
    tile = tile_of(units)
    return pl.pallas_call(
        ffn_forward_kernel,
        grid=(units // tile,),
        in_specs=[whole(rows.shape), col_tile(width, tile), col_tile(width, tile)],
        out_specs=[col_tile(count, tile)] * 3,
        out_shape=[
            jax.ShapeDtypeStruct((count, units), F32),
            jax.ShapeDtypeStruct((count, units), F32),
            jax.ShapeDtypeStruct((count, units), BF16),
        ],
        name="ffn_forward",
    )(rows, w_gate, w_up)


def ffn_back_kernel(dy_ref, wd_ref, g_ref, u_ref, dg_ref, du_ref):
    grad_hidden = dot(dy_ref[...], wd_ref[...], 1, 0)
    gate = g_ref[...]
    sig = jax.nn.sigmoid(gate)
    slope = sig * (1.0 + gate * (1.0 - sig))
    dg_ref[...] = (grad_hidden * u_ref[...] * slope).astype(BF16)
    du_ref[...] = (grad_hidden * (gate * sig)).astype(BF16)


def ffn_back(grad_rows, micro, w_down, gate, up):
    count, units = gate.shape
    width = w_down.shape[0]
    tile = tile_of(units)
    return pl.pallas_call(
        ffn_back_kernel,
        grid=(units // tile,),
        in_specs=[
            pl.BlockSpec((count, width), lambda n: (micro, 0), pipeline_mode=pl.Buffered(1)),
            col_tile(width, tile),
            col_tile(count, tile),
            col_tile(count, tile),
        ],
        out_specs=[col_tile(count, tile)] * 2,
        out_shape=[jax.ShapeDtypeStruct((count, units), BF16)] * 2,
        name="ffn_back",
    )(grad_rows, w_down, gate, up)


def to_peers_kernel(terms, micros, *refs):
    left = [r[...] for r in refs[:terms]]
    right = [r[...] for r in refs[terms : 2 * terms]]
    outs = refs[2 * terms :]
    total = None
    for a, b in zip(left, right):
        part = dot(a, b, 1, 1)
        total = part if total is None else total + part
    size = outs[0].shape[0] // micros
    for m in range(micros):
        for k, out in enumerate(outs):
            first = (m * len(outs) + k) * size
            out[m * size : (m + 1) * size, :] = total[first : first + size].astype(out.dtype)


def to_peers(lefts, rights, micros, peers):
    count, units = lefts[0].shape
    width = rights[0].shape[0]
    tile = tile_of(width)
    terms = len(lefts)
    rows = count // peers
    return pl.pallas_call(
        functools.partial(to_peers_kernel, terms, micros),
        grid=(width // tile,),
        in_specs=[whole(left.shape) for left in lefts]
        + [pl.BlockSpec((tile, units), lambda n: (n, 0))] * terms,
        out_specs=[col_tile(rows, tile)] * peers,
        out_shape=[
            jax.ShapeDtypeStruct((rows, width), BF16 if k else F32) for k in range(peers)
        ],
        name="to_peers",
    )(*lefts, *rights)


def row_tile(rows):
    return math.gcd(rows, 64)


def row_block(tile, width, first=0):
    return pl.BlockSpec((tile, width), lambda n: (first + n, 0))


def paired_store(ref, values, parts):
    size = values.shape[1] // parts
    for i, f in enumerate(paired_order(parts)):
        ref[:, i * size : (i + 1) * size] = values[:, f * size : (f + 1) * size]


def norm_rows_kernel(parts, x_ref, gain_ref, own_ref, *refs):
    blocks, (branch_ref, res_ref, normed_ref) = refs[:-3], refs[-3:]
    branch = own_ref[...]
    for ref in blocks:
        branch = branch + ref[...].astype(F32)
    res = x_ref[...].astype(F32) + branch
    unit, _ = normalize(res)
    branch_ref[...] = branch
    res_ref[...] = res
    paired_store(normed_ref, (unit * gain_ref[...]).astype(BF16), parts)


def norm_rows(inputs, micro, gain, own, blocks, parts):
    rows, width = own.shape
    tile = row_tile(rows)
    return pl.pallas_call(
        functools.partial(norm_rows_kernel, parts),
        grid=(rows // tile,),
        in_specs=[row_block(tile, width, micro * (rows // tile)), whole(gain.shape)]
        + [row_block(tile, width)] * (1 + len(blocks)),
        out_specs=[row_block(tile, width)] * 3,
        out_shape=[jax.ShapeDtypeStruct((rows, width), kind) for kind in (F32, F32, BF16)],
        name="norm_rows",
    )(inputs, gain, own, *blocks)


def peer_sum_kernel(*refs):
    count = (len(refs) - 2) // 2
    for pieces, out in ((refs[:count], refs[-2]), (refs[count:-2], refs[-1])):
        total = pieces[0][...]
        for ref in pieces[1:]:
            total = total + ref[...].astype(F32)
        out[...] = total.astype(out.dtype)


def peer_sum(own, blocks):
    rows, width = own.shape[0] // 2, own.shape[1]
    tile = row_tile(rows)
    pieces = [own] + list(blocks)
    return pl.pallas_call(
        peer_sum_kernel,
        grid=(rows // tile,),
        in_specs=[
            row_block(tile, width, half * (rows // tile)) for half in range(2) for _ in pieces
        ],
        out_specs=[row_block(tile, width)] * 2,
        out_shape=[jax.ShapeDtypeStruct((rows, width), kind) for kind in (F32, BF16)],
        name="peer_sum",
    )(*pieces, *pieces)


def norm_grad_kernel(parts, dy_ref, gain_ref, near_ref, far_ref, res_ref, grad_ref, low_ref, sum_ref, dn_ref):
    paired_store(dn_ref, near_ref[...] + far_ref[...].astype(F32), parts)
    unit, scale = normalize(res_ref[...])
    part, gain_part = norm_back(dn_ref[...], unit, scale, gain_ref[...])
    grad = dy_ref[...].astype(F32) + part
    grad_ref[...] = grad
    low_ref[...] = grad.astype(BF16)

    @pl.when(pl.program_id(0) == 0)
    def _():
        sum_ref[...] = jnp.zeros_like(sum_ref)

    sum_ref[...] += gain_part[None]


def norm_grad(grads, micro, gain, near, far, res, parts):
    rows, width = near.shape
    tile = row_tile(rows)
    return pl.pallas_call(
        functools.partial(norm_grad_kernel, parts),
        grid=(rows // tile,),
        in_specs=[row_block(tile, width, micro * (rows // tile)), whole(gain.shape)]
        + [row_block(tile, width)] * 3,
        out_specs=[row_block(tile, width)] * 2 + [pl.BlockSpec((1, width), lambda n: (0, 0))],
        out_shape=[
            jax.ShapeDtypeStruct((rows, width), F32),
            jax.ShapeDtypeStruct((rows, width), BF16),
            jax.ShapeDtypeStruct((1, width), F32),
        ],
        scratch_shapes=[pltpu.VMEM((tile, width), F32)],
        name="norm_grad",
    )(grads, gain, near, far, res)


def turn(values, cos_tab, sin_tab):
    half = HEAD_DIM // 2
    first, second = values[:half], values[half:]
    return jnp.concatenate(
        [first * cos_tab - second * sin_tab, second * cos_tab + first * sin_tab], axis=0
    )


def project_kernel(labels, *refs):
    count = len(labels)
    wq_ref, wk_ref, wv_ref, cos_ref, sin_ref = refs[count : count + 5]
    outs = refs[count + 5 :]
    span = outs[0].shape[3]
    weights = jnp.concatenate([wq_ref[...], wk_ref[...], wv_ref[...]], axis=1)
    for ref, places in zip(refs, labels):
        cols_all = dot(ref[...], weights, 1, 0).T
        for i, (m, k) in enumerate(places):
            cols = cols_all[:, i * span : (i + 1) * span]
            cos_tab = cos_ref[m, :, k * span : (k + 1) * span]
            sin_tab = sin_ref[m, :, k * span : (k + 1) * span]
            for h in range(2):
                for kind in range(3):
                    first = (2 * kind + h) * HEAD_DIM
                    value = cols[first : first + HEAD_DIM]
                    if kind < 2:
                        value = turn(value, cos_tab, sin_tab)
                    outs[m][h, k, kind * HEAD_DIM : (kind + 1) * HEAD_DIM, :] = value.astype(BF16)


def project(pieces, labels, weights, cos_tab, sin_tab, span):
    micros, _, tokens = cos_tab.shape
    width = weights.shape[0]
    cols = weights.shape[1] // 3
    blocks = cols // (2 * HEAD_DIM)
    seqs = tokens // span
    out = (cols // HEAD_DIM, seqs, 3 * HEAD_DIM, span)
    return pl.pallas_call(
        functools.partial(project_kernel, labels),
        grid=(blocks,),
        in_specs=[whole(p.shape) for p in pieces]
        + [
            pl.BlockSpec((width, 2 * HEAD_DIM), lambda n, kind=kind: (0, kind * blocks + n))
            for kind in range(3)
        ]
        + [whole(cos_tab.shape)] * 2,
        out_specs=[pl.BlockSpec((2,) + out[1:], lambda n: (n, 0, 0, 0))] * micros,
        out_shape=[jax.ShapeDtypeStruct(out, BF16)] * micros,
        name="project",
    )(*pieces, weights, weights, weights, cos_tab, sin_tab)


def mix_out_kernel(micros, x_ref, w_ref, mix_ref, *outs):
    heads, seqs, _, span = x_ref.shape
    peers = len(outs) // micros
    own = seqs // (micros * peers)

    @pl.when(pl.program_id(0) == 0)
    def _():
        for q in range(seqs):
            mix = x_ref[:, q].reshape(heads * HEAD_DIM, span)
            mix_ref[q * span : (q + 1) * span, :] = mix.T

    total = dot(mix_ref[...], w_ref[...], 1, 1)
    size = own * span
    for i, out in enumerate(outs):
        out[...] = total[i * size : (i + 1) * size].astype(out.dtype)


def mix_out(packed, weights, micros, peers):
    _, seqs, _, span = packed.shape
    width, cols = weights.shape
    tile = tile_of(width)
    rows = seqs * span // (micros * peers)
    kinds = [BF16 if k else F32 for _ in range(micros) for k in range(peers)]
    return pl.pallas_call(
        functools.partial(mix_out_kernel, micros),
        grid=(width // tile,),
        in_specs=[whole(packed.shape), pl.BlockSpec((tile, cols), lambda n: (n, 0))],
        out_specs=[pl.BlockSpec((seqs * span, cols), lambda n: (0, 0))]
        + [col_tile(rows, tile)] * len(kinds),
        out_shape=[jax.ShapeDtypeStruct((seqs * span, cols), BF16)]
        + [jax.ShapeDtypeStruct((rows, width), kind) for kind in kinds],
        name="mix_out",
    )(packed, weights)


def mix_back_kernel(*refs):
    pieces, (w_ref, out_ref) = refs[:-2], refs[-2:]
    heads, _, _, span = out_ref.shape
    q = 0
    for ref in pieces:
        cols = dot(ref[...], w_ref[...], 1, 0).T.astype(BF16)
        for i in range(ref.shape[0] // span):
            for h in range(heads):
                out_ref[h, q] = cols[
                    h * HEAD_DIM : (h + 1) * HEAD_DIM, i * span : (i + 1) * span
                ]
            q += 1


def mix_back(pieces, weights, span):
    width, cols = weights.shape
    tile = tile_of(cols)
    seqs = sum(p.shape[0] for p in pieces) // span
    heads = cols // HEAD_DIM
    return pl.pallas_call(
        mix_back_kernel,
        grid=(cols // tile,),
        in_specs=[whole(p.shape) for p in pieces] + [col_tile(width, tile)],
        out_specs=pl.BlockSpec((tile // HEAD_DIM, seqs, HEAD_DIM, span), lambda n: (n, 0, 0, 0)),
        out_shape=jax.ShapeDtypeStruct((heads, seqs, HEAD_DIM, span), BF16),
        name="mix_back",
    )(*pieces, weights)


def unturn_kernel(blocks, *refs):
    packed, (cos_ref, sin_ref, out_ref) = refs[:-3], refs[-3:]
    _, seqs, _, span = packed[0].shape
    plain = pl.program_id(0) >= 2 * blocks
    for m, ref in enumerate(packed):
        for k in range(seqs):
            cos_tab = jnp.where(plain, 1.0, cos_ref[m, :, k * span : (k + 1) * span])
            sin_tab = jnp.where(plain, 0.0, -sin_ref[m, :, k * span : (k + 1) * span])
            pair = jnp.concatenate(
                [turn(ref[h, k].astype(F32), cos_tab, sin_tab) for h in range(2)], axis=0
            )
            first = (m * seqs + k) * span
            out_ref[first : first + span, :] = pair.T.astype(BF16)


def unturn(packed, cos_tab, sin_tab):
    heads, seqs, _, span = packed[0].shape
    blocks = heads // 2
    rows = len(packed) * seqs * span
    return pl.pallas_call(
        functools.partial(unturn_kernel, blocks),
        grid=(3 * blocks,),
        in_specs=[
            pl.BlockSpec(
                (2, seqs, HEAD_DIM, span), lambda n: (n % blocks, 0, n // blocks, 0)
            )
        ]
        * len(packed)
        + [whole(cos_tab.shape)] * 2,
        out_specs=col_tile(rows, 2 * HEAD_DIM),
        out_shape=jax.ShapeDtypeStruct((rows, 3 * heads * HEAD_DIM), BF16),
        name="unturn",
    )(*packed, cos_tab, sin_tab)


class HeadSplit:
    def __init__(self, n_fsdp, head_count, seqs):
        self.head_groups = math.gcd(n_fsdp, head_count)
        self.seq_groups = n_fsdp // self.head_groups
        self.heads_per = head_count // self.head_groups
        self.seqs_per = seqs // self.seq_groups

    def to_heads(self, packed):
        width, span = packed.shape[2:]
        packed = packed.reshape(
            self.head_groups, self.heads_per, -1, self.seq_groups, self.seqs_per, width, span
        ).transpose(3, 0, 2, 1, 4, 5, 6)
        packed = packed.reshape(self.seq_groups * self.head_groups, -1, width, span)
        return lax.all_to_all(packed, "fsdp", split_axis=0, concat_axis=0, tiled=True)

    def to_spans(self, packed):
        width, span = packed.shape[2:]
        packed = lax.all_to_all(packed, "fsdp", split_axis=0, concat_axis=0, tiled=True)
        packed = packed.reshape(
            self.seq_groups, self.head_groups, -1, self.heads_per, self.seqs_per, width, span
        ).transpose(1, 3, 2, 0, 4, 5, 6)
        return packed.reshape(self.head_groups * self.heads_per, -1, width, span)

    def pair_prefix(self, prefix, fsdp_index):
        mine = lax.dynamic_slice_in_dim(
            prefix, (fsdp_index // self.head_groups) * self.seqs_per, self.seqs_per, 0
        )
        return jnp.tile(mine, self.heads_per)


def layer(
    inputs,
    out_grads,
    prefix_len,
    positions,
    attn_gain,
    w_query,
    w_key,
    w_value,
    w_out,
    mlp_gain,
    w_gate,
    w_up,
    w_down,
):
    micro_count, seq_dev, span_len, model_width = inputs.shape
    n_tensor = lax.axis_size("tensor")
    n_fsdp = lax.axis_size("fsdp")
    seq_mb = seq_dev * n_tensor
    seq_len = span_len * n_fsdp
    own_rows = seq_dev * span_len
    head_cols = w_query.shape[1]
    head_count = head_cols // HEAD_DIM
    ff_cols = w_gate.shape[1]
    fsdp_index = lax.axis_index("fsdp")
    tensor_index = lax.axis_index("tensor")
    query_index = fsdp_index * span_len + jnp.arange(span_len, dtype=jnp.int32)
    split = HeadSplit(n_fsdp, head_count, seq_mb)
    micros = range(micro_count)

    def gather(shard):
        return lax.all_gather(shard, "fsdp", axis=0, tiled=True)

    def scatter(grad):
        return lax.psum_scatter(grad, "fsdp", scatter_dimension=0, tiled=True).astype(F32)

    gains = lax.all_gather(jnp.stack([attn_gain, mlp_gain]), "fsdp", axis=1, tiled=True)
    gain_attn = gains[0].astype(F32)
    gain_mlp = gains[1].astype(F32)
    full_qkv = gather(jnp.concatenate([w_query, w_key, w_value], axis=1))
    full_out = gather(w_out)
    side = (fsdp_index // PAIR) % 2

    order = (
        ((tensor_index ^ jnp.arange(n_tensor, dtype=jnp.int32)) * seq_dev)[:, None]
        + jnp.arange(seq_dev, dtype=jnp.int32)
    ).reshape(-1)
    prefix_all = jnp.take(prefix_len, order, axis=1)
    own_prefix = prefix_all[:, :seq_dev]
    pos_all = jnp.take(positions, order, axis=1)
    half_dim = HEAD_DIM // 2
    ladder = jnp.arange(half_dim, dtype=F32) * (2.0 / HEAD_DIM)
    inverse = 1.0 / rope_base**ladder

    x_float = inputs.reshape(micro_count * own_rows, model_width).astype(F32)
    grad_own = out_grads.reshape(micro_count * own_rows, model_width)
    unit_attn, scale_attn = normalize(x_float)
    normed = (unit_attn * gain_attn).astype(BF16)
    normed_pieces = spread_pieces(normed, False)
    cos_tab, sin_tab, pair_prefix = [], [], []
    for m in micros:
        angles = inverse[:, None] * pos_all[m].astype(F32).reshape(-1)[None, :]
        cos_tab.append(jnp.cos(angles))
        sin_tab.append(jnp.sin(angles))
        pair_prefix.append(split.pair_prefix(prefix_all[m], fsdp_index))
    cos_all = jnp.stack(cos_tab)
    sin_all = jnp.stack(sin_tab)
    half_cols = ff_cols // 2
    ffn_near = half_of([w_gate, w_up, w_down], side)
    ffn_far = half_of([w_gate, w_up, w_down], 1 - side)
    grad_pair = pair_join(after(paired(grad_own), full_qkv), micro_count)
    labels, taken = [], [0] * n_tensor
    spans_of = [(m, r) for m in micros for r in range(seq_dev)]
    peer = 0
    for piece in normed_pieces:
        size = piece.shape[0] // span_len
        start = taken[peer]
        labels.append(
            tuple((m, peer * seq_dev + r) for m, r in spans_of[start : start + size])
        )
        taken[peer] += size
        if taken[peer] == len(spans_of):
            peer += 1
    stack = project(normed_pieces, tuple(labels), full_qkv, cos_all, sin_all, span_len)
    packed = []
    for m in micros:
        packed.append(split.to_heads(stack[m]))
    normed_rows = gather_rows(whole_blocks(after(normed_pieces, stack)), micro_count)
    grad_pair = after(grad_pair, stack)
    grad_blocks = spread(grad_pair)
    ffn_other = swap(after(ffn_far, packed[-1]), "fsdp", PAIR)
    attn_out, attn_lse = [None] * micro_count, [None] * micro_count
    done = full_out
    for m in reversed(micros):
        attn_out[m], attn_lse[m] = attend_forward(pair_prefix[m], after(packed[m], done))
        done = attn_lse[m]
    mix_packed = split.to_spans(jnp.concatenate(attn_out, axis=1))
    ffn_other = after(ffn_other, attn_lse)
    shards = [
        own_half(
            side,
            ffn_near[:, i * half_cols : (i + 1) * half_cols],
            ffn_other[:, i * half_cols : (i + 1) * half_cols],
        )
        for i in range(3)
    ]
    full_gate = gather_half(after(shards[0], mix_packed))
    branch, resid, others, normed_mlp, joined = [], [], [], [], []
    flat_inputs = inputs.reshape(micro_count * own_rows, model_width)
    gain_rows = gain_mlp[None]
    mix_rows, *parts = mix_out(mix_packed, full_out, micro_count, n_tensor)
    for m in micros:
        own, *sent = parts[m * n_tensor : (m + 1) * n_tensor]
        blocks = peer_swaps([own] + sent)
        if m:
            blocks = after(blocks, normed_mlp)
        part, res, normed = norm_rows(flat_inputs, m, gain_rows, own, blocks, n_fsdp)
        branch.append(part)
        resid.append(res)
        normed_mlp.append(normed)
        others.append(swap(normed, "fsdp", PAIR))
    for m in micros:
        other = after(others[m], joined) if m else others[m]
        joined.append(jnp.concatenate([normed_mlp[m], other], axis=0))
    full_up = gather_half(after(shards[1], joined))
    full_down = gather_half(shards[2])
    mlp_rows, first = [], None
    for m in micros:
        blocks = spread(joined[m] if first is None else after(joined[m], first), False)
        if first is None:
            first = blocks[1:3]
            grad_rows = gather_rows(after(grad_blocks, first), micro_count)
        mlp_rows.append(gather_rows(blocks, 1))

    hidden, gate_val, up_val = [], [], []
    for m in micros:
        gate, up, hid = ffn_forward(mlp_rows[m], full_gate, full_up)
        gate_val.append(gate)
        up_val.append(up)
        hidden.append(hid)
    hidden = jnp.concatenate(hidden, axis=0)
    down_grad = dot(grad_rows, hidden, 0, 0).astype(BF16)
    full_down = after(full_down, down_grad)
    part_down = scatter_half(down_grad)
    grad_gu, normed_part = [], []
    for m in micros:
        gate_in = after(gate_val[m], normed_part) if m else gate_val[m]
        gate, up = ffn_back(grad_rows, m, full_down, gate_in, up_val[m])
        grad_gu.append(jnp.concatenate([gate, up], axis=1))
        normed_part.append(to_peers([gate, up], [full_gate, full_up], 1, n_tensor))
    all_mlp_rows = jnp.concatenate(after(mlp_rows, normed_part), axis=0)
    gu_grad = dot(all_mlp_rows, jnp.concatenate(grad_gu, axis=0), 0, 0).astype(BF16)
    part_gu = scatter_half(after(gu_grad, part_down))
    grad_resid, branch_rows, near_far, mlp_gain_parts = [], [], [], []
    for m in micros:
        blocks = peer_swaps(normed_part[m])
        blocks = after(blocks, near_far[-1][0] if m else gu_grad)
        near, far = peer_sum(normed_part[m][0], blocks)
        near_far.append((near, swap(far, "fsdp", PAIR)))
    low = None
    for m in micros:
        near, far = near_far[m]
        if m:
            far = after(far, low)
        grad_res, low, gain_part = norm_grad(grad_own, m, gain_rows, near, far, resid[m], n_fsdp)
        mlp_gain_parts.append(gain_part[0])
        grad_resid.append(grad_res)
        branch_rows += spread(low)
    mlp_gain_sum = sum(mlp_gain_parts)
    grad_mix = mix_back(branch_rows, full_out, span_len)
    grad_out_all = split.to_heads(grad_mix)
    out_grad = dot(
        jnp.concatenate(after(branch_rows, grad_mix), axis=0), mix_rows, 0, 0
    ).astype(BF16)

    mlp_blocks = to_peers([after(hidden, out_grad)], [full_down], micro_count, n_tensor)
    own_out = scatter(after(out_grad, part_gu, mlp_blocks))

    grad_raw = []
    packed_grads = []
    for m in micros:
        grad_out = after(grad_out_all, mlp_blocks, part_down if m else own_out)
        packed_grad = attend_back(pair_prefix[m], packed[m], attn_out[m], grad_out, attn_lse[m], m)
        packed_grads.append(packed_grad)
        grad_raw.append(split.to_spans(packed_grad))

    mlp_part = collect(mlp_blocks, token=packed_grads[0])
    near = [mlp_part[2 * m * own_rows : (2 * m + 1) * own_rows] for m in micros]
    far = [mlp_part[(2 * m + 1) * own_rows : (2 * m + 2) * own_rows] for m in micros]
    far = swap(jnp.concatenate(far, axis=0).astype(BF16), "fsdp", PAIR)
    grad_qkv = unturn(grad_raw, cos_all, sin_all)
    qkv_grad = dot(normed_rows, grad_qkv, 0, 0).astype(BF16)
    own_gate, own_up = settle_half(part_gu, side, 2, qkv_grad)
    (own_down,) = settle_half(part_down, side, 1, qkv_grad)
    part = to_peers([after(grad_qkv, qkv_grad)], [full_qkv], micro_count, n_tensor)
    grad_normed = collect(part)
    far = after(far, part).astype(F32)
    mlp_out = paired(jnp.concatenate(near, axis=0) + far)
    branch = jnp.concatenate(branch, axis=0)
    result = jnp.concatenate(resid, axis=0) + mlp_out
    output = result.astype(BF16).reshape(inputs.shape)
    valid = (query_index[None, None, :] >= own_prefix[:, :, None]).reshape(-1)
    stats = jnp.stack(
        [
            jnp.sum(
                jnp.where(valid, jnp.sum(part * part, axis=1), 0.0).reshape(
                    micro_count, seq_dev, span_len
                ),
                axis=2,
            )
            for part in (result, branch, mlp_out)
        ],
        axis=-1,
    )

    own_qkv = scatter(qkv_grad)
    part, attn_gain_sum = norm_back(grad_normed, unit_attn, scale_attn, gain_attn)
    input_grad = (jnp.concatenate(grad_resid, axis=0) + part).reshape(inputs.shape)

    stat_sum = tree_sum(stats, "fsdp")
    gain_sum = tree_sum(tree_sum(jnp.stack([attn_gain_sum, mlp_gain_sum]), "tensor"), "fsdp")
    row_share = model_width // n_fsdp
    own_gain = lax.dynamic_slice_in_dim(gain_sum, fsdp_index * row_share, row_share, 1)
    counts = ((seq_len - own_prefix) * model_width).astype(F32)
    rms_stats = jnp.sqrt(stat_sum / counts[..., None] + stat_eps)
    return (
        output,
        input_grad,
        own_gain[0],
        own_qkv[:, :head_cols],
        own_qkv[:, head_cols : 2 * head_cols],
        own_qkv[:, 2 * head_cols :],
        own_out,
        own_gain[1],
        own_gate,
        own_up,
        own_down,
        rms_stats,
    )


def solution(mesh):
    in_specs = (
        P(None, "tensor", "fsdp", None),
        P(None, "tensor", "fsdp", None),
        P(),
        P(None, None, "fsdp"),
        P("fsdp"),
        P("fsdp", "tensor"),
        P("fsdp", "tensor"),
        P("fsdp", "tensor"),
        P("fsdp", "tensor"),
        P("fsdp"),
        P("fsdp", "tensor"),
        P("fsdp", "tensor"),
        P("fsdp", "tensor"),
    )
    out_specs = (
        P(None, "tensor", "fsdp", None),
        P(None, "tensor", "fsdp", None),
        P("fsdp"),
        P("fsdp", "tensor"),
        P("fsdp", "tensor"),
        P("fsdp", "tensor"),
        P("fsdp", "tensor"),
        P("fsdp"),
        P("fsdp", "tensor"),
        P("fsdp", "tensor"),
        P("fsdp", "tensor"),
        P(None, "tensor", None),
    )
    return jax.shard_map(layer, mesh=mesh, in_specs=in_specs, out_specs=out_specs, check_vma=False)
```

```python
import functools
import math

import jax
import jax.numpy as jnp
from jax import lax
from jax.experimental import pallas as pl
from jax.experimental.pallas import tpu as pltpu
from jax.sharding import PartitionSpec as P

HEAD_DIM = 64

rope_base = 130000.0
norm_eps = 1e-05
stat_eps = 1e-06
LOG2E = math.log2(math.e)
MASKED = -1e30
PAIR = 2
FSDP, TENSOR = "fsdp", "tensor"
BF16 = jnp.bfloat16
F32 = jnp.float32


def dot(left, right, left_dim, right_dim):
    return lax.dot_general(
        left, right, (((left_dim,), (right_dim,)), ((), ())), preferred_element_type=F32
    )


def normalize(values):
    row_scale = lax.rsqrt(jnp.mean(values * values, axis=-1, keepdims=True) + norm_eps)
    return (values * row_scale, row_scale)


def norm_back(grad_in, unit_rows, row_scale, gain):
    scaled = grad_in * gain
    inner_mean = jnp.mean(scaled * unit_rows, axis=-1, keepdims=True)
    return (
        row_scale * (scaled - unit_rows * inner_mean),
        jnp.sum(grad_in * unit_rows, axis=tuple(range(grad_in.ndim - 1))),
    )


def swap(value, axis, distance):
    count = lax.axis_size(axis)
    return lax.ppermute(value, axis, [(a, a ^ distance) for a in range(count)])


def after(value, *others):
    return lax.optimization_barrier((value, others))[0]


def spread_pieces(value, direct=True):
    count = lax.axis_size(TENSOR)
    if direct or count != 4:
        return [value] + [swap(value, TENSOR, k) for k in range(1, count)]
    half = value.shape[0] // 2
    one = swap(value, TENSOR, 1)
    two = swap(value, TENSOR, 2)
    low = swap(two[:half], TENSOR, 1)
    high = swap(one[half:], TENSOR, 2)
    return [value, one, two, low, high]


def whole_blocks(pieces):
    rows = pieces[0].shape[0]
    far = [p for p in pieces if p.shape[0] < rows]
    return [p for p in pieces if p.shape[0] == rows] + (
        [jnp.concatenate(far, axis=0)] if far else []
    )


def spread(value, direct=True):
    return whole_blocks(spread_pieces(value, direct))


def collect(parts, direct=True, token=None):
    count = lax.axis_size(TENSOR)
    if direct or count != 4:
        blocks = [swap(parts[k].astype(BF16), TENSOR, k) for k in range(1, count)]
        if token is not None:
            blocks = after(blocks, token)
        total = parts[0]
        for block in blocks:
            total = total + block.astype(F32)
        return total
    half = parts[0].shape[0] // 2
    far = parts[3].astype(BF16)
    low = swap(far[:half], TENSOR, 1).astype(F32)
    high = swap(far[half:], TENSOR, 2).astype(F32)
    one = jnp.concatenate([parts[1][:half], parts[1][half:] + high], axis=0)
    two = jnp.concatenate([parts[2][:half] + low, parts[2][half:]], axis=0)
    one = swap(one.astype(BF16), TENSOR, 1).astype(F32)
    two = swap(two.astype(BF16), TENSOR, 2).astype(F32)
    return parts[0] + one + two


def peer_swaps(parts):
    return [swap(part, TENSOR, k) for k, part in enumerate(parts) if k]


def pair_join(value, micros):
    other = swap(value, FSDP, PAIR)
    size = value.shape[0] // micros
    parts = [v[m * size : (m + 1) * size] for m in range(micros) for v in (value, other)]
    return jnp.concatenate(parts, axis=0)


def gather_rows(blocks, micros):
    size = blocks[0].shape[0] // micros
    return jnp.concatenate(
        [b[m * size : (m + 1) * size] for m in range(micros) for b in blocks], axis=0
    )


def paired_order(count):
    return [(f & ~3) | ((f & 1) << 1) | ((f >> 1) & 1) for f in range(count)]


def paired(values):
    count = lax.axis_size(FSDP)
    size = values.shape[-1] // count
    order = paired_order(count)
    parts = [lax.slice_in_dim(values, f * size, (f + 1) * size, axis=-1) for f in order]
    return jnp.concatenate(parts, axis=-1)


def pair_groups():
    count = lax.axis_size(FSDP)
    return [[f for f in range(count) if bool(f & PAIR) == side] for side in (False, True)]


def half_of(shards, side):
    half = shards[0].shape[1] // 2
    return jnp.concatenate(
        [lax.dynamic_slice_in_dim(s, side * half, half, 1) for s in shards], axis=1
    )


def order_pair(side, mine, other):
    return jnp.where(side == 0, mine, other), jnp.where(side == 0, other, mine)


def own_half(side, mine, other):
    return jnp.concatenate(order_pair(side, mine, other), axis=0)


def gather_half(shard):
    return lax.all_gather(
        shard,
        FSDP,
        axis=0,
        tiled=True,
        axis_index_groups=pair_groups(),
    )


def scatter_half(grad):
    return lax.psum_scatter(
        grad, FSDP, scatter_dimension=0, tiled=True, axis_index_groups=pair_groups()
    )


def settle_half(part, side, pieces, token):
    rows = part.shape[0] // 2
    mine = lax.dynamic_slice_in_dim(part, side * rows, rows, 0)
    other = swap(lax.dynamic_slice_in_dim(part, (1 - side) * rows, rows, 0), FSDP, PAIR)
    low, high = order_pair(side, mine, after(other, token))
    half = part.shape[1] // pieces
    return [
        jnp.concatenate(
            [low[:, i * half : (i + 1) * half], high[:, i * half : (i + 1) * half]], axis=1
        ).astype(F32)
        for i in range(pieces)
    ]


def tree_sum(value, axis):
    step = 1
    while step < lax.axis_size(axis):
        value = value + swap(value, axis, step)
        step *= 2
    return value


def span_block(ref, first, count, lo, hi):
    return jnp.concatenate([ref[first + i, 0, lo:hi, :] for i in range(count)], axis=1)


def attn_blocks(spans, span_len):
    group = max(1, min(spans, 256 // span_len))
    while spans % group:
        group -= 1
    return group, spans // group


def key_count(q_block, block, prefix, blocks):
    return jnp.minimum(jnp.maximum(q_block + 1, (prefix + block - 1) // block), blocks)


def allowed_mask(k_block, q_block, block, prefix):
    key_id = k_block * block + lax.broadcasted_iota(jnp.int32, (block, block), 0)
    query_id = q_block * block + lax.broadcasted_iota(jnp.int32, (block, block), 1)
    return (key_id <= query_id) | (key_id < prefix)


def forward_kernel(prefix_ref, x_ref, out_ref, lse_ref, key_ref):
    spans, _, _, span_len = x_ref.shape
    group, blocks = attn_blocks(spans, span_len)
    block = group * span_len
    prefix = prefix_ref[pl.program_id(0)]
    coef = HEAD_DIM**-0.5 * LOG2E
    for kb in range(blocks):
        key_ref[pl.ds(kb * block, block), :] = span_block(
            x_ref, kb * group, group, HEAD_DIM, 2 * HEAD_DIM
        ).T
    for qb in range(blocks):
        q_t = span_block(x_ref, qb * group, group, 0, HEAD_DIM)

        def step(kb, carry, masked=True):
            top, total, acc = carry
            first = pl.multiple_of(kb * block, block) if masked else kb * block
            keys = key_ref[pl.ds(first, block), :]
            scores = dot(keys, q_t, 1, 0) * coef
            if masked:
                scores = jnp.where(allowed_mask(kb, qb, block, prefix), scores, MASKED)
            new_top = jnp.maximum(top, jnp.max(scores, axis=0, keepdims=True))
            probs = jnp.exp2(scores - new_top)
            shrink = jnp.exp2(top - new_top)
            total = shrink * total + jnp.sum(probs, axis=0, keepdims=True)
            v_t = span_block(x_ref, kb * group, group, 2 * HEAD_DIM, 3 * HEAD_DIM)
            acc = shrink * acc + dot(v_t, probs.astype(BF16), 1, 0)
            return new_top, total, acc

        carry = (
            jnp.full((1, block), MASKED, F32),
            jnp.zeros((1, block), F32),
            jnp.zeros((HEAD_DIM, block), F32),
        )
        for kb in range(qb):
            carry = step(kb, carry, False)
        top, total, acc = lax.fori_loop(
            qb, key_count(qb, block, prefix, blocks), step, carry
        )
        out = (acc / total).astype(BF16)
        for i in range(group):
            out_ref[qb * group + i, 0] = out[:, i * span_len : (i + 1) * span_len]
        lse_ref[0, :, qb * block : (qb + 1) * block] = top + jnp.log2(total)


def backward_kernel(
    prefix_ref, x_ref, o_ref, do_ref, lse_ref, dx_ref, key_ref, val_ref, dk_ref, dv_ref
):
    spans, _, _, span_len = x_ref.shape
    group, blocks = attn_blocks(spans, span_len)
    block = group * span_len
    prefix = prefix_ref[pl.program_id(0)]
    scale = HEAD_DIM**-0.5
    coef = scale * LOG2E
    for kb in range(blocks):
        rows = pl.ds(kb * block, block)
        key_ref[rows, :] = span_block(x_ref, kb * group, group, HEAD_DIM, 2 * HEAD_DIM).T
        val_ref[rows, :] = span_block(x_ref, kb * group, group, 2 * HEAD_DIM, 3 * HEAD_DIM).T
    dk_ref[...] = jnp.zeros_like(dk_ref)
    dv_ref[...] = jnp.zeros_like(dv_ref)
    for qb in range(blocks):
        q_t = span_block(x_ref, qb * group, group, 0, HEAD_DIM)
        do_t = span_block(do_ref, qb * group, group, 0, HEAD_DIM)
        o_t = span_block(o_ref, qb * group, group, 0, HEAD_DIM)
        delta = jnp.sum(do_t.astype(F32) * o_t.astype(F32), axis=0, keepdims=True)
        lse = lse_ref[0, :, qb * block : (qb + 1) * block]

        def step(kb, dq, masked=True):
            rows = pl.ds(pl.multiple_of(kb * block, block) if masked else kb * block, block)
            scores = dot(key_ref[rows, :], q_t, 1, 0) * coef
            if masked:
                scores = jnp.where(allowed_mask(kb, qb, block, prefix), scores, MASKED)
            probs = jnp.exp2(scores - lse)
            grad_probs = dot(val_ref[rows, :], do_t, 1, 0)
            grad_scores = (probs * (grad_probs - delta)).astype(BF16)
            dv_ref[kb] += dot(do_t, probs.astype(BF16), 1, 1)
            dk_ref[kb] += dot(q_t, grad_scores, 1, 1)
            k_t = span_block(x_ref, kb * group, group, HEAD_DIM, 2 * HEAD_DIM)
            return dq + dot(k_t, grad_scores, 1, 0)

        dq = jnp.zeros((HEAD_DIM, block), F32)
        for kb in range(qb):
            dq = step(kb, dq, False)
        dq = lax.fori_loop(qb, key_count(qb, block, prefix, blocks), step, dq)
        dq = (dq * scale).astype(BF16)
        for i in range(group):
            dx_ref[qb * group + i, 0, :HEAD_DIM, :] = dq[:, i * span_len : (i + 1) * span_len]
    for kb in range(blocks):
        dk = (dk_ref[kb] * scale).astype(BF16)
        dv = dv_ref[kb].astype(BF16)
        for i in range(group):
            cols = slice(i * span_len, (i + 1) * span_len)
            dx_ref[kb * group + i, 0, HEAD_DIM : 2 * HEAD_DIM, :] = dk[:, cols]
            dx_ref[kb * group + i, 0, 2 * HEAD_DIM :, :] = dv[:, cols]


def pair_spec(shape, first=0):
    return pl.BlockSpec((shape[0], 1) + shape[2:], lambda p, pre: (0, first + p, 0, 0))


def lse_spec(tokens):
    return pl.BlockSpec((1, 1, tokens), lambda p, pre: (p, 0, 0))


def attend_forward(prefix, packed):
    spans, _, _, span_len = packed.shape
    pairs = prefix.shape[0]
    tokens = spans * span_len
    out_shape = (spans, pairs, HEAD_DIM, span_len)
    return pl.pallas_call(
        forward_kernel,
        out_shape=(
            jax.ShapeDtypeStruct(out_shape, BF16),
            jax.ShapeDtypeStruct((pairs, 1, tokens), F32),
        ),
        grid_spec=pltpu.PrefetchScalarGridSpec(
            num_scalar_prefetch=1,
            grid=(pairs,),
            in_specs=[pair_spec(packed.shape)],
            out_specs=[pair_spec(out_shape), lse_spec(tokens)],
            scratch_shapes=[pltpu.VMEM((tokens, HEAD_DIM), BF16)],
        ),
    )(prefix, packed)


def attend_back(prefix, packed, out, grad_out, lse, micro):
    spans, _, width, span_len = packed.shape
    pairs = prefix.shape[0]
    grad_shape = (spans, pairs, width, span_len)
    tokens = spans * span_len
    group, blocks = attn_blocks(spans, span_len)
    acc = pltpu.VMEM((blocks, HEAD_DIM, group * span_len), F32)
    return pl.pallas_call(
        backward_kernel,
        out_shape=jax.ShapeDtypeStruct(grad_shape, BF16),
        grid_spec=pltpu.PrefetchScalarGridSpec(
            num_scalar_prefetch=1,
            grid=(pairs,),
            in_specs=[
                pair_spec(packed.shape),
                pair_spec(out.shape),
                pair_spec(grad_out.shape, micro * pairs),
                lse_spec(tokens),
            ],
            out_specs=pair_spec(grad_shape),
            scratch_shapes=[
                pltpu.VMEM((tokens, HEAD_DIM), BF16),
                pltpu.VMEM((tokens, HEAD_DIM), BF16),
                acc,
                acc,
            ],
        ),
    )(prefix, packed, out, grad_out, lse)


def tile_of(size):
    return math.gcd(size, 256)


def whole(shape):
    return pl.BlockSpec(shape, lambda n: (0,) * len(shape), pipeline_mode=pl.Buffered(1))


def col_tile(rows, tile):
    return pl.BlockSpec((rows, tile), lambda n: (0, n))


def ffn_forward_kernel(x_ref, wg_ref, wu_ref, g_ref, u_ref, h_ref):
    x = x_ref[...]
    gate = dot(x, wg_ref[...], 1, 0)
    up = dot(x, wu_ref[...], 1, 0)
    g_ref[...] = gate
    u_ref[...] = up
    h_ref[...] = (gate * jax.nn.sigmoid(gate) * up).astype(BF16)


def ffn_forward(rows, w_gate, w_up):
    count, width = rows.shape
    units = w_gate.shape[1]
    tile = tile_of(units)
    return pl.pallas_call(
        ffn_forward_kernel,
        grid=(units // tile,),
        in_specs=[whole(rows.shape), col_tile(width, tile), col_tile(width, tile)],
        out_specs=[col_tile(count, tile)] * 3,
        out_shape=[
            jax.ShapeDtypeStruct((count, units), F32),
            jax.ShapeDtypeStruct((count, units), F32),
            jax.ShapeDtypeStruct((count, units), BF16),
        ],
    )(rows, w_gate, w_up)


def ffn_back_kernel(dy_ref, wd_ref, g_ref, u_ref, dg_ref, du_ref):
    grad_hidden = dot(dy_ref[...], wd_ref[...], 1, 0)
    gate = g_ref[...]
    sig = jax.nn.sigmoid(gate)
    slope = sig * (1.0 + gate * (1.0 - sig))
    dg_ref[...] = (grad_hidden * u_ref[...] * slope).astype(BF16)
    du_ref[...] = (grad_hidden * (gate * sig)).astype(BF16)


def ffn_back(grad_rows, micro, w_down, gate, up):
    count, units = gate.shape
    width = w_down.shape[0]
    tile = tile_of(units)
    return pl.pallas_call(
        ffn_back_kernel,
        grid=(units // tile,),
        in_specs=[
            pl.BlockSpec((count, width), lambda n: (micro, 0), pipeline_mode=pl.Buffered(1)),
            col_tile(width, tile),
            col_tile(count, tile),
            col_tile(count, tile),
        ],
        out_specs=[col_tile(count, tile)] * 2,
        out_shape=[jax.ShapeDtypeStruct((count, units), BF16)] * 2,
    )(grad_rows, w_down, gate, up)


def to_peers_kernel(terms, micros, *refs):
    left = [r[...] for r in refs[:terms]]
    right = [r[...] for r in refs[terms : 2 * terms]]
    outs = refs[2 * terms :]
    total = None
    for a, b in zip(left, right):
        part = dot(a, b, 1, 1)
        total = part if total is None else total + part
    size = outs[0].shape[0] // micros
    for m in range(micros):
        for k, out in enumerate(outs):
            first = (m * len(outs) + k) * size
            out[m * size : (m + 1) * size, :] = total[first : first + size].astype(out.dtype)


def to_peers(lefts, rights, micros, peers):
    count, units = lefts[0].shape
    width = rights[0].shape[0]
    tile = tile_of(width)
    terms = len(lefts)
    rows = count // peers
    return pl.pallas_call(
        functools.partial(to_peers_kernel, terms, micros),
        grid=(width // tile,),
        in_specs=[whole(left.shape) for left in lefts]
        + [pl.BlockSpec((tile, units), lambda n: (n, 0))] * terms,
        out_specs=[col_tile(rows, tile)] * peers,
        out_shape=[
            jax.ShapeDtypeStruct((rows, width), BF16 if k else F32) for k in range(peers)
        ],
    )(*lefts, *rights)


def row_tile(rows):
    return math.gcd(rows, 64)


def row_block(tile, width, first=0):
    return pl.BlockSpec((tile, width), lambda n: (first + n, 0))


def paired_store(ref, values, parts):
    size = values.shape[1] // parts
    for i, f in enumerate(paired_order(parts)):
        ref[:, i * size : (i + 1) * size] = values[:, f * size : (f + 1) * size]


def norm_rows_kernel(parts, x_ref, gain_ref, own_ref, *refs):
    blocks, (branch_ref, res_ref, normed_ref) = refs[:-3], refs[-3:]
    branch = own_ref[...]
    for ref in blocks:
        branch = branch + ref[...].astype(F32)
    res = x_ref[...].astype(F32) + branch
    unit, _ = normalize(res)
    branch_ref[...] = branch
    res_ref[...] = res
    paired_store(normed_ref, (unit * gain_ref[...]).astype(BF16), parts)


def norm_rows(inputs, micro, gain, own, blocks, parts):
    rows, width = own.shape
    tile = row_tile(rows)
    return pl.pallas_call(
        functools.partial(norm_rows_kernel, parts),
        grid=(rows // tile,),
        in_specs=[row_block(tile, width, micro * (rows // tile)), whole(gain.shape)]
        + [row_block(tile, width)] * (1 + len(blocks)),
        out_specs=[row_block(tile, width)] * 3,
        out_shape=[jax.ShapeDtypeStruct((rows, width), kind) for kind in (F32, F32, BF16)],
    )(inputs, gain, own, *blocks)


def join_kernel(near_ref, far_ref, out_ref):
    rows = near_ref.shape[0]
    out_ref[:rows, :] = near_ref[...]
    out_ref[rows:, :] = far_ref[...]


def join(near, far):
    rows, width = near.shape
    return pl.pallas_call(
        join_kernel, out_shape=jax.ShapeDtypeStruct((2 * rows, width), near.dtype)
    )(near, far)


def peer_sum_kernel(*refs):
    count = (len(refs) - 2) // 2
    for pieces, out in ((refs[:count], refs[-2]), (refs[count:-2], refs[-1])):
        total = pieces[0][...]
        for ref in pieces[1:]:
            total = total + ref[...].astype(F32)
        out[...] = total.astype(out.dtype)


def peer_sum(own, blocks):
    rows, width = own.shape[0] // 2, own.shape[1]
    tile = row_tile(rows)
    pieces = [own] + list(blocks)
    return pl.pallas_call(
        peer_sum_kernel,
        grid=(rows // tile,),
        in_specs=[
            row_block(tile, width, half * (rows // tile)) for half in range(2) for _ in pieces
        ],
        out_specs=[row_block(tile, width)] * 2,
        out_shape=[jax.ShapeDtypeStruct((rows, width), kind) for kind in (F32, BF16)],
    )(*pieces, *pieces)


def norm_grad_kernel(parts, dy_ref, gain_ref, near_ref, far_ref, res_ref, grad_ref, low_ref, sum_ref, dn_ref):
    paired_store(dn_ref, near_ref[...] + far_ref[...].astype(F32), parts)
    unit, scale = normalize(res_ref[...])
    part, gain_part = norm_back(dn_ref[...], unit, scale, gain_ref[...])
    grad = dy_ref[...].astype(F32) + part
    grad_ref[...] = grad
    low_ref[...] = grad.astype(BF16)

    @pl.when(pl.program_id(0) == 0)
    def _():
        sum_ref[...] = jnp.zeros_like(sum_ref)

    sum_ref[...] += gain_part[None]


def norm_grad(grads, micro, gain, near, far, res, parts):
    rows, width = near.shape
    tile = row_tile(rows)
    return pl.pallas_call(
        functools.partial(norm_grad_kernel, parts),
        grid=(rows // tile,),
        in_specs=[row_block(tile, width, micro * (rows // tile)), whole(gain.shape)]
        + [row_block(tile, width)] * 3,
        out_specs=[row_block(tile, width)] * 2 + [pl.BlockSpec((1, width), lambda n: (0, 0))],
        out_shape=[
            jax.ShapeDtypeStruct((rows, width), F32),
            jax.ShapeDtypeStruct((rows, width), BF16),
            jax.ShapeDtypeStruct((1, width), F32),
        ],
        scratch_shapes=[pltpu.VMEM((tile, width), F32)],
    )(grads, gain, near, far, res)


def turn(values, cos_tab, sin_tab):
    half = HEAD_DIM // 2
    first, second = values[:half], values[half:]
    return jnp.concatenate(
        [first * cos_tab - second * sin_tab, second * cos_tab + first * sin_tab], axis=0
    )


def project_kernel(labels, *refs):
    count = len(labels)
    wq_ref, wk_ref, wv_ref, cos_ref, sin_ref = refs[count : count + 5]
    outs = refs[count + 5 :]
    span = outs[0].shape[3]
    weights = jnp.concatenate([wq_ref[...], wk_ref[...], wv_ref[...]], axis=1)
    for ref, places in zip(refs, labels):
        cols_all = dot(ref[...], weights, 1, 0).T
        for i, (m, k) in enumerate(places):
            cols = cols_all[:, i * span : (i + 1) * span]
            cos_tab = cos_ref[m, :, k * span : (k + 1) * span]
            sin_tab = sin_ref[m, :, k * span : (k + 1) * span]
            for h in range(2):
                for kind in range(3):
                    first = (2 * kind + h) * HEAD_DIM
                    value = cols[first : first + HEAD_DIM]
                    if kind < 2:
                        value = turn(value, cos_tab, sin_tab)
                    outs[m][h, k, kind * HEAD_DIM : (kind + 1) * HEAD_DIM, :] = value.astype(BF16)


def project(pieces, labels, weights, cos_tab, sin_tab, span):
    micros, _, tokens = cos_tab.shape
    width = weights.shape[0]
    cols = weights.shape[1] // 3
    blocks = cols // (2 * HEAD_DIM)
    seqs = tokens // span
    out = (cols // HEAD_DIM, seqs, 3 * HEAD_DIM, span)
    return pl.pallas_call(
        functools.partial(project_kernel, labels),
        grid=(blocks,),
        in_specs=[whole(p.shape) for p in pieces]
        + [
            pl.BlockSpec((width, 2 * HEAD_DIM), lambda n, kind=kind: (0, kind * blocks + n))
            for kind in range(3)
        ]
        + [whole(cos_tab.shape)] * 2,
        out_specs=[pl.BlockSpec((2,) + out[1:], lambda n: (n, 0, 0, 0))] * micros,
        out_shape=[jax.ShapeDtypeStruct(out, BF16)] * micros,
    )(*pieces, weights, weights, weights, cos_tab, sin_tab)


def mix_out_kernel(micros, x_ref, w_ref, mix_ref, *outs):
    heads, seqs, _, span = x_ref.shape
    peers = len(outs) // micros
    own = seqs // (micros * peers)

    @pl.when(pl.program_id(0) == 0)
    def _():
        for q in range(seqs):
            mix = x_ref[:, q].reshape(heads * HEAD_DIM, span)
            mix_ref[q * span : (q + 1) * span, :] = mix.T

    total = dot(mix_ref[...], w_ref[...], 1, 1)
    size = own * span
    for i, out in enumerate(outs):
        out[...] = total[i * size : (i + 1) * size].astype(out.dtype)


def mix_out(packed, weights, micros, peers):
    _, seqs, _, span = packed.shape
    width, cols = weights.shape
    tile = tile_of(width)
    rows = seqs * span // (micros * peers)
    kinds = [BF16 if k else F32 for _ in range(micros) for k in range(peers)]
    return pl.pallas_call(
        functools.partial(mix_out_kernel, micros),
        grid=(width // tile,),
        in_specs=[whole(packed.shape), pl.BlockSpec((tile, cols), lambda n: (n, 0))],
        out_specs=[pl.BlockSpec((seqs * span, cols), lambda n: (0, 0))]
        + [col_tile(rows, tile)] * len(kinds),
        out_shape=[jax.ShapeDtypeStruct((seqs * span, cols), BF16)]
        + [jax.ShapeDtypeStruct((rows, width), kind) for kind in kinds],
    )(packed, weights)


def mix_back_kernel(*refs):
    pieces, (w_ref, out_ref) = refs[:-2], refs[-2:]
    heads, _, _, span = out_ref.shape
    q = 0
    for ref in pieces:
        cols = dot(ref[...], w_ref[...], 1, 0).T.astype(BF16)
        for i in range(ref.shape[0] // span):
            for h in range(heads):
                out_ref[h, q] = cols[
                    h * HEAD_DIM : (h + 1) * HEAD_DIM, i * span : (i + 1) * span
                ]
            q += 1


def mix_back(pieces, weights, span):
    width, cols = weights.shape
    tile = tile_of(cols)
    seqs = sum(p.shape[0] for p in pieces) // span
    heads = cols // HEAD_DIM
    return pl.pallas_call(
        mix_back_kernel,
        grid=(cols // tile,),
        in_specs=[whole(p.shape) for p in pieces] + [col_tile(width, tile)],
        out_specs=pl.BlockSpec((tile // HEAD_DIM, seqs, HEAD_DIM, span), lambda n: (n, 0, 0, 0)),
        out_shape=jax.ShapeDtypeStruct((heads, seqs, HEAD_DIM, span), BF16),
    )(*pieces, weights)


def unturn_kernel(ref, cos_ref, sin_ref, *refs):
    out_ref = refs[-1]
    heads, seqs, _, span = ref.shape
    plain = pl.program_id(0) >= 2
    for k in range(seqs):
        cos_tab = jnp.where(plain, 1.0, cos_ref[:, k * span : (k + 1) * span])
        sin_tab = jnp.where(plain, 0.0, -sin_ref[:, k * span : (k + 1) * span])
        for h in range(0, heads, 2):
            pair = jnp.concatenate(
                [turn(ref[h + i, k].astype(F32), cos_tab, sin_tab) for i in range(2)], axis=0
            )
            out_ref[k * span : (k + 1) * span, h * HEAD_DIM : (h + 2) * HEAD_DIM] = pair.T.astype(
                BF16
            )


def unturn(packed, micro, micros, cos_tab, sin_tab, into):
    heads, seqs, _, span = packed.shape
    rows = seqs * span
    extra = [] if into is None else [into]
    return pl.pallas_call(
        unturn_kernel,
        grid=(3,),
        in_specs=[pl.BlockSpec((heads, seqs, HEAD_DIM, span), lambda n: (0, 0, n, 0))]
        + [whole(cos_tab.shape)] * 2
        + [pl.BlockSpec(memory_space=pl.ANY) for _ in extra],
        out_specs=pl.BlockSpec((rows, heads * HEAD_DIM), lambda n: (micro, n)),
        out_shape=jax.ShapeDtypeStruct((micros * rows, 3 * heads * HEAD_DIM), BF16),
        input_output_aliases={3: 0} if extra else {},
    )(packed, cos_tab, sin_tab, *extra)


class HeadSplit:
    def __init__(self, n_fsdp, head_count, seqs):
        self.head_groups = math.gcd(n_fsdp, head_count)
        self.seq_groups = n_fsdp // self.head_groups
        self.heads_per = head_count // self.head_groups
        self.seqs_per = seqs // self.seq_groups

    def to_heads(self, packed):
        width, span = packed.shape[2:]
        packed = packed.reshape(
            self.head_groups, self.heads_per, -1, self.seq_groups, self.seqs_per, width, span
        ).transpose(3, 0, 2, 1, 4, 5, 6)
        packed = packed.reshape(self.seq_groups * self.head_groups, -1, width, span)
        return lax.all_to_all(packed, FSDP, split_axis=0, concat_axis=0, tiled=True)

    def to_spans(self, packed):
        width, span = packed.shape[2:]
        packed = lax.all_to_all(packed, FSDP, split_axis=0, concat_axis=0, tiled=True)
        packed = packed.reshape(
            self.seq_groups, self.head_groups, -1, self.heads_per, self.seqs_per, width, span
        ).transpose(1, 3, 2, 0, 4, 5, 6)
        return packed.reshape(self.head_groups * self.heads_per, -1, width, span)

    def pair_prefix(self, prefix, fsdp_index):
        mine = lax.dynamic_slice_in_dim(
            prefix, (fsdp_index // self.head_groups) * self.seqs_per, self.seqs_per, 0
        )
        return jnp.tile(mine, self.heads_per)


def layer(
    inputs,
    out_grads,
    prefix_len,
    positions,
    attn_gain,
    w_query,
    w_key,
    w_value,
    w_out,
    mlp_gain,
    w_gate,
    w_up,
    w_down,
):
    micro_count, seq_dev, span_len, model_width = inputs.shape
    n_tensor = lax.axis_size(TENSOR)
    n_fsdp = lax.axis_size(FSDP)
    seq_mb = seq_dev * n_tensor
    seq_len = span_len * n_fsdp
    own_rows = seq_dev * span_len
    head_cols = w_query.shape[1]
    head_count = head_cols // HEAD_DIM
    ff_cols = w_gate.shape[1]
    fsdp_index = lax.axis_index(FSDP)
    tensor_index = lax.axis_index(TENSOR)
    query_index = fsdp_index * span_len + jnp.arange(span_len, dtype=jnp.int32)
    split = HeadSplit(n_fsdp, head_count, seq_mb)
    micros = range(micro_count)

    def gather(shard):
        return lax.all_gather(shard, FSDP, axis=0, tiled=True)

    def scatter(grad):
        return lax.psum_scatter(grad, FSDP, scatter_dimension=0, tiled=True).astype(F32)

    gains = lax.all_gather(jnp.stack([attn_gain, mlp_gain]), FSDP, axis=1, tiled=True)
    gain_attn = gains[0].astype(F32)
    gain_mlp = gains[1].astype(F32)
    full_qkv = gather(jnp.concatenate([w_query, w_key, w_value], axis=1))
    full_out = gather(w_out)
    side = (fsdp_index // PAIR) % 2

    order = (
        ((tensor_index ^ jnp.arange(n_tensor, dtype=jnp.int32)) * seq_dev)[:, None]
        + jnp.arange(seq_dev, dtype=jnp.int32)
    ).reshape(-1)
    prefix_all = jnp.take(prefix_len, order, axis=1)
    own_prefix = prefix_all[:, :seq_dev]
    pos_all = jnp.take(positions, order, axis=1)
    half_dim = HEAD_DIM // 2
    ladder = jnp.arange(half_dim, dtype=F32) * (2.0 / HEAD_DIM)
    inverse = 1.0 / rope_base**ladder

    x_float = inputs.reshape(micro_count * own_rows, model_width).astype(F32)
    grad_own = out_grads.reshape(micro_count * own_rows, model_width)
    unit_attn, scale_attn = normalize(x_float)
    normed = (unit_attn * gain_attn).astype(BF16)
    normed_pieces = spread_pieces(normed, False)
    cos_tab, sin_tab, pair_prefix = [], [], []
    for m in micros:
        angles = inverse[:, None] * pos_all[m].astype(F32).reshape(-1)[None, :]
        cos_tab.append(jnp.cos(angles))
        sin_tab.append(jnp.sin(angles))
        pair_prefix.append(split.pair_prefix(prefix_all[m], fsdp_index))
    cos_all = jnp.stack(cos_tab)
    sin_all = jnp.stack(sin_tab)
    half_cols = ff_cols // 2
    ffn_near = half_of([w_gate, w_up, w_down], side)
    ffn_far = half_of([w_gate, w_up, w_down], 1 - side)
    grad_pair = pair_join(after(paired(grad_own), full_qkv), micro_count)
    labels, taken = [], [0] * n_tensor
    spans_of = [(m, r) for m in micros for r in range(seq_dev)]
    peer = 0
    for piece in normed_pieces:
        size = piece.shape[0] // span_len
        start = taken[peer]
        labels.append(
            tuple((m, peer * seq_dev + r) for m, r in spans_of[start : start + size])
        )
        taken[peer] += size
        if taken[peer] == len(spans_of):
            peer += 1
    stack = project(normed_pieces, tuple(labels), full_qkv, cos_all, sin_all, span_len)
    packed = []
    for m in micros:
        packed.append(split.to_heads(stack[m]))
    normed_rows = gather_rows(whole_blocks(after(normed_pieces, stack)), micro_count)
    grad_pair = after(grad_pair, stack)
    grad_blocks = spread(grad_pair)
    ffn_other = swap(after(ffn_far, packed[-1]), FSDP, PAIR)
    attn_out, attn_lse = [None] * micro_count, [None] * micro_count
    done = full_out
    for m in reversed(micros):
        attn_out[m], attn_lse[m] = attend_forward(pair_prefix[m], after(packed[m], done))
        done = attn_lse[m]
    mix_packed = split.to_spans(jnp.concatenate(attn_out, axis=1))
    ffn_other = after(ffn_other, attn_lse)
    shards = [
        own_half(
            side,
            ffn_near[:, i * half_cols : (i + 1) * half_cols],
            ffn_other[:, i * half_cols : (i + 1) * half_cols],
        )
        for i in range(3)
    ]
    full_gate = gather_half(after(shards[0], mix_packed))
    branch, resid, others, normed_mlp, joined = [], [], [], [], []
    flat_inputs = inputs.reshape(micro_count * own_rows, model_width)
    gain_rows = gain_mlp[None]
    mix_rows, *parts = mix_out(mix_packed, full_out, micro_count, n_tensor)
    for m in micros:
        own, *sent = parts[m * n_tensor : (m + 1) * n_tensor]
        blocks = peer_swaps([own] + sent)
        if m:
            blocks = after(blocks, normed_mlp)
        part, res, normed = norm_rows(flat_inputs, m, gain_rows, own, blocks, n_fsdp)
        branch.append(part)
        resid.append(res)
        normed_mlp.append(normed)
        others.append(swap(normed, FSDP, PAIR))
    for m in micros:
        other = after(others[m], joined) if m else others[m]
        joined.append(join(normed_mlp[m], other))
    full_up = gather_half(after(shards[1], joined))
    full_down = gather_half(shards[2])
    mlp_rows, first = [], None
    for m in micros:
        blocks = spread(joined[m] if first is None else after(joined[m], first), False)
        if first is None:
            first = blocks[1:3]
            grad_rows = gather_rows(after(grad_blocks, first), micro_count)
        mlp_rows.append(gather_rows(blocks, 1))

    hidden, gate_val, up_val = [], [], []
    for m in micros:
        gate, up, hid = ffn_forward(mlp_rows[m], full_gate, full_up)
        gate_val.append(gate)
        up_val.append(up)
        hidden.append(hid)
    hidden = jnp.concatenate(hidden, axis=0)
    down_grad = dot(grad_rows, hidden, 0, 0).astype(BF16)
    full_down = after(full_down, down_grad)
    part_down = scatter_half(down_grad)
    grad_gu, normed_part = [], []
    for m in micros:
        gate_in = after(gate_val[m], normed_part) if m else gate_val[m]
        gate, up = ffn_back(grad_rows, m, full_down, gate_in, up_val[m])
        grad_gu.append(jnp.concatenate([gate, up], axis=1))
        normed_part.append(to_peers([gate, up], [full_gate, full_up], 1, n_tensor))
    all_mlp_rows = jnp.concatenate(after(mlp_rows, normed_part), axis=0)
    gu_grad = dot(all_mlp_rows, jnp.concatenate(grad_gu, axis=0), 0, 0).astype(BF16)
    part_gu = scatter_half(after(gu_grad, part_down))
    grad_resid, branch_rows, near_far, mlp_gain_parts = [], [], [], []
    for m in micros:
        blocks = peer_swaps(normed_part[m])
        blocks = after(blocks, near_far[-1][0] if m else gu_grad)
        near, far = peer_sum(normed_part[m][0], blocks)
        near_far.append((near, swap(far, FSDP, PAIR)))
    low = None
    for m in micros:
        near, far = near_far[m]
        if m:
            far = after(far, low)
        grad_res, low, gain_part = norm_grad(grad_own, m, gain_rows, near, far, resid[m], n_fsdp)
        mlp_gain_parts.append(gain_part[0])
        grad_resid.append(grad_res)
        branch_rows += spread(low)
    mlp_gain_sum = sum(mlp_gain_parts)
    grad_mix = mix_back(branch_rows, full_out, span_len)
    grad_out_all = split.to_heads(grad_mix)
    out_grad = dot(
        jnp.concatenate(after(branch_rows, grad_mix), axis=0), mix_rows, 0, 0
    ).astype(BF16)

    mlp_blocks = to_peers([after(hidden, out_grad)], [full_down], micro_count, n_tensor)
    own_out = scatter(after(out_grad, part_gu, mlp_blocks))

    grad_raw = []
    packed_grads = []
    for m in micros:
        grad_out = after(grad_out_all, mlp_blocks, part_down if m else own_out)
        packed_grad = attend_back(pair_prefix[m], packed[m], attn_out[m], grad_out, attn_lse[m], m)
        packed_grads.append(packed_grad)
        grad_raw.append(split.to_spans(packed_grad))

    mlp_part = collect(mlp_blocks, token=packed_grads[0])
    near = [mlp_part[2 * m * own_rows : (2 * m + 1) * own_rows] for m in micros]
    far = [mlp_part[(2 * m + 1) * own_rows : (2 * m + 2) * own_rows] for m in micros]
    far = swap(jnp.concatenate(far, axis=0).astype(BF16), FSDP, PAIR)
    grad_qkv = None
    for m in reversed(micros):
        grad_qkv = unturn(grad_raw[m], m, micro_count, cos_all[m], sin_all[m], grad_qkv)
    qkv_grad = dot(normed_rows, grad_qkv, 0, 0).astype(BF16)
    own_gate, own_up = settle_half(part_gu, side, 2, qkv_grad)
    (own_down,) = settle_half(part_down, side, 1, qkv_grad)
    part = to_peers([after(grad_qkv, qkv_grad)], [full_qkv], micro_count, n_tensor)
    grad_normed = collect(part, False)
    far = after(far, part).astype(F32)
    mlp_out = paired(jnp.concatenate(near, axis=0) + far)
    branch = jnp.concatenate(branch, axis=0)
    result = jnp.concatenate(resid, axis=0) + mlp_out
    output = result.astype(BF16).reshape(inputs.shape)
    valid = (query_index[None, None, :] >= own_prefix[:, :, None]).reshape(-1)
    stats = jnp.stack(
        [
            jnp.sum(
                jnp.where(valid, jnp.sum(part * part, axis=1), 0.0).reshape(
                    micro_count, seq_dev, span_len
                ),
                axis=2,
            )
            for part in (result, branch, mlp_out)
        ],
        axis=-1,
    )

    own_qkv = scatter(qkv_grad)
    part, attn_gain_sum = norm_back(grad_normed, unit_attn, scale_attn, gain_attn)
    input_grad = (jnp.concatenate(grad_resid, axis=0) + part).reshape(inputs.shape)

    stat_sum = tree_sum(stats, FSDP)
    gain_sum = tree_sum(tree_sum(jnp.stack([attn_gain_sum, mlp_gain_sum]), TENSOR), FSDP)
    row_share = model_width // n_fsdp
    own_gain = lax.dynamic_slice_in_dim(gain_sum, fsdp_index * row_share, row_share, 1)
    counts = ((seq_len - own_prefix) * model_width).astype(F32)
    rms_stats = jnp.sqrt(stat_sum / counts[..., None] + stat_eps)
    return (
        output,
        input_grad,
        own_gain[0],
        own_qkv[:, :head_cols],
        own_qkv[:, head_cols : 2 * head_cols],
        own_qkv[:, 2 * head_cols :],
        own_out,
        own_gain[1],
        own_gate,
        own_up,
        own_down,
        rms_stats,
    )


def solution(mesh):
    in_specs = (
        P(None, TENSOR, FSDP, None),
        P(None, TENSOR, FSDP, None),
        P(),
        P(None, None, FSDP),
        P(FSDP),
        P(FSDP, TENSOR),
        P(FSDP, TENSOR),
        P(FSDP, TENSOR),
        P(FSDP, TENSOR),
        P(FSDP),
        P(FSDP, TENSOR),
        P(FSDP, TENSOR),
        P(FSDP, TENSOR),
    )
    out_specs = (
        P(None, TENSOR, FSDP, None),
        P(None, TENSOR, FSDP, None),
        P(FSDP),
        P(FSDP, TENSOR),
        P(FSDP, TENSOR),
        P(FSDP, TENSOR),
        P(FSDP, TENSOR),
        P(FSDP),
        P(FSDP, TENSOR),
        P(FSDP, TENSOR),
        P(FSDP, TENSOR),
        P(None, TENSOR, None),
    )
    return jax.shard_map(layer, mesh=mesh, in_specs=in_specs, out_specs=out_specs, check_vma=False)
```

```python
import functools
import math

import jax
import jax.numpy as jnp
from jax import lax
from jax.experimental import pallas as pl
from jax.experimental.pallas import tpu as pltpu
from jax.sharding import PartitionSpec as P

HEAD_DIM = 64

rope_base = 130000.0
norm_eps = 1e-05
stat_eps = 1e-06
LOG2E = math.log2(math.e)
MASKED = -1e30
PAIR = 2
FSDP, TENSOR = "fsdp", "tensor"
BF16 = jnp.bfloat16
F32 = jnp.float32


def dot(left, right, left_dim, right_dim):
    return lax.dot_general(
        left, right, (((left_dim,), (right_dim,)), ((), ())), preferred_element_type=F32
    )


def normalize(values):
    row_scale = lax.rsqrt(jnp.mean(values * values, axis=-1, keepdims=True) + norm_eps)
    return (values * row_scale, row_scale)


def norm_back(grad_in, unit_rows, row_scale, gain):
    scaled = grad_in * gain
    inner_mean = jnp.mean(scaled * unit_rows, axis=-1, keepdims=True)
    return (
        row_scale * (scaled - unit_rows * inner_mean),
        jnp.sum(grad_in * unit_rows, axis=tuple(range(grad_in.ndim - 1))),
    )


def swap(value, axis, distance):
    count = lax.axis_size(axis)
    return lax.ppermute(value, axis, [(a, a ^ distance) for a in range(count)])


def after(value, *others):
    return lax.optimization_barrier((value, others))[0]


def spread_pieces(value, direct=True):
    count = lax.axis_size(TENSOR)
    if direct or count != 4:
        return [value] + [swap(value, TENSOR, k) for k in range(1, count)]
    half = value.shape[0] // 2
    one = swap(value, TENSOR, 1)
    two = swap(value, TENSOR, 2)
    low = swap(two[:half], TENSOR, 1)
    high = swap(one[half:], TENSOR, 2)
    return [value, one, two, low, high]


def whole_blocks(pieces):
    rows = pieces[0].shape[0]
    far = [p for p in pieces if p.shape[0] < rows]
    return [p for p in pieces if p.shape[0] == rows] + (
        [jnp.concatenate(far, axis=0)] if far else []
    )


def spread(value, direct=True):
    return whole_blocks(spread_pieces(value, direct))


def collect(parts, direct=True, token=None):
    count = lax.axis_size(TENSOR)
    if direct or count != 4:
        blocks = [swap(parts[k].astype(BF16), TENSOR, k) for k in range(1, count)]
        if token is not None:
            blocks = after(blocks, token)
        total = parts[0]
        for block in blocks:
            total = total + block.astype(F32)
        return total
    half = parts[0].shape[0] // 2
    far = parts[3].astype(BF16)
    low = swap(far[:half], TENSOR, 1).astype(F32)
    high = swap(far[half:], TENSOR, 2).astype(F32)
    one = jnp.concatenate([parts[1][:half], parts[1][half:] + high], axis=0)
    two = jnp.concatenate([parts[2][:half] + low, parts[2][half:]], axis=0)
    one = swap(one.astype(BF16), TENSOR, 1).astype(F32)
    two = swap(two.astype(BF16), TENSOR, 2).astype(F32)
    return parts[0] + one + two


def peer_swaps(parts):
    return [swap(part, TENSOR, k) for k, part in enumerate(parts) if k]


def pair_join(value, micros):
    other = swap(value, FSDP, PAIR)
    size = value.shape[0] // micros
    parts = [v[m * size : (m + 1) * size] for m in range(micros) for v in (value, other)]
    return jnp.concatenate(parts, axis=0)


def gather_rows(blocks, micros):
    size = blocks[0].shape[0] // micros
    return jnp.concatenate(
        [b[m * size : (m + 1) * size] for m in range(micros) for b in blocks], axis=0
    )


def paired_order(count):
    return [(f & ~3) | ((f & 1) << 1) | ((f >> 1) & 1) for f in range(count)]


def paired(values):
    count = lax.axis_size(FSDP)
    size = values.shape[-1] // count
    order = paired_order(count)
    parts = [lax.slice_in_dim(values, f * size, (f + 1) * size, axis=-1) for f in order]
    return jnp.concatenate(parts, axis=-1)


def pair_groups():
    count = lax.axis_size(FSDP)
    return [[f for f in range(count) if bool(f & PAIR) == side] for side in (False, True)]


def half_of(shards, side):
    half = shards[0].shape[1] // 2
    return jnp.concatenate(
        [lax.dynamic_slice_in_dim(s, side * half, half, 1) for s in shards], axis=1
    )


def order_pair(side, mine, other):
    return jnp.where(side == 0, mine, other), jnp.where(side == 0, other, mine)


def own_half(side, mine, other):
    return jnp.concatenate(order_pair(side, mine, other), axis=0)


def gather_half(shard):
    return lax.all_gather(
        shard,
        FSDP,
        axis=0,
        tiled=True,
        axis_index_groups=pair_groups(),
    )


def scatter_half(grad):
    return lax.psum_scatter(
        grad, FSDP, scatter_dimension=0, tiled=True, axis_index_groups=pair_groups()
    )


def settle_half(part, side, pieces, token):
    rows = part.shape[0] // 2
    mine = lax.dynamic_slice_in_dim(part, side * rows, rows, 0)
    other = swap(lax.dynamic_slice_in_dim(part, (1 - side) * rows, rows, 0), FSDP, PAIR)
    low, high = order_pair(side, mine, after(other, token))
    half = part.shape[1] // pieces
    return [
        jnp.concatenate(
            [low[:, i * half : (i + 1) * half], high[:, i * half : (i + 1) * half]], axis=1
        ).astype(F32)
        for i in range(pieces)
    ]


def span_block(ref, first, count, lo, hi):
    return jnp.concatenate([ref[first + i, 0, lo:hi, :] for i in range(count)], axis=1)


def attn_blocks(spans, span_len):
    group = max(1, min(spans, 256 // span_len))
    while spans % group:
        group -= 1
    return group, spans // group


def key_count(q_block, block, prefix, blocks):
    return jnp.minimum(jnp.maximum(q_block + 1, (prefix + block - 1) // block), blocks)


def allowed_mask(k_block, q_block, block, prefix):
    key_id = k_block * block + lax.broadcasted_iota(jnp.int32, (block, block), 0)
    query_id = q_block * block + lax.broadcasted_iota(jnp.int32, (block, block), 1)
    return (key_id <= query_id) | (key_id < prefix)


def forward_kernel(prefix_ref, x_ref, out_ref, lse_ref, key_ref):
    spans, _, _, span_len = x_ref.shape
    group, blocks = attn_blocks(spans, span_len)
    block = group * span_len
    prefix = prefix_ref[pl.program_id(0)]
    coef = HEAD_DIM**-0.5 * LOG2E
    for kb in range(blocks):
        key_ref[pl.ds(kb * block, block), :] = span_block(
            x_ref, kb * group, group, HEAD_DIM, 2 * HEAD_DIM
        ).T
    for qb in range(blocks):
        q_t = span_block(x_ref, qb * group, group, 0, HEAD_DIM)

        def step(kb, carry, masked=True):
            top, total, acc = carry
            first = pl.multiple_of(kb * block, block) if masked else kb * block
            keys = key_ref[pl.ds(first, block), :]
            scores = dot(keys, q_t, 1, 0) * coef
            if masked:
                scores = jnp.where(allowed_mask(kb, qb, block, prefix), scores, MASKED)
            new_top = jnp.maximum(top, jnp.max(scores, axis=0, keepdims=True))
            probs = jnp.exp2(scores - new_top)
            shrink = jnp.exp2(top - new_top)
            total = shrink * total + jnp.sum(probs, axis=0, keepdims=True)
            v_t = span_block(x_ref, kb * group, group, 2 * HEAD_DIM, 3 * HEAD_DIM)
            acc = shrink * acc + dot(v_t, probs.astype(BF16), 1, 0)
            return new_top, total, acc

        carry = (
            jnp.full((1, block), MASKED, F32),
            jnp.zeros((1, block), F32),
            jnp.zeros((HEAD_DIM, block), F32),
        )
        for kb in range(qb):
            carry = step(kb, carry, False)
        top, total, acc = lax.fori_loop(
            qb, key_count(qb, block, prefix, blocks), step, carry
        )
        out = (acc / total).astype(BF16)
        for i in range(group):
            out_ref[qb * group + i, 0] = out[:, i * span_len : (i + 1) * span_len]
        lse_ref[0, :, qb * block : (qb + 1) * block] = top + jnp.log2(total)


def backward_kernel(
    prefix_ref, x_ref, o_ref, do_ref, lse_ref, dx_ref, key_ref, val_ref, dk_ref, dv_ref
):
    spans, _, _, span_len = x_ref.shape
    group, blocks = attn_blocks(spans, span_len)
    block = group * span_len
    prefix = prefix_ref[pl.program_id(0)]
    scale = HEAD_DIM**-0.5
    coef = scale * LOG2E
    for kb in range(blocks):
        rows = pl.ds(kb * block, block)
        key_ref[rows, :] = span_block(x_ref, kb * group, group, HEAD_DIM, 2 * HEAD_DIM).T
        val_ref[rows, :] = span_block(x_ref, kb * group, group, 2 * HEAD_DIM, 3 * HEAD_DIM).T
    dk_ref[...] = jnp.zeros_like(dk_ref)
    dv_ref[...] = jnp.zeros_like(dv_ref)
    for qb in range(blocks):
        q_t = span_block(x_ref, qb * group, group, 0, HEAD_DIM)
        do_t = span_block(do_ref, qb * group, group, 0, HEAD_DIM)
        o_t = span_block(o_ref, qb * group, group, 0, HEAD_DIM)
        delta = jnp.sum(do_t.astype(F32) * o_t.astype(F32), axis=0, keepdims=True)
        lse = lse_ref[0, :, qb * block : (qb + 1) * block]

        def step(kb, dq, masked=True):
            rows = pl.ds(pl.multiple_of(kb * block, block) if masked else kb * block, block)
            scores = dot(key_ref[rows, :], q_t, 1, 0) * coef
            if masked:
                scores = jnp.where(allowed_mask(kb, qb, block, prefix), scores, MASKED)
            probs = jnp.exp2(scores - lse)
            grad_probs = dot(val_ref[rows, :], do_t, 1, 0)
            grad_scores = (probs * (grad_probs - delta)).astype(BF16)
            dv_ref[kb] += dot(do_t, probs.astype(BF16), 1, 1)
            dk_ref[kb] += dot(q_t, grad_scores, 1, 1)
            k_t = span_block(x_ref, kb * group, group, HEAD_DIM, 2 * HEAD_DIM)
            return dq + dot(k_t, grad_scores, 1, 0)

        dq = jnp.zeros((HEAD_DIM, block), F32)
        for kb in range(qb):
            dq = step(kb, dq, False)
        dq = lax.fori_loop(qb, key_count(qb, block, prefix, blocks), step, dq)
        dq = (dq * scale).astype(BF16)
        for i in range(group):
            dx_ref[qb * group + i, 0, :HEAD_DIM, :] = dq[:, i * span_len : (i + 1) * span_len]
    for kb in range(blocks):
        dk = (dk_ref[kb] * scale).astype(BF16)
        dv = dv_ref[kb].astype(BF16)
        for i in range(group):
            cols = slice(i * span_len, (i + 1) * span_len)
            dx_ref[kb * group + i, 0, HEAD_DIM : 2 * HEAD_DIM, :] = dk[:, cols]
            dx_ref[kb * group + i, 0, 2 * HEAD_DIM :, :] = dv[:, cols]


def pair_spec(shape, first=0):
    return pl.BlockSpec((shape[0], 1) + shape[2:], lambda p, pre: (0, first + p, 0, 0))


def lse_spec(tokens):
    return pl.BlockSpec((1, 1, tokens), lambda p, pre: (p, 0, 0))


def attend_forward(prefix, packed):
    spans, _, _, span_len = packed.shape
    pairs = prefix.shape[0]
    tokens = spans * span_len
    out_shape = (spans, pairs, HEAD_DIM, span_len)
    return pl.pallas_call(
        forward_kernel,
        out_shape=(
            jax.ShapeDtypeStruct(out_shape, BF16),
            jax.ShapeDtypeStruct((pairs, 1, tokens), F32),
        ),
        grid_spec=pltpu.PrefetchScalarGridSpec(
            num_scalar_prefetch=1,
            grid=(pairs,),
            in_specs=[pair_spec(packed.shape)],
            out_specs=[pair_spec(out_shape), lse_spec(tokens)],
            scratch_shapes=[pltpu.VMEM((tokens, HEAD_DIM), BF16)],
        ),
    )(prefix, packed)


def attend_back(prefix, packed, out, grad_out, lse, micro):
    spans, _, width, span_len = packed.shape
    pairs = prefix.shape[0]
    grad_shape = (spans, pairs, width, span_len)
    tokens = spans * span_len
    group, blocks = attn_blocks(spans, span_len)
    acc = pltpu.VMEM((blocks, HEAD_DIM, group * span_len), F32)
    return pl.pallas_call(
        backward_kernel,
        out_shape=jax.ShapeDtypeStruct(grad_shape, BF16),
        grid_spec=pltpu.PrefetchScalarGridSpec(
            num_scalar_prefetch=1,
            grid=(pairs,),
            in_specs=[
                pair_spec(packed.shape),
                pair_spec(out.shape),
                pair_spec(grad_out.shape, micro * pairs),
                lse_spec(tokens),
            ],
            out_specs=pair_spec(grad_shape),
            scratch_shapes=[
                pltpu.VMEM((tokens, HEAD_DIM), BF16),
                pltpu.VMEM((tokens, HEAD_DIM), BF16),
                acc,
                acc,
            ],
        ),
    )(prefix, packed, out, grad_out, lse)


def tile_of(size):
    return math.gcd(size, 256)


def whole(shape):
    return pl.BlockSpec(shape, lambda n: (0,) * len(shape), pipeline_mode=pl.Buffered(1))


def col_tile(rows, tile):
    return pl.BlockSpec((rows, tile), lambda n: (0, n))


def ffn_forward_kernel(x_ref, wg_ref, wu_ref, g_ref, u_ref, h_ref):
    x = x_ref[...]
    gate = dot(x, wg_ref[...], 1, 0)
    up = dot(x, wu_ref[...], 1, 0)
    g_ref[...] = gate
    u_ref[...] = up
    h_ref[...] = (gate * jax.nn.sigmoid(gate) * up).astype(BF16)


def ffn_forward(rows, w_gate, w_up):
    count, width = rows.shape
    units = w_gate.shape[1]
    tile = tile_of(units)
    return pl.pallas_call(
        ffn_forward_kernel,
        grid=(units // tile,),
        in_specs=[whole(rows.shape), col_tile(width, tile), col_tile(width, tile)],
        out_specs=[col_tile(count, tile)] * 3,
        out_shape=[
            jax.ShapeDtypeStruct((count, units), F32),
            jax.ShapeDtypeStruct((count, units), F32),
            jax.ShapeDtypeStruct((count, units), BF16),
        ],
    )(rows, w_gate, w_up)


def ffn_back_kernel(dy_ref, wd_ref, g_ref, u_ref, dg_ref, du_ref):
    grad_hidden = dot(dy_ref[...], wd_ref[...], 1, 0)
    gate = g_ref[...]
    sig = jax.nn.sigmoid(gate)
    slope = sig * (1.0 + gate * (1.0 - sig))
    dg_ref[...] = (grad_hidden * u_ref[...] * slope).astype(BF16)
    du_ref[...] = (grad_hidden * (gate * sig)).astype(BF16)


def ffn_back(grad_rows, micro, w_down, gate, up):
    count, units = gate.shape
    width = w_down.shape[0]
    tile = tile_of(units)
    return pl.pallas_call(
        ffn_back_kernel,
        grid=(units // tile,),
        in_specs=[
            pl.BlockSpec((count, width), lambda n: (micro, 0), pipeline_mode=pl.Buffered(1)),
            col_tile(width, tile),
            col_tile(count, tile),
            col_tile(count, tile),
        ],
        out_specs=[col_tile(count, tile)] * 2,
        out_shape=[jax.ShapeDtypeStruct((count, units), BF16)] * 2,
    )(grad_rows, w_down, gate, up)


def to_peers_kernel(terms, micros, *refs):
    left = [r[...] for r in refs[:terms]]
    right = [r[...] for r in refs[terms : 2 * terms]]
    outs = refs[2 * terms :]
    total = None
    for a, b in zip(left, right):
        part = dot(a, b, 1, 1)
        total = part if total is None else total + part
    size = outs[0].shape[0] // micros
    for m in range(micros):
        for k, out in enumerate(outs):
            first = (m * len(outs) + k) * size
            out[m * size : (m + 1) * size, :] = total[first : first + size].astype(out.dtype)


def to_peers(lefts, rights, micros, peers):
    count, units = lefts[0].shape
    width = rights[0].shape[0]
    tile = tile_of(width)
    terms = len(lefts)
    rows = count // peers
    return pl.pallas_call(
        functools.partial(to_peers_kernel, terms, micros),
        grid=(width // tile,),
        in_specs=[whole(left.shape) for left in lefts]
        + [pl.BlockSpec((tile, units), lambda n: (n, 0))] * terms,
        out_specs=[col_tile(rows, tile)] * peers,
        out_shape=[
            jax.ShapeDtypeStruct((rows, width), BF16 if k else F32) for k in range(peers)
        ],
    )(*lefts, *rights)


def row_tile(rows):
    return math.gcd(rows, 64)


def row_block(tile, width, first=0):
    return pl.BlockSpec((tile, width), lambda n: (first + n, 0))


def paired_store(ref, values, parts):
    size = values.shape[1] // parts
    for i, f in enumerate(paired_order(parts)):
        ref[:, i * size : (i + 1) * size] = values[:, f * size : (f + 1) * size]


def norm_rows_kernel(parts, x_ref, gain_ref, own_ref, *refs):
    blocks, (branch_ref, res_ref, normed_ref) = refs[:-3], refs[-3:]
    branch = own_ref[...]
    for ref in blocks:
        branch = branch + ref[...].astype(F32)
    res = x_ref[...].astype(F32) + branch
    unit, _ = normalize(res)
    branch_ref[...] = branch
    res_ref[...] = res
    paired_store(normed_ref, (unit * gain_ref[...]).astype(BF16), parts)


def norm_rows(inputs, micro, gain, own, blocks, parts):
    rows, width = own.shape
    tile = row_tile(rows)
    return pl.pallas_call(
        functools.partial(norm_rows_kernel, parts),
        grid=(rows // tile,),
        in_specs=[row_block(tile, width, micro * (rows // tile)), whole(gain.shape)]
        + [row_block(tile, width)] * (1 + len(blocks)),
        out_specs=[row_block(tile, width)] * 3,
        out_shape=[jax.ShapeDtypeStruct((rows, width), kind) for kind in (F32, F32, BF16)],
    )(inputs, gain, own, *blocks)


def join_kernel(near_ref, far_ref, out_ref):
    rows = near_ref.shape[0]
    out_ref[:rows, :] = near_ref[...]
    out_ref[rows:, :] = far_ref[...]


def join(near, far):
    rows, width = near.shape
    return pl.pallas_call(
        join_kernel, out_shape=jax.ShapeDtypeStruct((2 * rows, width), near.dtype)
    )(near, far)


def peer_sum_kernel(*refs):
    count = (len(refs) - 2) // 2
    for pieces, out in ((refs[:count], refs[-2]), (refs[count:-2], refs[-1])):
        total = pieces[0][...]
        for ref in pieces[1:]:
            total = total + ref[...].astype(F32)
        out[...] = total.astype(out.dtype)


def peer_sum(own, blocks):
    rows, width = own.shape[0] // 2, own.shape[1]
    tile = row_tile(rows)
    pieces = [own] + list(blocks)
    return pl.pallas_call(
        peer_sum_kernel,
        grid=(rows // tile,),
        in_specs=[
            row_block(tile, width, half * (rows // tile)) for half in range(2) for _ in pieces
        ],
        out_specs=[row_block(tile, width)] * 2,
        out_shape=[jax.ShapeDtypeStruct((rows, width), kind) for kind in (F32, BF16)],
    )(*pieces, *pieces)


def norm_grad_kernel(parts, dy_ref, gain_ref, near_ref, far_ref, res_ref, grad_ref, low_ref, sum_ref, dn_ref):
    paired_store(dn_ref, near_ref[...] + far_ref[...].astype(F32), parts)
    unit, scale = normalize(res_ref[...])
    part, gain_part = norm_back(dn_ref[...], unit, scale, gain_ref[...])
    grad = dy_ref[...].astype(F32) + part
    grad_ref[...] = grad
    low_ref[...] = grad.astype(BF16)

    @pl.when(pl.program_id(0) == 0)
    def _():
        sum_ref[...] = jnp.zeros_like(sum_ref)

    sum_ref[...] += gain_part[None]


def norm_grad(grads, micro, gain, near, far, res, parts):
    rows, width = near.shape
    tile = row_tile(rows)
    return pl.pallas_call(
        functools.partial(norm_grad_kernel, parts),
        grid=(rows // tile,),
        in_specs=[row_block(tile, width, micro * (rows // tile)), whole(gain.shape)]
        + [row_block(tile, width)] * 3,
        out_specs=[row_block(tile, width)] * 2 + [pl.BlockSpec((1, width), lambda n: (0, 0))],
        out_shape=[
            jax.ShapeDtypeStruct((rows, width), F32),
            jax.ShapeDtypeStruct((rows, width), BF16),
            jax.ShapeDtypeStruct((1, width), F32),
        ],
        scratch_shapes=[pltpu.VMEM((tile, width), F32)],
    )(grads, gain, near, far, res)


def turn(values, cos_tab, sin_tab):
    half = HEAD_DIM // 2
    first, second = values[:half], values[half:]
    return jnp.concatenate(
        [first * cos_tab - second * sin_tab, second * cos_tab + first * sin_tab], axis=0
    )


def project_kernel(labels, *refs):
    count = len(labels)
    wq_ref, wk_ref, wv_ref, cos_ref, sin_ref = refs[count : count + 5]
    outs = refs[count + 5 :]
    span = outs[0].shape[3]
    weights = jnp.concatenate([wq_ref[...], wk_ref[...], wv_ref[...]], axis=1)
    for ref, places in zip(refs, labels):
        cols_all = dot(ref[...], weights, 1, 0).T
        for i, (m, k) in enumerate(places):
            cols = cols_all[:, i * span : (i + 1) * span]
            cos_tab = cos_ref[m, :, k * span : (k + 1) * span]
            sin_tab = sin_ref[m, :, k * span : (k + 1) * span]
            for h in range(2):
                for kind in range(3):
                    first = (2 * kind + h) * HEAD_DIM
                    value = cols[first : first + HEAD_DIM]
                    if kind < 2:
                        value = turn(value, cos_tab, sin_tab)
                    outs[m][h, k, kind * HEAD_DIM : (kind + 1) * HEAD_DIM, :] = value.astype(BF16)


def project(pieces, labels, weights, cos_tab, sin_tab, span):
    micros, _, tokens = cos_tab.shape
    width = weights.shape[0]
    cols = weights.shape[1] // 3
    blocks = cols // (2 * HEAD_DIM)
    seqs = tokens // span
    out = (cols // HEAD_DIM, seqs, 3 * HEAD_DIM, span)
    return pl.pallas_call(
        functools.partial(project_kernel, labels),
        grid=(blocks,),
        in_specs=[whole(p.shape) for p in pieces]
        + [
            pl.BlockSpec((width, 2 * HEAD_DIM), lambda n, kind=kind: (0, kind * blocks + n))
            for kind in range(3)
        ]
        + [whole(cos_tab.shape)] * 2,
        out_specs=[pl.BlockSpec((2,) + out[1:], lambda n: (n, 0, 0, 0))] * micros,
        out_shape=[jax.ShapeDtypeStruct(out, BF16)] * micros,
    )(*pieces, weights, weights, weights, cos_tab, sin_tab)


def mix_out_kernel(micros, x_ref, w_ref, mix_ref, *outs):
    heads, seqs, _, span = x_ref.shape
    peers = len(outs) // micros
    own = seqs // (micros * peers)

    @pl.when(pl.program_id(0) == 0)
    def _():
        for q in range(seqs):
            mix = x_ref[:, q].reshape(heads * HEAD_DIM, span)
            mix_ref[q * span : (q + 1) * span, :] = mix.T

    total = dot(mix_ref[...], w_ref[...], 1, 1)
    size = own * span
    for i, out in enumerate(outs):
        out[...] = total[i * size : (i + 1) * size].astype(out.dtype)


def mix_out(packed, weights, micros, peers):
    _, seqs, _, span = packed.shape
    width, cols = weights.shape
    tile = tile_of(width)
    rows = seqs * span // (micros * peers)
    kinds = [BF16 if k else F32 for _ in range(micros) for k in range(peers)]
    return pl.pallas_call(
        functools.partial(mix_out_kernel, micros),
        grid=(width // tile,),
        in_specs=[whole(packed.shape), pl.BlockSpec((tile, cols), lambda n: (n, 0))],
        out_specs=[pl.BlockSpec((seqs * span, cols), lambda n: (0, 0))]
        + [col_tile(rows, tile)] * len(kinds),
        out_shape=[jax.ShapeDtypeStruct((seqs * span, cols), BF16)]
        + [jax.ShapeDtypeStruct((rows, width), kind) for kind in kinds],
    )(packed, weights)


def mix_back_kernel(*refs):
    pieces, (w_ref, out_ref) = refs[:-2], refs[-2:]
    heads, _, _, span = out_ref.shape
    q = 0
    for ref in pieces:
        cols = dot(ref[...], w_ref[...], 1, 0).T.astype(BF16)
        for i in range(ref.shape[0] // span):
            for h in range(heads):
                out_ref[h, q] = cols[
                    h * HEAD_DIM : (h + 1) * HEAD_DIM, i * span : (i + 1) * span
                ]
            q += 1


def mix_back(pieces, weights, span):
    width, cols = weights.shape
    tile = tile_of(cols)
    seqs = sum(p.shape[0] for p in pieces) // span
    heads = cols // HEAD_DIM
    return pl.pallas_call(
        mix_back_kernel,
        grid=(cols // tile,),
        in_specs=[whole(p.shape) for p in pieces] + [col_tile(width, tile)],
        out_specs=pl.BlockSpec((tile // HEAD_DIM, seqs, HEAD_DIM, span), lambda n: (n, 0, 0, 0)),
        out_shape=jax.ShapeDtypeStruct((heads, seqs, HEAD_DIM, span), BF16),
    )(*pieces, weights)


def unturn_kernel(ref, cos_ref, sin_ref, *refs):
    out_ref = refs[-1]
    heads, seqs, _, span = ref.shape
    plain = pl.program_id(0) >= 2
    for k in range(seqs):
        cos_tab = jnp.where(plain, 1.0, cos_ref[:, k * span : (k + 1) * span])
        sin_tab = jnp.where(plain, 0.0, -sin_ref[:, k * span : (k + 1) * span])
        for h in range(0, heads, 2):
            pair = jnp.concatenate(
                [turn(ref[h + i, k].astype(F32), cos_tab, sin_tab) for i in range(2)], axis=0
            )
            out_ref[k * span : (k + 1) * span, h * HEAD_DIM : (h + 2) * HEAD_DIM] = pair.T.astype(
                BF16
            )


def unturn(packed, micro, micros, cos_tab, sin_tab, into):
    heads, seqs, _, span = packed.shape
    rows = seqs * span
    extra = [] if into is None else [into]
    return pl.pallas_call(
        unturn_kernel,
        grid=(3,),
        in_specs=[pl.BlockSpec((heads, seqs, HEAD_DIM, span), lambda n: (0, 0, n, 0))]
        + [whole(cos_tab.shape)] * 2
        + [pl.BlockSpec(memory_space=pl.ANY) for _ in extra],
        out_specs=pl.BlockSpec((rows, heads * HEAD_DIM), lambda n: (micro, n)),
        out_shape=jax.ShapeDtypeStruct((micros * rows, 3 * heads * HEAD_DIM), BF16),
        input_output_aliases={3: 0} if extra else {},
    )(packed, cos_tab, sin_tab, *extra)


class HeadSplit:
    def __init__(self, n_fsdp, head_count, seqs):
        self.head_groups = math.gcd(n_fsdp, head_count)
        self.seq_groups = n_fsdp // self.head_groups
        self.heads_per = head_count // self.head_groups
        self.seqs_per = seqs // self.seq_groups

    def to_heads(self, packed):
        width, span = packed.shape[2:]
        packed = packed.reshape(
            self.head_groups, self.heads_per, -1, self.seq_groups, self.seqs_per, width, span
        ).transpose(3, 0, 2, 1, 4, 5, 6)
        packed = packed.reshape(self.seq_groups * self.head_groups, -1, width, span)
        return lax.all_to_all(packed, FSDP, split_axis=0, concat_axis=0, tiled=True)

    def to_spans(self, packed):
        width, span = packed.shape[2:]
        packed = lax.all_to_all(packed, FSDP, split_axis=0, concat_axis=0, tiled=True)
        packed = packed.reshape(
            self.seq_groups, self.head_groups, -1, self.heads_per, self.seqs_per, width, span
        ).transpose(1, 3, 2, 0, 4, 5, 6)
        return packed.reshape(self.head_groups * self.heads_per, -1, width, span)

    def pair_prefix(self, prefix, fsdp_index):
        mine = lax.dynamic_slice_in_dim(
            prefix, (fsdp_index // self.head_groups) * self.seqs_per, self.seqs_per, 0
        )
        return jnp.tile(mine, self.heads_per)


def layer(
    inputs,
    out_grads,
    prefix_len,
    positions,
    attn_gain,
    w_query,
    w_key,
    w_value,
    w_out,
    mlp_gain,
    w_gate,
    w_up,
    w_down,
):
    micro_count, seq_dev, span_len, model_width = inputs.shape
    n_tensor = lax.axis_size(TENSOR)
    n_fsdp = lax.axis_size(FSDP)
    seq_mb = seq_dev * n_tensor
    seq_len = span_len * n_fsdp
    own_rows = seq_dev * span_len
    head_cols = w_query.shape[1]
    head_count = head_cols // HEAD_DIM
    ff_cols = w_gate.shape[1]
    fsdp_index = lax.axis_index(FSDP)
    tensor_index = lax.axis_index(TENSOR)
    query_index = fsdp_index * span_len + jnp.arange(span_len, dtype=jnp.int32)
    split = HeadSplit(n_fsdp, head_count, seq_mb)
    micros = range(micro_count)

    def gather(shard):
        return lax.all_gather(shard, FSDP, axis=0, tiled=True)

    def scatter(grad):
        return lax.psum_scatter(grad, FSDP, scatter_dimension=0, tiled=True).astype(F32)

    gains = lax.all_gather(jnp.stack([attn_gain, mlp_gain]), FSDP, axis=1, tiled=True)
    gain_attn = gains[0].astype(F32)
    gain_mlp = gains[1].astype(F32)
    full_qkv = gather(jnp.concatenate([w_query, w_key, w_value], axis=1))
    full_out = gather(w_out)
    side = (fsdp_index // PAIR) % 2

    order = (
        ((tensor_index ^ jnp.arange(n_tensor, dtype=jnp.int32)) * seq_dev)[:, None]
        + jnp.arange(seq_dev, dtype=jnp.int32)
    ).reshape(-1)
    prefix_all = jnp.take(prefix_len, order, axis=1)
    own_prefix = prefix_all[:, :seq_dev]
    pos_all = jnp.take(positions, order, axis=1)
    half_dim = HEAD_DIM // 2
    ladder = jnp.arange(half_dim, dtype=F32) * (2.0 / HEAD_DIM)
    inverse = 1.0 / rope_base**ladder

    x_float = inputs.reshape(micro_count * own_rows, model_width).astype(F32)
    grad_own = out_grads.reshape(micro_count * own_rows, model_width)
    unit_attn, scale_attn = normalize(x_float)
    normed = (unit_attn * gain_attn).astype(BF16)
    normed_pieces = spread_pieces(normed, False)
    cos_tab, sin_tab, pair_prefix = [], [], []
    for m in micros:
        angles = inverse[:, None] * pos_all[m].astype(F32).reshape(-1)[None, :]
        cos_tab.append(jnp.cos(angles))
        sin_tab.append(jnp.sin(angles))
        pair_prefix.append(split.pair_prefix(prefix_all[m], fsdp_index))
    cos_all = jnp.stack(cos_tab)
    sin_all = jnp.stack(sin_tab)
    half_cols = ff_cols // 2
    ffn_near = half_of([w_gate, w_up, w_down], side)
    ffn_far = half_of([w_gate, w_up, w_down], 1 - side)
    grad_pair = pair_join(after(paired(grad_own), full_qkv), micro_count)
    labels, taken = [], [0] * n_tensor
    spans_of = [(m, r) for m in micros for r in range(seq_dev)]
    peer = 0
    for piece in normed_pieces:
        size = piece.shape[0] // span_len
        start = taken[peer]
        labels.append(
            tuple((m, peer * seq_dev + r) for m, r in spans_of[start : start + size])
        )
        taken[peer] += size
        if taken[peer] == len(spans_of):
            peer += 1
    stack = project(normed_pieces, tuple(labels), full_qkv, cos_all, sin_all, span_len)
    packed = []
    for m in micros:
        packed.append(split.to_heads(stack[m]))
    normed_rows = gather_rows(whole_blocks(after(normed_pieces, stack)), micro_count)
    grad_pair = after(grad_pair, stack)
    grad_blocks = spread(grad_pair)
    ffn_other = swap(after(ffn_far, packed[-1]), FSDP, PAIR)
    attn_out, attn_lse = [None] * micro_count, [None] * micro_count
    done = full_out
    for m in reversed(micros):
        attn_out[m], attn_lse[m] = attend_forward(pair_prefix[m], after(packed[m], done))
        done = attn_lse[m]
    mix_packed = split.to_spans(jnp.concatenate(attn_out, axis=1))
    ffn_other = after(ffn_other, attn_lse)
    shards = [
        own_half(
            side,
            ffn_near[:, i * half_cols : (i + 1) * half_cols],
            ffn_other[:, i * half_cols : (i + 1) * half_cols],
        )
        for i in range(3)
    ]
    full_gate = gather_half(after(shards[0], mix_packed))
    branch, resid, others, normed_mlp, joined = [], [], [], [], []
    flat_inputs = inputs.reshape(micro_count * own_rows, model_width)
    gain_rows = gain_mlp[None]
    mix_rows, *parts = mix_out(mix_packed, full_out, micro_count, n_tensor)
    for m in micros:
        own, *sent = parts[m * n_tensor : (m + 1) * n_tensor]
        blocks = peer_swaps([own] + sent)
        if m:
            blocks = after(blocks, normed_mlp)
        part, res, normed = norm_rows(flat_inputs, m, gain_rows, own, blocks, n_fsdp)
        branch.append(part)
        resid.append(res)
        normed_mlp.append(normed)
        others.append(swap(normed, FSDP, PAIR))
    for m in micros:
        other = after(others[m], joined) if m else others[m]
        joined.append(join(normed_mlp[m], other))
    full_up = gather_half(after(shards[1], joined))
    full_down = gather_half(shards[2])
    mlp_rows, first = [], None
    for m in micros:
        blocks = spread(joined[m] if first is None else after(joined[m], first), False)
        first = blocks[1:3]
        mlp_rows.append(gather_rows(blocks, 1))
    grad_rows = gather_rows(after(grad_blocks, first), micro_count)

    hidden, gate_val, up_val = [], [], []
    for m in micros:
        gate, up, hid = ffn_forward(mlp_rows[m], full_gate, full_up)
        gate_val.append(gate)
        up_val.append(up)
        hidden.append(hid)
    hidden = jnp.concatenate(hidden, axis=0)
    down_grad = dot(grad_rows, hidden, 0, 0).astype(BF16)
    full_down = after(full_down, down_grad)
    part_down = scatter_half(down_grad)
    grad_gu, normed_part = [], []
    for m in micros:
        gate_in = after(gate_val[m], normed_part) if m else gate_val[m]
        gate, up = ffn_back(grad_rows, m, full_down, gate_in, up_val[m])
        grad_gu.append(jnp.concatenate([gate, up], axis=1))
        normed_part.append(to_peers([gate, up], [full_gate, full_up], 1, n_tensor))
    all_mlp_rows = jnp.concatenate(after(mlp_rows, normed_part), axis=0)
    gu_grad = dot(all_mlp_rows, jnp.concatenate(grad_gu, axis=0), 0, 0).astype(BF16)
    part_gu = scatter_half(after(gu_grad, part_down))
    grad_resid, branch_rows, near_far, mlp_gain_parts = [], [], [], []
    for m in micros:
        blocks = peer_swaps(normed_part[m])
        blocks = after(blocks, near_far[-1][0] if m else gu_grad)
        near, far = peer_sum(normed_part[m][0], blocks)
        near_far.append((near, swap(far, FSDP, PAIR)))
    low = None
    for m in micros:
        near, far = near_far[m]
        if m:
            far = after(far, low)
        grad_res, low, gain_part = norm_grad(grad_own, m, gain_rows, near, far, resid[m], n_fsdp)
        mlp_gain_parts.append(gain_part[0])
        grad_resid.append(grad_res)
        branch_rows += spread(low)
    mlp_gain_sum = sum(mlp_gain_parts)
    grad_mix = mix_back(branch_rows, full_out, span_len)
    grad_out_all = split.to_heads(grad_mix)
    out_grad = dot(
        jnp.concatenate(after(branch_rows, grad_mix), axis=0), mix_rows, 0, 0
    ).astype(BF16)

    mlp_blocks = to_peers([after(hidden, out_grad)], [full_down], micro_count, n_tensor)
    own_out = scatter(after(out_grad, part_gu, mlp_blocks))

    grad_raw = []
    packed_grads = []
    for m in micros:
        grad_out = after(grad_out_all, mlp_blocks, part_down if m else own_out)
        packed_grad = attend_back(pair_prefix[m], packed[m], attn_out[m], grad_out, attn_lse[m], m)
        packed_grads.append(packed_grad)
        grad_raw.append(split.to_spans(packed_grad))

    mlp_part = collect(mlp_blocks, token=packed_grads[0])
    near = [mlp_part[2 * m * own_rows : (2 * m + 1) * own_rows] for m in micros]
    far = [mlp_part[(2 * m + 1) * own_rows : (2 * m + 2) * own_rows] for m in micros]
    far = swap(jnp.concatenate(far, axis=0).astype(BF16), FSDP, PAIR)
    grad_qkv = None
    for m in reversed(micros):
        grad_qkv = unturn(grad_raw[m], m, micro_count, cos_all[m], sin_all[m], grad_qkv)
    qkv_grad = dot(normed_rows, grad_qkv, 0, 0).astype(BF16)
    own_gate, own_up = settle_half(part_gu, side, 2, qkv_grad)
    (own_down,) = settle_half(part_down, side, 1, qkv_grad)
    part = to_peers([after(grad_qkv, qkv_grad)], [full_qkv], micro_count, n_tensor)
    grad_normed = collect(part, False)
    far = after(far, grad_normed).astype(F32)
    mlp_out = paired(jnp.concatenate(near, axis=0) + far)
    branch = jnp.concatenate(branch, axis=0)
    result = jnp.concatenate(resid, axis=0) + mlp_out
    output = result.astype(BF16).reshape(inputs.shape)
    valid = (query_index[None, None, :] >= own_prefix[:, :, None]).reshape(-1)
    stats = jnp.stack(
        [
            jnp.sum(
                jnp.where(valid, jnp.sum(part * part, axis=1), 0.0).reshape(
                    micro_count, seq_dev, span_len
                ),
                axis=2,
            )
            for part in (result, branch, mlp_out)
        ],
        axis=-1,
    )

    own_qkv = scatter(qkv_grad)
    part, attn_gain_sum = norm_back(grad_normed, unit_attn, scale_attn, gain_attn)
    input_grad = (jnp.concatenate(grad_resid, axis=0) + part).reshape(inputs.shape)

    gain_cols = jnp.stack([attn_gain_sum, mlp_gain_sum], axis=0).reshape(2, n_fsdp, -1)
    row_share = model_width // n_fsdp
    stat_row = jnp.broadcast_to(stats.reshape(1, -1), (n_fsdp, stats.size))
    pad = -stats.size % 128
    small = jnp.concatenate(
        [gain_cols[0], gain_cols[1], stat_row, jnp.zeros((n_fsdp, pad), F32)], axis=1
    )
    small = lax.all_to_all(small, FSDP, split_axis=0, concat_axis=0, tiled=True)
    small = jnp.sum(small, axis=0)
    own_gain = small[: 2 * row_share]
    own_gain = sum([own_gain] + [swap(own_gain, TENSOR, k) for k in range(1, n_tensor)])
    own_gain = own_gain.reshape(2, row_share)
    stat_sum = small[2 * row_share : 2 * row_share + stats.size].reshape(stats.shape)
    counts = ((seq_len - own_prefix) * model_width).astype(F32)
    rms_stats = jnp.sqrt(stat_sum / counts[..., None] + stat_eps)
    return (
        output,
        input_grad,
        own_gain[0],
        own_qkv[:, :head_cols],
        own_qkv[:, head_cols : 2 * head_cols],
        own_qkv[:, 2 * head_cols :],
        own_out,
        own_gain[1],
        own_gate,
        own_up,
        own_down,
        rms_stats,
    )


def solution(mesh):
    in_specs = (
        P(None, TENSOR, FSDP, None),
        P(None, TENSOR, FSDP, None),
        P(),
        P(None, None, FSDP),
        P(FSDP),
        P(FSDP, TENSOR),
        P(FSDP, TENSOR),
        P(FSDP, TENSOR),
        P(FSDP, TENSOR),
        P(FSDP),
        P(FSDP, TENSOR),
        P(FSDP, TENSOR),
        P(FSDP, TENSOR),
    )
    out_specs = (
        P(None, TENSOR, FSDP, None),
        P(None, TENSOR, FSDP, None),
        P(FSDP),
        P(FSDP, TENSOR),
        P(FSDP, TENSOR),
        P(FSDP, TENSOR),
        P(FSDP, TENSOR),
        P(FSDP),
        P(FSDP, TENSOR),
        P(FSDP, TENSOR),
        P(FSDP, TENSOR),
        P(None, TENSOR, None),
    )
    return jax.shard_map(layer, mesh=mesh, in_specs=in_specs, out_specs=out_specs, check_vma=False)
```
